32 devices in a mesh: dp: 16 (over z, y, x), tensor: 2 (over core).
Axes of the slice: x: 2, y: 2, z: 4, core: 2. Of those that a mesh axis runs over, the one named last changes fastest.
Arguments:
- tokens: bfloat16 [32768, 768], P(('dp', 'tensor')), may hold values from -6 to 6
- grad_out: bfloat16 [32768, 768], P(('dp', 'tensor')), may hold values from -6 to 6
- prefix: int32 [32], P('dp'), may hold values from 102 to 512
- pre_gain: float32 [768], replicated, may hold values from 0.5 to 1.5
- pre_bias: float32 [768], replicated, may hold values from -1 to 1
- qkv_weight: bfloat16 [768, 3, 768], P(None, None, 'tensor'), may hold values from -0.21875 to 0.21875
- qv_bias: float32 [2, 768], P(None, 'tensor'), may hold values from -1.5 to 1.5
- sub_gain: float32 [768], P('tensor'), may hold values from 0.5 to 1.5
- sub_bias: float32 [768], P('tensor'), may hold values from -1 to 1
- out_weight: bfloat16 [768, 768], P('tensor'), may hold values from -0.375 to 0.375
- out_bias: float32 [768], replicated, may hold values from -1 to 1
- ffn_gain: float32 [768], replicated, may hold values from 0.5 to 1.5
- ffn_bias: float32 [768], replicated, may hold values from -1 to 1
- up_weight: bfloat16 [768, 3072], P(None, 'tensor'), may hold values from -0.375 to 0.375
- up_bias: float32 [3072], P('tensor'), may hold values from -2.5 to 2.5
- inner_gain: float32 [3072], P('tensor'), may hold values from 0.5 to 1.5
- inner_bias: float32 [3072], P('tensor'), may hold values from -1 to 1
- down_weight: bfloat16 [3072, 768], P('tensor'), may hold values from -0.1875 to 0.1875
- down_bias: float32 [768], replicated, may hold values from -1 to 1
Outputs:
- output: bfloat16 [32768, 768], P(('dp', 'tensor'))
- input_grad: float32 [32768, 768], P(('dp', 'tensor'))
- grad_pre_gain: float32 [768], replicated
- grad_pre_bias: float32 [768], replicated
- grad_qkv_weight: float32 [768, 3, 768], P(None, None, 'tensor')
- grad_qv_bias: float32 [2, 768], P(None, 'tensor')
- grad_sub_gain: float32 [768], P('tensor')
- grad_sub_bias: float32 [768], P('tensor')
- grad_out_weight: float32 [768, 768], P('tensor')
- grad_out_bias: float32 [768], replicated
- grad_ffn_gain: float32 [768], replicated
- grad_ffn_bias: float32 [768], replicated
- grad_up_weight: float32 [768, 3072], P(None, 'tensor')
- grad_up_bias: float32 [3072], P('tensor')
- grad_inner_gain: float32 [3072], P('tensor')
- grad_inner_bias: float32 [3072], P('tensor')
- grad_down_weight: float32 [3072, 768], P('tensor')
- grad_down_bias: float32 [768], replicated
The draws below stay inside these ranges and needn't reach their ends.
All inputs are finite; a program needn't handle non-finite values.
Results may differ from the reference program's by a relative error of at most 0.013.
Values may be sent and summed in bfloat16 or wider, within the bound.
A program may use at most 192 MiB of HBM per device.

```python
import jax
import jax.numpy as jnp
from jax import lax

D = 768
HEADS = 12
HEAD_DIM = 64
FF = 3072
SEQ_LEN = 1024
SEQS = 32
TOKENS = 32768
QBLOCK = 512


def touch_ends(result, stream_key, least, largest):
    index_at = [jax.random.randint(jax.random.fold_in(stream_key, axis), (), 0, length) for axis, length in enumerate(result.shape)]
    widest = result.shape.index(max(result.shape))
    beside = index_at[:widest] + [(index_at[widest] + 1) % result.shape[widest]] + index_at[widest + 1:]
    return result.at[tuple(index_at)].set(least).at[tuple(beside)].set(largest)


def steps_of(rng, extent, split, least, top_value):
    gain = 1.0
    for dim, blocks in split:
        draws = jax.random.uniform(jax.random.fold_in(jax.random.fold_in(rng, 6), dim), (blocks,), jnp.float32, least / len(split), top_value / len(split))
        gain = gain * jnp.repeat(jnp.exp(draws), extent[dim] // blocks).reshape((-1,) + (1,) * (len(extent) - 1 - dim))
    return gain


def scatter_about(rng, dims, scale, limit, shards=(), kind=jnp.bfloat16):
    entries = jax.random.normal(rng, dims, jnp.float32) * scale
    if len(shards) > 0:
        entries = steps_of(rng, dims, shards, -0.22, 0.18) * entries
    return jnp.clip(entries, min=-limit, max=limit).astype(kind)


def setup_inputs(seed: int = 0) -> dict:
    keys = jax.random.split(jax.random.key(seed), 20)
    tokens = scatter_about(keys[0], (TOKENS, D), 1.0, 6.0, ((0, 32),))
    grad_out = scatter_about(keys[1], (TOKENS, D), 1.0, 6.0, ((0, 32),))
    prefix = touch_ends(jax.random.randint(keys[2], (SEQS,), SEQ_LEN // 10, SEQ_LEN // 2 + 1), jax.random.fold_in(keys[2], 1), SEQ_LEN // 10, (SEQ_LEN // 2 + 1) - 1).astype(jnp.int32)
    pre_gain = jnp.clip(1.0 + 0.1 * jax.random.normal(keys[3], (D,), jnp.float32), 0.5, 1.5)
    pre_bias = scatter_about(keys[4], (D,), 0.2, 1.0, (), jnp.float32)
    qkv_weight = scatter_about(keys[5], (D, 3, D), D ** -0.5, 0.21875, ((2, 2),))
    qv_bias = scatter_about(keys[6], (2, D), 0.3, 1.5, ((1, 2),), jnp.float32)
    sub_gain = jnp.clip(1.0 + 0.1 * jax.random.normal(keys[7], (D,), jnp.float32), 0.5, 1.5)
    sub_bias = scatter_about(keys[8], (D,), 0.2, 1.0, ((0, 2),), jnp.float32)
    out_weight = scatter_about(keys[9], (D, D), (D // 3) ** -0.5, 0.375, ((0, 2),))
    out_bias = scatter_about(keys[10], (D,), 0.2, 1.0, (), jnp.float32)
    ffn_gain = jnp.clip(1.0 + 0.1 * jax.random.normal(keys[11], (D,), jnp.float32), 0.5, 1.5)
    ffn_bias = scatter_about(keys[12], (D,), 0.2, 1.0, (), jnp.float32)
    up_weight = scatter_about(keys[13], (D, FF), (D // 3) ** -0.5, 0.375, ((1, 2),))
    up_bias = scatter_about(keys[14], (FF,), 0.5, 2.5, ((0, 2),), jnp.float32)
    inner_gain = jnp.clip(1.0 + 0.1 * jax.random.normal(keys[15], (FF,), jnp.float32), 0.5, 1.5)
    inner_bias = scatter_about(keys[16], (FF,), 0.2, 1.0, ((0, 2),), jnp.float32)
    down_weight = scatter_about(keys[17], (FF, D), (FF // 3) ** -0.5, 0.1875, ((0, 2),))
    down_bias = scatter_about(keys[18], (D,), 0.2, 1.0, (), jnp.float32)
    return dict(tokens=tokens, grad_out=grad_out, prefix=prefix, pre_gain=pre_gain, pre_bias=pre_bias, qkv_weight=qkv_weight, qv_bias=qv_bias, sub_gain=sub_gain, sub_bias=sub_bias, out_weight=out_weight, out_bias=out_bias, ffn_gain=ffn_gain, ffn_bias=ffn_bias, up_weight=up_weight, up_bias=up_bias, inner_gain=inner_gain, inner_bias=inner_bias, down_weight=down_weight, down_bias=down_bias)


@jax.custom_vjp
def low(v):
    return lax.optimization_barrier(v.astype(jnp.bfloat16)).astype(jnp.float32)

@jax.custom_vjp
def low_back(v):
    return v

def low_keep(v):
    return (low(v), None)

def low_pass(kept, grad):
    return (grad,)

def back_keep(v):
    return (v, None)

def back_low(kept, grad):
    return (low(grad),)
low.defvjp(low_keep, low_pass)
low_back.defvjp(back_keep, back_low)
highest = lax.Precision.HIGHEST
norm_eps = 1e-05

def layer_norm(values, norm_gain, norm_bias):
    centre = values - lax.optimization_barrier(jnp.mean(values, axis=-1, keepdims=True))
    spread = lax.optimization_barrier(jnp.mean(centre * centre, axis=-1, keepdims=True))
    return centre * lax.rsqrt(spread + norm_eps) * norm_gain + norm_bias

def matmul(left_rows, weight):
    return jnp.dot(left_rows, weight, precision=highest, preferred_element_type=jnp.float32)

def attention(queries, key_rows, value_rows, prefix_len):
    length = queries.shape[0]
    block_count = length // QBLOCK
    key_heads = key_rows.reshape(length, HEADS, HEAD_DIM)
    value_heads = value_rows.reshape(length, HEADS, HEAD_DIM)

    def one_block(block_items):
        row_start, query_block = block_items
        query_heads = query_block.reshape(QBLOCK, HEADS, HEAD_DIM)
        scores = low_back(jnp.einsum('qhd,khd->hqk', query_heads, key_heads, precision=highest) * HEAD_DIM ** (-0.5))
        query_pos = row_start + lax.iota(jnp.int32, QBLOCK)
        key_pos = lax.iota(jnp.int32, length)
        visible = (key_pos[None, :] <= query_pos[:, None]) | (key_pos[None, :] < prefix_len)
        scores = jnp.where(visible[None], scores, -1e+30)
        weights = jax.nn.softmax(scores, axis=-1)
        mixed_heads = jnp.einsum('hqk,khd->qhd', low(weights), value_heads, precision=highest)
        return mixed_heads.reshape(QBLOCK, D)
    starts = jnp.arange(block_count, dtype=jnp.int32) * QBLOCK
    blocks = lax.map(jax.checkpoint(one_block), (starts, queries.reshape(block_count, QBLOCK, D)))
    return blocks.reshape(length, D)

def forward(params, seq_tokens, prefix_len):
    pre_gain, pre_bias, qkv_weight, qv_bias, sub_gain, sub_bias, out_weight, out_bias, ffn_gain, ffn_bias, up_weight, up_bias, inner_gain, inner_bias, down_weight, down_bias = params
    normed_one = low(layer_norm(seq_tokens, pre_gain, pre_bias))
    projected = low_back(jnp.einsum('ld,dcn->lcn', normed_one, qkv_weight, precision=highest))
    queries = low(projected[:, 0] + qv_bias[0])
    key_rows = low(projected[:, 1])
    value_rows = low(projected[:, 2] + qv_bias[1])
    attended = low_back(attention(queries, key_rows, value_rows, prefix_len))
    normed_two = low(layer_norm(attended, sub_gain, sub_bias))
    middle = seq_tokens + low_back(matmul(normed_two, out_weight)) + out_bias
    normed_three = low(layer_norm(middle, ffn_gain, ffn_bias))
    hidden = low_back(matmul(normed_three, up_weight)) + up_bias
    normed_four = low(layer_norm(jax.nn.gelu(hidden, approximate=False), inner_gain, inner_bias))
    return middle + low_back(matmul(normed_four, down_weight)) + down_bias

def reference(tokens, grad_out, prefix, pre_gain, pre_bias, qkv_weight, qv_bias, sub_gain, sub_bias, out_weight, out_bias, ffn_gain, ffn_bias, up_weight, up_bias, inner_gain, inner_bias, down_weight, down_bias):
    params = (pre_gain.astype(jnp.float32), pre_bias.astype(jnp.float32), qkv_weight.astype(jnp.float32), qv_bias.astype(jnp.float32), sub_gain.astype(jnp.float32), sub_bias.astype(jnp.float32), out_weight.astype(jnp.float32), out_bias.astype(jnp.float32), ffn_gain.astype(jnp.float32), ffn_bias.astype(jnp.float32), up_weight.astype(jnp.float32), up_bias.astype(jnp.float32), inner_gain.astype(jnp.float32), inner_bias.astype(jnp.float32), down_weight.astype(jnp.float32), down_bias.astype(jnp.float32))
    seq_inputs = tokens.astype(jnp.float32).reshape(SEQS, SEQ_LEN, D)
    seq_cotangents = grad_out.astype(jnp.float32).reshape(SEQS, SEQ_LEN, D)

    def one_sequence(running, seq_items):
        seq_tokens, seq_cotangent, prefix_len = seq_items

        def apply_layer(layer_params, layer_tokens):
            return forward(layer_params, layer_tokens, prefix_len)
        seq_output, pullback = jax.vjp(apply_layer, params, seq_tokens)
        grad_params, grad_tokens = pullback(seq_cotangent)
        running = jax.tree.map(jnp.add, running, grad_params)
        return (running, (seq_output.astype(jnp.bfloat16), grad_tokens))
    zeros_init = jax.tree.map(jnp.zeros_like, params)
    totals, (outputs, grad_inputs) = lax.scan(one_sequence, zeros_init, (seq_inputs, seq_cotangents, prefix))
    return (outputs.reshape(TOKENS, D), grad_inputs.reshape(TOKENS, D), totals[0], totals[1], totals[2], totals[3], totals[4], totals[5], totals[6], totals[7], totals[8], totals[9], totals[10], totals[11], totals[12], totals[13], totals[14], totals[15])
```

```python
import functools
import jax
import jax.numpy as jnp
from jax import lax
from jax.sharding import PartitionSpec as P
from jax.experimental import pallas as pl
from jax.experimental.pallas import tpu as pltpu

D = 768
HEAD_DIM = 64
PREFIX_MAX = 512
EPS = 1e-05
F32 = jnp.float32
BF16 = jnp.bfloat16
QB = 512


def nn(a, b):
    return lax.dot_general(a, b, (((1,), (0,)), ((), ())), preferred_element_type=F32)


def nt(a, b):
    return lax.dot_general(a, b, (((1,), (1,)), ((), ())), preferred_element_type=F32)


def tn(a, b):
    return lax.dot_general(a, b, (((0,), (0,)), ((), ())), preferred_element_type=F32)


def halves(v):
    left = lax.broadcasted_iota(jnp.int32, v.shape, 1) < HEAD_DIM
    zero = jnp.zeros_like(v)
    return jnp.where(left, v, zero), jnp.where(left, zero, v)


def spans(start, length, block):
    last = min(length, max(start + block, PREFIX_MAX))
    out = []
    if start:
        out.append((0, start, False))
    out.append((start, last, True))
    return out


def masked(scores, key_start, query_start, prefix):
    key_pos = key_start + lax.broadcasted_iota(jnp.int32, scores.shape, 0)
    query_pos = query_start + lax.broadcasted_iota(jnp.int32, scores.shape, 1)
    seen = key_pos <= query_pos
    if key_start < PREFIX_MAX:
        seen = seen | (key_pos < prefix)
    return jnp.where(seen, scores, -1e30)


def attn_fwd_kernel(prefix_ref, q_ref, k_ref, v_ref, o_ref, lse_ref):
    length = q_ref.shape[0]
    prefix = prefix_ref[0]
    keys = halves(k_ref[...])
    value_t = v_ref[...].T
    for start in range(0, length, QB):
        query = q_ref[start : start + QB, :] * jnp.asarray(HEAD_DIM**-0.5, BF16)
        parts = []
        for head in range(2):
            scores = []
            for first, last, mask in spans(start, length, QB):
                s = nt(keys[head][first:last], query)
                scores.append(masked(s, first, start, prefix) if mask else s)
            peak = functools.reduce(jnp.maximum, [jnp.max(s, axis=0, keepdims=True) for s in scores])
            total = jnp.zeros_like(peak)
            mixed = jnp.zeros((HEAD_DIM, QB), F32)
            rows = slice(head * HEAD_DIM, (head + 1) * HEAD_DIM)
            for s, (first, last, _) in zip(scores, spans(start, length, QB)):
                w = jnp.exp(s - peak)
                total = total + jnp.sum(w, axis=0, keepdims=True)
                mixed = mixed + nn(value_t[rows, first:last], w.astype(BF16))
            parts.append(mixed / total)
            lse_ref[0, head : head + 1, start : start + QB] = peak + jnp.log(total)
        o_ref[start : start + QB, :] = jnp.concatenate(parts, axis=0).T


def attn_fwd(prefix, qkv):
    length = qkv.shape[0]
    pairs = D // 128
    col = lambda c: pl.BlockSpec((length, 128), lambda i, c=c: (0, c * pairs + i))
    return pl.pallas_call(
        attn_fwd_kernel,
        grid=(pairs,),
        in_specs=[pl.BlockSpec(memory_space=pltpu.SMEM), col(0), col(1), col(2)],
        out_specs=[
            pl.BlockSpec((length, 128), lambda i: (0, i)),
            pl.BlockSpec((1, 8, length), lambda i: (i, 0, 0)),
        ],
        out_shape=[
            jax.ShapeDtypeStruct((length, D), F32),
            jax.ShapeDtypeStruct((pairs, 8, length), F32),
        ],
        name="attn_fwd",
    )(prefix, qkv, qkv, qkv)


def attn_bwd_kernel(prefix_ref, q_ref, k_ref, v_ref, o_ref, g_ref, lse_ref, dq_ref, dk_ref, dv_ref, bias_ref):
    length = q_ref.shape[0]
    prefix = prefix_ref[0]
    scale = HEAD_DIM**-0.5
    keys = halves(k_ref[...])
    values = halves(v_ref[...])
    key_t = k_ref[...].T
    delta_t = (o_ref[...] * g_ref[...].astype(F32)).T
    dk = [jnp.zeros((b - a, 128), F32) for a, b in zip(range(0, length, QB), range(QB, length + 1, QB))]
    dv = list(dk)
    qsum = jnp.zeros((8, 128), F32)
    for start in range(0, length, QB):
        cols = slice(start, start + QB)
        query = q_ref[cols, :] * jnp.asarray(scale, BF16)
        query_half = halves(query)
        grad = g_ref[cols, :]
        grad_half = halves(grad)
        parts = []
        for head in range(2):
            rows = slice(head * HEAD_DIM, (head + 1) * HEAD_DIM)
            lse = lse_ref[0, head : head + 1, cols]
            delta = jnp.sum(delta_t[rows, cols], axis=0, keepdims=True)
            dq = jnp.zeros((HEAD_DIM, QB), F32)
            for first in range(0, length, QB):
                live = [s for s in spans(start, length, QB) if s[0] <= first < s[1]]
                if not live:
                    continue
                last = first + QB
                s = nt(keys[head][first:last], query)
                if live[0][2]:
                    s = masked(s, first, start, prefix)
                w = jnp.exp(s - lse)
                dp = nt(values[head][first:last], grad)
                ds = (w * (dp - delta)).astype(BF16)
                b = first // QB
                dv[b] = dv[b] + nn(w.astype(BF16), grad_half[head])
                dk[b] = dk[b] + nn(ds, query_half[head])
                dq = dq + nn(key_t[rows, first:last], ds)
            parts.append(dq)
        dq = jnp.concatenate(parts, axis=0).T * scale
        qsum = qsum + jnp.sum(dq.reshape(QB // 8, 8, 128), axis=0)
        dq_ref[cols, :] = dq.astype(BF16)
    vsum = jnp.zeros((8, 128), F32)
    for b in range(length // QB):
        cols = slice(b * QB, (b + 1) * QB)
        dk_ref[cols, :] = dk[b].astype(BF16)
        dv_ref[cols, :] = dv[b].astype(BF16)
        vsum = vsum + jnp.sum(dv[b].reshape(QB // 8, 8, 128), axis=0)
    bias_ref[0:1, :] = jnp.sum(qsum, axis=0, keepdims=True)
    bias_ref[1:2, :] = jnp.sum(vsum, axis=0, keepdims=True)


def attn_bwd(prefix, qkv, attended, grad_attended, lse):
    length = qkv.shape[0]
    pairs = D // 128
    col = lambda c: pl.BlockSpec((length, 128), lambda i, c=c: (0, c * pairs + i))
    one = pl.BlockSpec((length, 128), lambda i: (0, i))
    return pl.pallas_call(
        attn_bwd_kernel,
        grid=(pairs,),
        in_specs=[
            pl.BlockSpec(memory_space=pltpu.SMEM), col(0), col(1), col(2), one, one,
            pl.BlockSpec((1, 8, length), lambda i: (i, 0, 0)),
        ],
        out_specs=[one, one, one, pl.BlockSpec((8, 128), lambda i: (0, i))],
        out_shape=[jax.ShapeDtypeStruct((length, D), BF16)] * 3 + [jax.ShapeDtypeStruct((8, D), F32)],
        name="attn_bwd",
    )(prefix, qkv, qkv, qkv, attended, grad_attended, lse)


def normed(v):
    centre = v - jnp.mean(v, axis=-1, keepdims=True)
    inv = lax.rsqrt(jnp.mean(centre * centre, axis=-1, keepdims=True) + EPS)
    return centre * inv, inv


def normed_back(e, xhat, inv):
    return inv * (e - jnp.mean(e, axis=-1, keepdims=True) - xhat * jnp.mean(e * xhat, axis=-1, keepdims=True))


def colsum(v):
    rows, cols = v.shape
    return jnp.sum(v.reshape(rows // 8, 8, cols), axis=0)


def mid_kernel(
    x_ref, att_ref, g_ref, vec_ref, wide_ref, wo_ref, wu_ref, wd_ref,
    out_ref, n2_ref, n3_ref, n4_ref, gh_ref, gm_ref, gml_ref, ga_ref, svec_ref, swide_ref,
    act_ref, slope_ref,
):
    @pl.when(pl.program_id(0) == 0)
    def _():
        svec_ref[...] = jnp.zeros_like(svec_ref)
        swide_ref[...] = jnp.zeros_like(swide_ref)

    sub_gain, sub_bias, out_bias, ffn_gain, ffn_bias, down_bias = [vec_ref[i : i + 1, :] for i in range(6)]
    up_bias, inner_gain, inner_bias = [wide_ref[i : i + 1, :] for i in range(3)]
    xhat2, inv2 = normed(att_ref[...])
    n2 = (xhat2 * sub_gain + sub_bias).astype(BF16)
    n2_ref[...] = n2
    middle = x_ref[...].astype(F32) + nn(n2, wo_ref[...]) + out_bias
    xhat3, inv3 = normed(middle)
    n3 = (xhat3 * ffn_gain + ffn_bias).astype(BF16)
    n3_ref[...] = n3
    hidden = nn(n3, wu_ref[...]) + up_bias
    half = 0.5 + 0.5 * lax.erf(hidden * (2.0**-0.5))
    act_ref[...] = hidden * half
    slope_ref[...] = half + hidden * (jnp.exp(-0.5 * hidden * hidden) * 0.3989422804014327)
    xhat4, inv4 = normed(act_ref[...])
    n4 = (xhat4 * inner_gain + inner_bias).astype(BF16)
    n4_ref[...] = n4
    act_ref[...] = xhat4
    out_ref[...] = (middle + nn(n4, wd_ref[...]) + down_bias).astype(BF16)
    g = g_ref[...]
    e = nt(g, wd_ref[...])
    xhat4 = act_ref[...]
    swide_ref[1] += colsum(e * xhat4)
    swide_ref[2] += colsum(e)
    gh = normed_back(e * inner_gain, xhat4, inv4) * slope_ref[...]
    swide_ref[0] += colsum(gh)
    ghl = gh.astype(BF16)
    gh_ref[...] = ghl
    gf = g.astype(F32)
    e = nt(ghl, wu_ref[...])
    svec_ref[3] += colsum(e * xhat3)
    svec_ref[4] += colsum(e)
    gm = gf + normed_back(e * ffn_gain, xhat3, inv3)
    svec_ref[2] += colsum(gm)
    svec_ref[5] += colsum(gf)
    gm_ref[...] = gm
    gml = gm.astype(BF16)
    gml_ref[...] = gml
    e = nt(gml, wo_ref[...])
    svec_ref[0] += colsum(e * xhat2)
    svec_ref[1] += colsum(e)
    ga_ref[...] = normed_back(e * sub_gain, xhat2, inv2).astype(BF16)


def middle_stage(x, att, g, vecs, wides, wo, wu, wd, block=256):
    rows = x.shape[0]
    ff = wu.shape[1]
    row = lambda n: pl.BlockSpec((block, n), lambda i: (i, 0))
    whole = lambda s: pl.BlockSpec(s, lambda i: (0,) * len(s), pipeline_mode=pl.Buffered(1))
    sds = jax.ShapeDtypeStruct
    return pl.pallas_call(
        mid_kernel,
        grid=(rows // block,),
        in_specs=[row(D), row(D), row(D), whole(vecs.shape), whole(wides.shape), whole(wo.shape), whole(wu.shape), whole(wd.shape)],
        out_specs=[row(D), row(D), row(D), row(ff), row(ff), row(D), row(D), row(D), whole((6, 8, D)), whole((3, 8, ff))],
        out_shape=[
            sds((rows, D), BF16), sds((rows, D), BF16), sds((rows, D), BF16), sds((rows, ff), BF16), sds((rows, ff), BF16),
            sds((rows, D), F32), sds((rows, D), BF16), sds((rows, D), BF16), sds((6, 8, D), F32), sds((3, 8, ff), F32),
        ],
        scratch_shapes=[pltpu.VMEM((block, ff), F32), pltpu.VMEM((block, ff), F32)],
        compiler_params=pltpu.CompilerParams(vmem_limit_bytes=62 * 2**20),
        name="middle_stage",
    )(x, att, g, vecs, wides, wo, wu, wd)


def layer(tokens, grad_out, prefix, pre_gain, pre_bias, wqkv, q_bias, v_bias, vecs, wides, wo, wu, wd):
    x = tokens.astype(F32)
    xhat1, inv1 = normed(x)
    n1 = (xhat1 * pre_gain + pre_bias).astype(BF16)
    bias = jnp.concatenate([q_bias, jnp.zeros_like(q_bias), v_bias])
    qkv = (nn(n1, wqkv) + bias).astype(BF16)
    attended, lse = attn_fwd(prefix, qkv)
    out, n2, n3, n4, gh, gm, gml, ga, svec, swide = middle_stage(tokens, attended, grad_out, vecs, wides, wo, wu, wd)
    dq, dk, dv, dbias = attn_bwd(prefix, qkv, attended, ga, lse)
    g_down = tn(n4, grad_out)
    g_up = tn(n3, gh)
    g_out = tn(n2, gml)
    gproj = jnp.concatenate([dq, dk, dv], axis=1)
    g_qkv = tn(n1, gproj)
    e = nt(gproj, wqkv)
    g_pre_gain = jnp.sum(e * xhat1, axis=0)
    g_pre_bias = jnp.sum(e, axis=0)
    input_grad = gm + normed_back(e * pre_gain, xhat1, inv1)
    return out, input_grad, g_pre_gain, g_pre_bias, g_qkv, dbias[:2], jnp.sum(svec, 1), jnp.sum(swide, 1), g_out, g_up, g_down


def swap(value):
    return lax.ppermute(value, "tensor", ((0, 1), (1, 0)))


def pair_sum(grad, axis):
    size = grad.shape[axis] // 2
    own = lax.slice_in_dim(grad, 0, size, axis=axis)
    other = lax.slice_in_dim(grad, size, 2 * size, axis=axis)
    return own + swap(other.astype(BF16)).astype(F32)


def body(
    tokens, grad_out, prefix, pre_gain, pre_bias, qkv_weight, qv_bias, sub_gain, sub_bias, out_weight, out_bias,
    ffn_gain, ffn_bias, up_weight, up_bias, inner_gain, inner_bias, down_weight, down_bias,
):
    side = lax.axis_index("tensor")
    local = lax.dynamic_slice_in_dim(prefix, side, 1)
    both = lambda v, axis: jnp.concatenate([v, swap(v)], axis=axis)
    wqkv = both(qkv_weight, 2).reshape(D, 3 * D)
    wo = both(out_weight, 0)
    wu = both(up_weight, 1)
    wd = both(down_weight, 0)
    half, ff_half = D // 2, up_bias.shape[0]
    small = jnp.concatenate([qv_bias.reshape(-1), sub_gain, sub_bias, up_bias, inner_gain, inner_bias])
    far = swap(small)
    cut = lambda start, size: jnp.concatenate([small[start : start + size], far[start : start + size]])
    q_bias, v_bias, sgain, sbias = [cut(i * half, half) for i in range(4)]
    ub, ig, ib = [cut(4 * half + i * ff_half, ff_half) for i in range(3)]
    vecs = jnp.stack([sgain, sbias, out_bias, ffn_gain, ffn_bias, down_bias])
    wides = jnp.stack([ub, ig, ib])
    out, input_grad, g_pre_gain, g_pre_bias, g_qkv, g_qv, g_vec, g_wide, g_out, g_up, g_down = layer(
        tokens, grad_out, local, pre_gain, pre_bias, wqkv, q_bias, v_bias, vecs, wides, wo, wu, wd
    )
    g_qkv = pair_sum(g_qkv.reshape(D, 3, D), 2)
    g_out = pair_sum(g_out, 0)
    g_up = pair_sum(g_up, 1)
    g_down = pair_sum(g_down, 0)
    split = jnp.concatenate([g_qv.reshape(2, 2, half), g_vec[:2].reshape(2, 2, half)])
    split = jnp.concatenate([split.transpose(1, 0, 2).reshape(2, -1), g_wide.reshape(3, 2, ff_half).transpose(1, 0, 2).reshape(2, -1)], axis=1)
    split = split[0] + swap(split[1])
    full = jnp.concatenate([jnp.stack([g_pre_gain, g_pre_bias]), g_vec[2:]])
    g_down, g_up = lax.psum((g_down, g_up), "dp")
    g_qkv, g_out, split = lax.psum((g_qkv, g_out, split), "dp")
    full = lax.psum(full, ("dp", "tensor"))
    r = lambda i: split[i * half : (i + 1) * half]
    w = lambda i: split[4 * half + i * ff_half : 4 * half + (i + 1) * ff_half]
    return (
        out, input_grad, full[0], full[1], g_qkv, jnp.stack([r(0), r(1)]), r(2), r(3), g_out, full[2], full[3], full[4],
        g_up, w(0), w(1), w(2), g_down, full[5],
    )


def solution(mesh):
    rows = P(("dp", "tensor"), None)
    wide, tall, vec, whole = P(None, "tensor"), P("tensor", None), P("tensor"), P()
    cube = P(None, None, "tensor")
    return jax.shard_map(
        body,
        mesh=mesh,
        in_specs=(
            rows, rows, P("dp"), whole, whole, cube, wide, vec, vec, tall, whole, whole, whole, wide, vec, vec, vec, tall, whole,
        ),
        out_specs=(
            rows, rows, whole, whole, cube, wide, vec, vec, tall, whole, whole, whole, wide, vec, vec, vec, tall, whole,
        ),
        check_vma=False,
    )
```

```python
import functools
import math

import jax
import jax.numpy as jnp
from jax import lax
from jax.sharding import PartitionSpec as P
from jax.experimental import pallas as pl
from jax.experimental.pallas import tpu as pltpu

D = 768
HEAD_DIM = 64
PREFIX_MAX = 512
EPS = 1e-05
F32 = jnp.float32
BF16 = jnp.bfloat16
QB = 512


def nn(a, b):
    return lax.dot_general(a, b, (((1,), (0,)), ((), ())), preferred_element_type=F32)


def nt(a, b):
    return lax.dot_general(a, b, (((1,), (1,)), ((), ())), preferred_element_type=F32)


def tn(a, b):
    return lax.dot_general(a, b, (((0,), (0,)), ((), ())), preferred_element_type=F32)


def halves(v):
    left = lax.broadcasted_iota(jnp.int32, v.shape, 1) < HEAD_DIM
    zero = jnp.zeros_like(v)
    return jnp.where(left, v, zero), jnp.where(left, zero, v)


def spans(start, length, block):
    last = min(length, max(start + block, PREFIX_MAX))
    out = []
    if start:
        out.append((0, start, False))
    out.append((start, last, True))
    return out


def masked(scores, key_start, query_start, prefix):
    key_pos = key_start + lax.broadcasted_iota(jnp.int32, scores.shape, 0)
    query_pos = query_start + lax.broadcasted_iota(jnp.int32, scores.shape, 1)
    seen = key_pos <= query_pos
    if key_start < PREFIX_MAX:
        seen = seen | (key_pos < prefix)
    return jnp.where(seen, scores, -1e30)


def head_block(i, c):
    each = D // 256
    return i // each * 3 * each + c * each + lax.rem(i, each)


def attn_fwd_kernel(prefix_ref, q_ref, k_ref, v_ref, o_ref, lse_ref):
    length = q_ref.shape[0]
    prefix = prefix_ref[0]
    keys = halves(k_ref[...])
    value_t = v_ref[...].T
    for start in range(0, length, QB):
        query = q_ref[start : start + QB, :] * jnp.asarray(HEAD_DIM**-0.5, BF16)
        parts = []
        for head in range(2):
            scores = []
            for first, last, mask in spans(start, length, QB):
                s = nt(keys[head][first:last], query)
                scores.append(masked(s, first, start, prefix) if mask else s)
            peak = functools.reduce(jnp.maximum, [jnp.max(s, axis=0, keepdims=True) for s in scores])
            total = jnp.zeros_like(peak)
            mixed = jnp.zeros((HEAD_DIM, QB), F32)
            rows = slice(head * HEAD_DIM, (head + 1) * HEAD_DIM)
            for s, (first, last, _) in zip(scores, spans(start, length, QB)):
                w = jnp.exp(s - peak)
                total = total + jnp.sum(w, axis=0, keepdims=True)
                mixed = mixed + nn(value_t[rows, first:last], w.astype(BF16))
            parts.append(mixed / total)
            lse_ref[0, head : head + 1, start : start + QB] = peak + jnp.log(total)
        o_ref[start : start + QB, :] = jnp.concatenate(parts, axis=0).T


def attn_fwd(prefix, qkv):
    length = qkv.shape[0]
    pairs = D // 128
    col = lambda c: pl.BlockSpec((length, 128), lambda i, c=c: (0, head_block(i, c)))
    return pl.pallas_call(
        attn_fwd_kernel,
        grid=(pairs,),
        in_specs=[pl.BlockSpec(memory_space=pltpu.SMEM), col(0), col(1), col(2)],
        out_specs=[
            pl.BlockSpec((length, 128), lambda i: (0, i)),
            pl.BlockSpec((1, 8, length), lambda i: (i, 0, 0)),
        ],
        out_shape=[
            jax.ShapeDtypeStruct((length, D), F32),
            jax.ShapeDtypeStruct((pairs, 8, length), F32),
        ],
        name="attn_fwd",
    )(prefix, qkv, qkv, qkv)


def attn_bwd_kernel(prefix_ref, q_ref, k_ref, v_ref, o_ref, g_ref, lse_ref, dq_ref, dk_ref, dv_ref, bias_ref):
    length = q_ref.shape[0]
    prefix = prefix_ref[0]
    scale = HEAD_DIM**-0.5
    keys = halves(k_ref[...])
    values = halves(v_ref[...])
    key_t = k_ref[...].T
    delta_t = (o_ref[...] * g_ref[...].astype(F32)).T
    dk = [jnp.zeros((b - a, 128), F32) for a, b in zip(range(0, length, QB), range(QB, length + 1, QB))]
    dv = list(dk)
    qsum = jnp.zeros((8, 128), F32)
    for start in range(0, length, QB):
        cols = slice(start, start + QB)
        query = q_ref[cols, :] * jnp.asarray(scale, BF16)
        query_half = halves(query)
        grad = g_ref[cols, :]
        grad_half = halves(grad)
        parts = []
        for head in range(2):
            rows = slice(head * HEAD_DIM, (head + 1) * HEAD_DIM)
            lse = lse_ref[0, head : head + 1, cols]
            delta = jnp.sum(delta_t[rows, cols], axis=0, keepdims=True)
            dq = jnp.zeros((HEAD_DIM, QB), F32)
            for first in range(0, length, QB):
                live = [s for s in spans(start, length, QB) if s[0] <= first < s[1]]
                if not live:
                    continue
                last = first + QB
                s = nt(keys[head][first:last], query)
                if live[0][2]:
                    s = masked(s, first, start, prefix)
                w = jnp.exp(s - lse)
                dp = nt(values[head][first:last], grad)
                ds = (w * (dp - delta)).astype(BF16)
                b = first // QB
                dv[b] = dv[b] + nn(w.astype(BF16), grad_half[head])
                dk[b] = dk[b] + nn(ds, query_half[head])
                dq = dq + nn(key_t[rows, first:last], ds)
            parts.append(dq)
        dq = jnp.concatenate(parts, axis=0).T * scale
        qsum = qsum + jnp.sum(dq.reshape(QB // 8, 8, 128), axis=0)
        dq_ref[cols, :] = dq.astype(BF16)
    vsum = jnp.zeros((8, 128), F32)
    for b in range(length // QB):
        cols = slice(b * QB, (b + 1) * QB)
        dk_ref[cols, :] = dk[b].astype(BF16)
        dv_ref[cols, :] = dv[b].astype(BF16)
        vsum = vsum + jnp.sum(dv[b].reshape(QB // 8, 8, 128), axis=0)
    bias_ref[0:1, :] = jnp.sum(qsum, axis=0, keepdims=True)
    bias_ref[1:2, :] = jnp.sum(vsum, axis=0, keepdims=True)


def attn_bwd(prefix, qkv, attended, grad_attended, lse):
    length = qkv.shape[0]
    pairs = D // 128
    col = lambda c: pl.BlockSpec((length, 128), lambda i, c=c: (0, head_block(i, c)))
    one = pl.BlockSpec((length, 128), lambda i: (0, i))
    return pl.pallas_call(
        attn_bwd_kernel,
        grid=(pairs,),
        in_specs=[
            pl.BlockSpec(memory_space=pltpu.SMEM), col(0), col(1), col(2), one, one,
            pl.BlockSpec((1, 8, length), lambda i: (i, 0, 0)),
        ],
        out_specs=[one, one, one, pl.BlockSpec((8, 128), lambda i: (0, i))],
        out_shape=[jax.ShapeDtypeStruct((length, D), BF16)] * 3 + [jax.ShapeDtypeStruct((8, D), F32)],
        name="attn_bwd",
    )(prefix, qkv, qkv, qkv, attended, grad_attended, lse)


def normed(v):
    centre = v - jnp.mean(v, axis=-1, keepdims=True)
    inv = lax.rsqrt(jnp.mean(centre * centre, axis=-1, keepdims=True) + EPS)
    return centre * inv, inv


def normed_back(e, xhat, inv):
    return inv * (e - jnp.mean(e, axis=-1, keepdims=True) - xhat * jnp.mean(e * xhat, axis=-1, keepdims=True))


def colsum(v):
    rows, cols = v.shape
    return jnp.sum(v.reshape(rows // 8, 8, cols), axis=0)


def mid_kernel(
    x_ref, att_ref, g_ref, vec_ref, wide_ref, wo_ref, wu_ref, wd_ref,
    out_ref, n2_ref, n3_ref, n4_ref, gh_ref, gm_ref, gml_ref, ga_ref, svec_ref, swide_ref,
    act_ref, slope_ref,
):
    @pl.when(pl.program_id(0) == 0)
    def _():
        svec_ref[...] = jnp.zeros_like(svec_ref)
        swide_ref[...] = jnp.zeros_like(swide_ref)

    sub_gain, sub_bias, out_bias, ffn_gain, ffn_bias, down_bias = [vec_ref[i : i + 1, :] for i in range(6)]
    up_bias, inner_gain, inner_bias = [wide_ref[i : i + 1, :] for i in range(3)]
    xhat2, inv2 = normed(att_ref[...])
    n2 = (xhat2 * sub_gain + sub_bias).astype(BF16)
    n2_ref[...] = n2
    middle = x_ref[...].astype(F32) + nn(n2, wo_ref[...]) + out_bias
    xhat3, inv3 = normed(middle)
    n3 = (xhat3 * ffn_gain + ffn_bias).astype(BF16)
    n3_ref[...] = n3
    hidden = nn(n3, wu_ref[...]) + up_bias
    half = 0.5 + 0.5 * lax.erf(hidden * (2.0**-0.5))
    act_ref[...] = hidden * half
    slope_ref[...] = half + hidden * (jnp.exp(-0.5 * hidden * hidden) * 0.3989422804014327)
    xhat4, inv4 = normed(act_ref[...])
    n4 = (xhat4 * inner_gain + inner_bias).astype(BF16)
    n4_ref[...] = n4
    act_ref[...] = xhat4
    out_ref[...] = (middle + nn(n4, wd_ref[...]) + down_bias).astype(BF16)
    g = g_ref[...]
    e = nt(g, wd_ref[...])
    xhat4 = act_ref[...]
    swide_ref[1] += colsum(e * xhat4)
    swide_ref[2] += colsum(e)
    gh = normed_back(e * inner_gain, xhat4, inv4) * slope_ref[...]
    swide_ref[0] += colsum(gh)
    ghl = gh.astype(BF16)
    gh_ref[...] = ghl
    gf = g.astype(F32)
    e = nt(ghl, wu_ref[...])
    svec_ref[3] += colsum(e * xhat3)
    svec_ref[4] += colsum(e)
    gm = gf + normed_back(e * ffn_gain, xhat3, inv3)
    svec_ref[2] += colsum(gm)
    svec_ref[5] += colsum(gf)
    gm_ref[...] = gm
    gml = gm.astype(BF16)
    gml_ref[...] = gml
    e = nt(gml, wo_ref[...])
    svec_ref[0] += colsum(e * xhat2)
    svec_ref[1] += colsum(e)
    ga_ref[...] = normed_back(e * sub_gain, xhat2, inv2).astype(BF16)


def middle_stage(x, att, g, vecs, wides, wo, wu, wd, block=256):
    rows = x.shape[0]
    ff = wu.shape[1]
    row = lambda n: pl.BlockSpec((block, n), lambda i: (i, 0))
    whole = lambda s: pl.BlockSpec(s, lambda i: (0,) * len(s), pipeline_mode=pl.Buffered(1))
    sds = jax.ShapeDtypeStruct
    return pl.pallas_call(
        mid_kernel,
        grid=(rows // block,),
        in_specs=[row(D), row(D), row(D), whole(vecs.shape), whole(wides.shape), whole(wo.shape), whole(wu.shape), whole(wd.shape)],
        out_specs=[row(D), row(D), row(D), row(ff), row(ff), row(D), row(D), row(D), whole((6, 8, D)), whole((3, 8, ff))],
        out_shape=[
            sds((rows, D), BF16), sds((rows, D), BF16), sds((rows, D), BF16), sds((rows, ff), BF16), sds((rows, ff), BF16),
            sds((rows, D), F32), sds((rows, D), BF16), sds((rows, D), BF16), sds((6, 8, D), F32), sds((3, 8, ff), F32),
        ],
        scratch_shapes=[pltpu.VMEM((block, ff), F32), pltpu.VMEM((block, ff), F32)],
        compiler_params=pltpu.CompilerParams(vmem_limit_bytes=62 * 2**20),
        name="middle_stage",
    )(x, att, g, vecs, wides, wo, wu, wd)


def layer(tokens, grad_out, prefix, pre_gain, pre_bias, wqkv, bias, vecs, wides, wo, wu, wd):
    x = tokens.astype(F32)
    xhat1, inv1 = normed(x)
    n1 = (xhat1 * pre_gain + pre_bias).astype(BF16)
    qkv = (nn(n1, wqkv) + bias).astype(BF16)
    attended, lse = attn_fwd(prefix, qkv)
    out, n2, n3, n4, gh, gm, gml, ga, svec, swide = middle_stage(tokens, attended, grad_out, vecs, wides, wo, wu, wd)
    dq, dk, dv, dbias = attn_bwd(prefix, qkv, attended, ga, lse)
    g_down = tn(n4, grad_out).astype(BF16)
    g_up = tn(n3, gh).astype(BF16)
    g_out = tn(n2, gml).astype(BF16)
    h = D // 2
    gproj = jnp.concatenate([v[:, s] for s in (slice(0, h), slice(h, D)) for v in (dq, dk, dv)], axis=1)
    g_qkv = tn(n1, gproj).astype(BF16)
    e = nt(gproj, wqkv)
    g_pre = jnp.stack([jnp.sum(e * xhat1, axis=0), jnp.sum(e, axis=0)])
    input_grad = gm + normed_back(e * pre_gain, xhat1, inv1)
    return out, input_grad, g_pre, g_qkv, dbias, jnp.sum(svec, 1), jnp.sum(swide, 1), g_out, g_up, g_down


def grid_of(count):
    side = 1
    while 2 * side**3 < count:
        side += 1
    return (2 * side, side, side) if 2 * side**3 == count else (count, 1, 1)


class Piece:
    def __init__(self, dims, first, near, far, total, bufs, sems, place):
        self.dims, self.first, self.near, self.far, self.total = dims, first, near, far, total
        self.mine, self.pair, self.land, self.part, self.land2, self.part2, self.land3 = bufs
        self.sems, self.place = sems, place
        self.count = 0
        self.flight = []

    def send(self, src, dst, where):
        copy = pltpu.make_async_remote_copy(
            src_ref=src, dst_ref=dst, send_sem=self.sems.at[0, self.count], recv_sem=self.sems.at[1, self.count],
            device_id=where, device_id_type=pl.DeviceIdType.MESH,
        )
        self.count += 1
        copy.start()
        self.flight.append(copy)

    def settle(self):
        for copy in self.flight:
            copy.wait()
        self.flight = []

    def device(self, axis, shift):
        at = list(self.place[:3])
        at[axis] = lax.rem(at[axis] + shift, self.dims[axis])
        nz, ny, nx = self.dims
        return at[axis], ((at[0] * ny + at[1]) * nx + at[2], self.place[3])

    def steps(self):
        z, y, x = self.place[:3]
        nz, ny, nx = self.dims
        one, two = (2, 1) if self.first == "x" else (1, 2)
        pick1 = lambda ref, p: ref.at[:, :, p] if one == 2 else ref.at[:, p]
        own1, own2 = (x, y) if one == 2 else (y, x)

        def start():
            local = pltpu.make_async_copy(self.near, self.mine, self.sems.at[0, self.count])
            self.count += 1
            local.start()
            self.send(self.far, self.pair, (self.place[4], 1 - self.place[3]))
            self.flight.append(local)

        def pair_add():
            self.settle()
            def one_row(i, _):
                self.mine[i] = (self.mine[i].astype(F32) + self.pair[i].astype(F32)).astype(self.mine.dtype)
                return 0
            lax.fori_loop(0, nz, one_row, 0)
            for s in range(1, self.dims[one]):
                p, dev = self.device(one, s)
                self.send(pick1(self.mine, p), self.land.at[s - 1], dev)

        def add_one():
            self.settle()
            def one_row(i, _):
                v = (self.mine[i, :, x] if one == 2 else self.mine[i, y]).astype(F32)
                for s in range(1, self.dims[one]):
                    v = v + self.land[s - 1, i].astype(F32)
                self.part[i] = v.astype(self.part.dtype)
                return 0
            lax.fori_loop(0, nz, one_row, 0)
            for s in range(1, self.dims[two]):
                p, dev = self.device(two, s)
                self.send(self.part.at[:, p], self.land2.at[s - 1], dev)

        def add_two():
            self.settle()
            def one_row(i, _):
                v = self.part[i, own2].astype(F32)
                for s in range(1, self.dims[two]):
                    v = v + self.land2[s - 1, i].astype(F32)
                self.part2[i] = v.astype(self.part2.dtype)
                return 0
            lax.fori_loop(0, nz, one_row, 0)
            for s in range(1, nz):
                p, dev = self.device(0, s)
                self.send(self.part2.at[p], self.land3.at[s - 1], dev)

        def add_three():
            self.settle()
            v = self.part2[z].astype(F32)
            for s in range(1, nz):
                v = v + self.land3[s - 1].astype(F32)
            self.total[z, y, x] = v.astype(self.total.dtype)
            spread(0, self.total.at[z, y, x])

        def spread(axis, ref):
            for s in range(1, self.dims[axis]):
                self.send(ref, ref, self.device(axis, s)[1])

        def wide_two():
            self.settle()
            spread(two, self.total.at[:, y, x])

        def wide_one():
            self.settle()
            spread(one, self.total.at[:, :, x] if one == 2 else self.total.at[:, y])

        return [start, pair_add, add_one, add_two, add_three, wide_two, wide_one, self.settle]


def buffers(dims, rows, width, dtype, first):
    nz, ny, nx = dims
    na, nb = (nx, ny) if first == "x" else (ny, nx)
    tail = (rows, width)
    shapes = [
        (nz, ny, nx) + tail, (nz, ny, nx) + tail, (max(na - 1, 1), nz, nb) + tail, (nz, nb) + tail,
        (max(nb - 1, 1), nz) + tail, (nz,) + tail, (max(nz - 1, 1),) + tail,
    ]
    copies = 2 + 2 * (na + nb + nz - 3)
    return [pltpu.VMEM(s, dtype) for s in shapes] + [pltpu.SemaphoreType.DMA((2, copies))]


def reduce_kernel(dims, views, firsts, *refs):
    count = len(firsts)
    sources = refs[: len(views)]
    totals = refs[len(views) : len(views) + count]
    scratch = refs[len(views) + count :]
    index, side = lax.axis_index("dp"), lax.axis_index("tensor")
    nz, ny, nx = dims
    place = (index // (ny * nx), lax.rem(index // nx, ny), lax.rem(index, nx), side, index)
    barrier = pltpu.get_barrier_semaphore()
    peers = [(index, 1 - side)]
    probe = Piece(dims, "x", None, None, None, [None] * 7, None, place)
    for axis in range(3):
        for s in range(1, dims[axis]):
            peers.append(probe.device(axis, s)[1])
    for peer in peers:
        pl.semaphore_signal(barrier, inc=1, device_id=peer, device_id_type=pl.DeviceIdType.MESH)
    pl.semaphore_wait(barrier, len(peers))
    plans = []
    at = 0
    for source, view in zip(sources, views):
        for near, far in view(source):
            plans.append(Piece(dims, firsts[at], near, far, totals[at], scratch[8 * at : 8 * at + 7], scratch[8 * at + 7], place).steps())
            at += 1
    slots = len(plans[0]) + (count + 1) // 2 - 1
    for slot in range(slots):
        for i, plan in enumerate(plans):
            if 0 <= slot - i // 2 < len(plan):
                plan[slot - i // 2]()


def all_reduce(dims, grads, small):
    g_down, g_up, g_qkv, g_out = grads
    nz, ny, nx = dims
    parts = nz * ny * nx
    ff = g_down.shape[0] // 2
    half = ff // 2
    rows_d, rows_u, rows_o = half // parts, D // parts, D // 2 // parts
    cut = 640
    down = g_down.reshape(2, 2, nz, ny, nx, rows_d, D)
    up = g_up.reshape(nz, ny, nx, rows_u, 2 * ff)
    qkv = g_qkv.reshape(nz, ny, nx, rows_u, 3 * D)
    out = g_out.reshape(2, nz, ny, nx, rows_o, D)
    cols = lambda r, a, n: r.at[:, :, :, :, a : a + n]
    wide = 3 * D // 2
    views = [
        lambda r: [(r.at[0, 0], r.at[1, 0]), (r.at[0, 1], r.at[1, 1])],
        lambda r: [(cols(r, 0, half), cols(r, ff, half)), (cols(r, half, half), cols(r, ff + half, half))],
        lambda r: [(cols(r, 0, cut), cols(r, wide, cut)), (cols(r, cut, wide - cut), cols(r, wide + cut, wide - cut))],
        lambda r: [(r.at[0], r.at[1])],
        lambda r: [(r.at[0], r.at[1])],
    ]
    sizes = [(rows_d, D, BF16)] * 2 + [(rows_u, half, BF16)] * 2 + [(rows_u, cut, BF16), (rows_u, wide - cut, BF16), (rows_o, D, BF16)]
    sizes.append(small.shape[-2:] + (F32,))
    firsts = ["x", "y"] * 3 + ["y", "x"]
    scratch = []
    for (r, w, t), first in zip(sizes, firsts):
        scratch += buffers(dims, r, w, t, first)
    totals = pl.pallas_call(
        functools.partial(reduce_kernel, dims, views, firsts),
        in_specs=[pl.BlockSpec(memory_space=pl.ANY)] * 5,
        out_specs=[pl.BlockSpec(memory_space=pltpu.VMEM)] * len(sizes),
        out_shape=[jax.ShapeDtypeStruct((nz, ny, nx, r, w), t) for r, w, t in sizes],
        scratch_shapes=scratch,
        compiler_params=pltpu.CompilerParams(collective_id=0, has_side_effects=True, vmem_limit_bytes=60 * 2**20),
        name="all_reduce",
    )(down, up, qkv, out, small)
    flat = [t.reshape(-1, t.shape[-1]) for t in totals]
    return (
        jnp.concatenate(flat[:2], axis=0).astype(F32),
        jnp.concatenate(flat[2:4], axis=1).astype(F32),
        jnp.concatenate(flat[4:6], axis=1).astype(F32),
        flat[6].astype(F32),
        flat[7].reshape(-1),
    )


def swap(value):
    return lax.ppermute(value, "tensor", ((0, 1), (1, 0)))


def body(
    dims, tokens, grad_out, prefix, pre_gain, pre_bias, qkv_weight, qv_bias, sub_gain, sub_bias, out_weight, out_bias,
    ffn_gain, ffn_bias, up_weight, up_bias, inner_gain, inner_bias, down_weight, down_bias,
):
    side = lax.axis_index("tensor")
    local = lax.dynamic_slice_in_dim(prefix, side, 1)
    both = lambda v, axis: jnp.concatenate([v, swap(v)], axis=axis)
    half, ff_half = D // 2, up_bias.shape[0]
    wqkv = both(qkv_weight.reshape(D, 3 * half), 1)
    wo = both(out_weight, 0)
    wu = both(up_weight, 1)
    wd = both(down_weight, 0)
    near = jnp.concatenate([qv_bias.reshape(-1), sub_gain, sub_bias, up_bias, inner_gain, inner_bias])
    far = swap(near)
    cut = lambda start, size: jnp.concatenate([near[start : start + size], far[start : start + size]])
    zero = jnp.zeros((half,), F32)
    bias = jnp.concatenate([p for v in (near, far) for p in (v[:half], zero, v[half : 2 * half])])
    sgain, sbias = [cut(i * half, half) for i in (2, 3)]
    ub, ig, ib = [cut(4 * half + i * ff_half, ff_half) for i in range(3)]
    vecs = jnp.stack([sgain, sbias, out_bias, ffn_gain, ffn_bias, down_bias])
    wides = jnp.stack([ub, ig, ib])
    out, input_grad, g_pre, g_qkv, g_qv, g_vec, g_wide, g_out, g_up, g_down = layer(
        tokens, grad_out, local, pre_gain, pre_bias, wqkv, bias, vecs, wides, wo, wu, wd
    )
    shared = jnp.concatenate([g_pre.reshape(-1), g_vec[2:].reshape(-1)])
    rows = -(-(4 * half + 3 * ff_half + 6 * D) // (128 * 8 * math.prod(dims))) * 8
    pad = jnp.zeros((rows * 128 * math.prod(dims) - (4 * half + 3 * ff_half + 6 * D),), F32)
    pack = lambda i: jnp.concatenate(
        [v[j, i * n : (i + 1) * n] for v, m, n in ((g_qv, 2, half), (g_vec, 2, half), (g_wide, 3, ff_half)) for j in range(m)] + [shared, pad]
    )
    small = jnp.stack([pack(0), pack(1)]).reshape((2,) + dims + (rows, 128))
    g_down, g_up, g_qkv, g_out, small = all_reduce(dims, (g_down, g_up, g_qkv, g_out), small)
    r = lambda i: small[i * half : (i + 1) * half]
    w = lambda i: small[4 * half + i * ff_half : 4 * half + (i + 1) * ff_half]
    base = 4 * half + 3 * ff_half
    f = lambda i: small[base + i * D : base + (i + 1) * D]
    return (
        out, input_grad, f(0), f(1), g_qkv.reshape(D, 3, half), small[: 2 * half].reshape(2, half), r(2), r(3), g_out,
        f(2), f(3), f(4), g_up, w(0), w(1), w(2), g_down, f(5),
    )


def solution(mesh):
    rows = P(("dp", "tensor"), None)
    wide, tall, vec, whole = P(None, "tensor"), P("tensor", None), P("tensor"), P()
    cube = P(None, None, "tensor")
    return jax.shard_map(
        functools.partial(body, grid_of(mesh.shape["dp"])),
        mesh=mesh,
        in_specs=(
            rows, rows, P("dp"), whole, whole, cube, wide, vec, vec, tall, whole, whole, whole, wide, vec, vec, vec, tall, whole,
        ),
        out_specs=(
            rows, rows, whole, whole, cube, wide, vec, vec, tall, whole, whole, whole, wide, vec, vec, vec, tall, whole,
        ),
        check_vma=False,
    )
```

```python
import functools
import math

import jax
import jax.numpy as jnp
from jax import lax
from jax.sharding import PartitionSpec as P
from jax.experimental import pallas as pl
from jax.experimental.pallas import tpu as pltpu

D = 768
HEAD_DIM = 64
PREFIX_MAX = 512
EPS = 1e-05
F32 = jnp.float32
BF16 = jnp.bfloat16
QB = 512


def nn(a, b):
    return lax.dot_general(a, b, (((1,), (0,)), ((), ())), preferred_element_type=F32)


def nt(a, b):
    return lax.dot_general(a, b, (((1,), (1,)), ((), ())), preferred_element_type=F32)


def tn(a, b):
    return lax.dot_general(a, b, (((0,), (0,)), ((), ())), preferred_element_type=F32)


def halves(v):
    left = lax.broadcasted_iota(jnp.int32, v.shape, 1) < HEAD_DIM
    zero = jnp.zeros_like(v)
    return jnp.where(left, v, zero), jnp.where(left, zero, v)


def spans(start, length, block):
    last = min(length, max(start + block, PREFIX_MAX))
    out = []
    if start:
        out.append((0, start, False))
    out.append((start, last, True))
    return out


def masked(scores, key_start, query_start, prefix):
    key_pos = key_start + lax.broadcasted_iota(jnp.int32, scores.shape, 0)
    query_pos = query_start + lax.broadcasted_iota(jnp.int32, scores.shape, 1)
    seen = key_pos <= query_pos
    if key_start < PREFIX_MAX:
        seen = seen | (key_pos < prefix)
    return jnp.where(seen, scores, -1e30)


def head_block(i, c):
    each = D // 256
    return i // each * 3 * each + c * each + lax.rem(i, each)


def attn_fwd_kernel(prefix_ref, q_ref, k_ref, v_ref, o_ref, lse_ref):
    length = q_ref.shape[0]
    prefix = prefix_ref[0]
    keys = halves(k_ref[...])
    value_t = v_ref[...].T
    for start in range(0, length, QB):
        query = q_ref[start : start + QB, :] * jnp.asarray(HEAD_DIM**-0.5, BF16)
        parts = []
        for head in range(2):
            scores = []
            for first, last, mask in spans(start, length, QB):
                s = nt(keys[head][first:last], query)
                scores.append(masked(s, first, start, prefix) if mask else s)
            peak = functools.reduce(jnp.maximum, [jnp.max(s, axis=0, keepdims=True) for s in scores])
            total = jnp.zeros_like(peak)
            mixed = jnp.zeros((HEAD_DIM, QB), F32)
            rows = slice(head * HEAD_DIM, (head + 1) * HEAD_DIM)
            for s, (first, last, _) in zip(scores, spans(start, length, QB)):
                w = jnp.exp(s - peak)
                total = total + jnp.sum(w, axis=0, keepdims=True)
                mixed = mixed + nn(value_t[rows, first:last], w.astype(BF16))
            parts.append(mixed / total)
            lse_ref[0, head : head + 1, start : start + QB] = peak + jnp.log(total)
        o_ref[start : start + QB, :] = jnp.concatenate(parts, axis=0).T


def attn_fwd(prefix, qkv):
    length = qkv.shape[0]
    pairs = D // 128
    col = lambda c: pl.BlockSpec((length, 128), lambda i, c=c: (0, head_block(i, c)))
    return pl.pallas_call(
        attn_fwd_kernel,
        grid=(pairs,),
        in_specs=[pl.BlockSpec(memory_space=pltpu.SMEM), col(0), col(1), col(2)],
        out_specs=[
            pl.BlockSpec((length, 128), lambda i: (0, i)),
            pl.BlockSpec((1, 8, length), lambda i: (i, 0, 0)),
        ],
        out_shape=[
            jax.ShapeDtypeStruct((length, D), F32),
            jax.ShapeDtypeStruct((pairs, 8, length), F32),
        ],
        name="attn_fwd",
    )(prefix, qkv, qkv, qkv)


def attn_bwd_kernel(prefix_ref, q_ref, k_ref, v_ref, o_ref, g_ref, lse_ref, dq_ref, dk_ref, dv_ref, bias_ref):
    length = q_ref.shape[0]
    prefix = prefix_ref[0]
    scale = HEAD_DIM**-0.5
    keys = halves(k_ref[...])
    values = halves(v_ref[...])
    key_t = k_ref[...].T
    delta_t = (o_ref[...] * g_ref[...].astype(F32)).T
    dk = [jnp.zeros((b - a, 128), F32) for a, b in zip(range(0, length, QB), range(QB, length + 1, QB))]
    dv = list(dk)
    qsum = jnp.zeros((8, 128), F32)
    for start in range(0, length, QB):
        cols = slice(start, start + QB)
        query = q_ref[cols, :] * jnp.asarray(scale, BF16)
        query_half = halves(query)
        grad = g_ref[cols, :]
        grad_half = halves(grad)
        parts = []
        for head in range(2):
            rows = slice(head * HEAD_DIM, (head + 1) * HEAD_DIM)
            lse = lse_ref[0, head : head + 1, cols]
            delta = jnp.sum(delta_t[rows, cols], axis=0, keepdims=True)
            dq = jnp.zeros((HEAD_DIM, QB), F32)
            for first in range(0, length, QB):
                live = [s for s in spans(start, length, QB) if s[0] <= first < s[1]]
                if not live:
                    continue
                last = first + QB
                s = nt(keys[head][first:last], query)
                if live[0][2]:
                    s = masked(s, first, start, prefix)
                w = jnp.exp(s - lse)
                dp = nt(values[head][first:last], grad)
                ds = (w * (dp - delta)).astype(BF16)
                b = first // QB
                dv[b] = dv[b] + nn(w.astype(BF16), grad_half[head])
                dk[b] = dk[b] + nn(ds, query_half[head])
                dq = dq + nn(key_t[rows, first:last], ds)
            parts.append(dq)
        dq = jnp.concatenate(parts, axis=0).T * scale
        qsum = qsum + jnp.sum(dq.reshape(QB // 8, 8, 128), axis=0)
        dq_ref[cols, :] = dq.astype(BF16)
    vsum = jnp.zeros((8, 128), F32)
    for b in range(length // QB):
        cols = slice(b * QB, (b + 1) * QB)
        dk_ref[cols, :] = dk[b].astype(BF16)
        dv_ref[cols, :] = dv[b].astype(BF16)
        vsum = vsum + jnp.sum(dv[b].reshape(QB // 8, 8, 128), axis=0)
    bias_ref[0:1, :] = jnp.sum(qsum, axis=0, keepdims=True)
    bias_ref[1:2, :] = jnp.sum(vsum, axis=0, keepdims=True)


def attn_bwd(prefix, qkv, attended, grad_attended, lse):
    length = qkv.shape[0]
    pairs = D // 128
    col = lambda c: pl.BlockSpec((length, 128), lambda i, c=c: (0, head_block(i, c)))
    one = pl.BlockSpec((length, 128), lambda i: (0, i))
    return pl.pallas_call(
        attn_bwd_kernel,
        grid=(pairs,),
        in_specs=[
            pl.BlockSpec(memory_space=pltpu.SMEM), col(0), col(1), col(2), one, one,
            pl.BlockSpec((1, 8, length), lambda i: (i, 0, 0)),
        ],
        out_specs=[one, one, one, pl.BlockSpec((8, 128), lambda i: (0, i))],
        out_shape=[jax.ShapeDtypeStruct((length, D), BF16)] * 3 + [jax.ShapeDtypeStruct((8, D), F32)],
        name="attn_bwd",
    )(prefix, qkv, qkv, qkv, attended, grad_attended, lse)


def normed(v):
    centre = v - jnp.mean(v, axis=-1, keepdims=True)
    inv = lax.rsqrt(jnp.mean(centre * centre, axis=-1, keepdims=True) + EPS)
    return centre * inv, inv


def normed_back(e, xhat, inv):
    return inv * (e - jnp.mean(e, axis=-1, keepdims=True) - xhat * jnp.mean(e * xhat, axis=-1, keepdims=True))


def colsum(v):
    rows, cols = v.shape
    return jnp.sum(v.reshape(rows // 8, 8, cols), axis=0)


def mid_kernel(
    x_ref, att_ref, g_ref, vec_ref, wide_ref, wo_ref, wu_ref, wd_ref,
    out_ref, n2_ref, n3_ref, n4_ref, gh_ref, gm_ref, gml_ref, ga_ref, svec_ref, swide_ref,
    act_ref, slope_ref,
):
    @pl.when(pl.program_id(0) == 0)
    def _():
        svec_ref[...] = jnp.zeros_like(svec_ref)
        swide_ref[...] = jnp.zeros_like(swide_ref)

    sub_gain, sub_bias, out_bias, ffn_gain, ffn_bias, down_bias = [vec_ref[i : i + 1, :] for i in range(6)]
    up_bias, inner_gain, inner_bias = [wide_ref[i : i + 1, :] for i in range(3)]
    xhat2, inv2 = normed(att_ref[...])
    n2 = (xhat2 * sub_gain + sub_bias).astype(BF16)
    n2_ref[...] = n2
    middle = x_ref[...].astype(F32) + nn(n2, wo_ref[...]) + out_bias
    xhat3, inv3 = normed(middle)
    n3 = (xhat3 * ffn_gain + ffn_bias).astype(BF16)
    n3_ref[...] = n3
    hidden = nn(n3, wu_ref[...]) + up_bias
    half = 0.5 + 0.5 * lax.erf(hidden * (2.0**-0.5))
    act_ref[...] = hidden * half
    slope_ref[...] = half + hidden * (jnp.exp(-0.5 * hidden * hidden) * 0.3989422804014327)
    xhat4, inv4 = normed(act_ref[...])
    n4 = (xhat4 * inner_gain + inner_bias).astype(BF16)
    n4_ref[...] = n4
    act_ref[...] = xhat4
    out_ref[...] = (middle + nn(n4, wd_ref[...]) + down_bias).astype(BF16)
    g = g_ref[...]
    e = nt(g, wd_ref[...])
    xhat4 = act_ref[...]
    swide_ref[1] += colsum(e * xhat4)
    swide_ref[2] += colsum(e)
    gh = normed_back(e * inner_gain, xhat4, inv4) * slope_ref[...]
    swide_ref[0] += colsum(gh)
    ghl = gh.astype(BF16)
    gh_ref[...] = ghl
    gf = g.astype(F32)
    e = nt(ghl, wu_ref[...])
    svec_ref[3] += colsum(e * xhat3)
    svec_ref[4] += colsum(e)
    gm = gf + normed_back(e * ffn_gain, xhat3, inv3)
    svec_ref[2] += colsum(gm)
    svec_ref[5] += colsum(gf)
    gm_ref[...] = gm
    gml = gm.astype(BF16)
    gml_ref[...] = gml
    e = nt(gml, wo_ref[...])
    svec_ref[0] += colsum(e * xhat2)
    svec_ref[1] += colsum(e)
    ga_ref[...] = normed_back(e * sub_gain, xhat2, inv2).astype(BF16)


def middle_stage(x, att, g, vecs, wides, wo, wu, wd, block=256):
    rows = x.shape[0]
    ff = wu.shape[1]
    row = lambda n: pl.BlockSpec((block, n), lambda i: (i, 0))
    whole = lambda s: pl.BlockSpec(s, lambda i: (0,) * len(s), pipeline_mode=pl.Buffered(1))
    sds = jax.ShapeDtypeStruct
    return pl.pallas_call(
        mid_kernel,
        grid=(rows // block,),
        in_specs=[row(D), row(D), row(D), whole(vecs.shape), whole(wides.shape), whole(wo.shape), whole(wu.shape), whole(wd.shape)],
        out_specs=[row(D), row(D), row(D), row(ff), row(ff), row(D), row(D), row(D), whole((6, 8, D)), whole((3, 8, ff))],
        out_shape=[
            sds((rows, D), BF16), sds((rows, D), BF16), sds((rows, D), BF16), sds((rows, ff), BF16), sds((rows, ff), BF16),
            sds((rows, D), F32), sds((rows, D), BF16), sds((rows, D), BF16), sds((6, 8, D), F32), sds((3, 8, ff), F32),
        ],
        scratch_shapes=[pltpu.VMEM((block, ff), F32), pltpu.VMEM((block, ff), F32)],
        compiler_params=pltpu.CompilerParams(vmem_limit_bytes=62 * 2**20),
        name="middle_stage",
    )(x, att, g, vecs, wides, wo, wu, wd)


def front(tokens, grad_out, prefix, pre_gain, pre_bias, wqkv, bias, vecs, wides, wo, wu, wd):
    x = tokens.astype(F32)
    xhat1, _ = normed(x)
    n1 = (xhat1 * pre_gain + pre_bias).astype(BF16)
    qkv = (nn(n1, wqkv) + bias).astype(BF16)
    attended, lse = attn_fwd(prefix, qkv)
    out, n2, n3, n4, gh, gm, gml, ga, svec, swide = middle_stage(tokens, attended, grad_out, vecs, wides, wo, wu, wd)
    g_down = tn(n4, grad_out).astype(BF16)
    g_up = tn(n3, gh).astype(BF16)
    g_out = tn(n2, gml).astype(BF16)
    return n1, qkv, attended, lse, out, gm, ga, svec, swide, g_down, g_up, g_out


def back(prefix, tokens, pre_gain, wqkv, n1, qkv, attended, lse, gm, ga):
    xhat1, inv1 = normed(tokens.astype(F32))
    dq, dk, dv, dbias = attn_bwd(prefix, qkv, attended, ga, lse)
    h = D // 2
    gproj = jnp.concatenate([v[:, s] for s in (slice(0, h), slice(h, D)) for v in (dq, dk, dv)], axis=1)
    g_qkv = tn(n1, gproj).astype(BF16)
    e = nt(gproj, wqkv)
    g_pre = jnp.stack([jnp.sum(e * xhat1, axis=0), jnp.sum(e, axis=0)])
    input_grad = gm + normed_back(e * pre_gain, xhat1, inv1)
    return input_grad, g_pre, g_qkv, dbias


def grid_of(count):
    side = 1
    while 2 * side**3 < count:
        side += 1
    return (2 * side, side, side) if 2 * side**3 == count else (count, 1, 1)


class Piece:
    def __init__(self, dims, first, near, far, total, bufs, sems, place):
        self.dims, self.first, self.near, self.far, self.total = dims, first, near, far, total
        self.mine, self.pair, self.land, self.part, self.land2, self.part2, self.land3 = bufs
        self.sems, self.place = sems, place
        self.count = 0
        self.flight = []

    def send(self, src, dst, where):
        copy = pltpu.make_async_remote_copy(
            src_ref=src, dst_ref=dst, send_sem=self.sems.at[0, self.count], recv_sem=self.sems.at[1, self.count],
            device_id=where, device_id_type=pl.DeviceIdType.MESH,
        )
        self.count += 1
        copy.start()
        self.flight.append(copy)

    def settle(self):
        for copy in self.flight:
            copy.wait()
        self.flight = []

    def device(self, axis, shift):
        at = list(self.place[:3])
        at[axis] = lax.rem(at[axis] + shift, self.dims[axis])
        nz, ny, nx = self.dims
        return at[axis], ((at[0] * ny + at[1]) * nx + at[2], self.place[3])

    def steps(self):
        z, y, x = self.place[:3]
        nz, ny, nx = self.dims
        one, two = (2, 1) if self.first == "x" else (1, 2)
        pick1 = lambda ref, p: ref.at[:, :, p] if one == 2 else ref.at[:, p]
        own1, own2 = (x, y) if one == 2 else (y, x)

        def start():
            local = pltpu.make_async_copy(self.near, self.mine, self.sems.at[0, self.count])
            self.count += 1
            local.start()
            self.send(self.far, self.pair, (self.place[4], 1 - self.place[3]))
            self.flight.append(local)

        def pair_add():
            self.settle()
            def one_row(i, _):
                self.mine[i] = (self.mine[i].astype(F32) + self.pair[i].astype(F32)).astype(self.mine.dtype)
                return 0
            lax.fori_loop(0, nz, one_row, 0)
            for s in range(1, self.dims[one]):
                p, dev = self.device(one, s)
                self.send(pick1(self.mine, p), self.land.at[s - 1], dev)

        def add_one():
            self.settle()
            def one_row(i, _):
                v = (self.mine[i, :, x] if one == 2 else self.mine[i, y]).astype(F32)
                for s in range(1, self.dims[one]):
                    v = v + self.land[s - 1, i].astype(F32)
                self.part[i] = v.astype(self.part.dtype)
                return 0
            lax.fori_loop(0, nz, one_row, 0)
            for s in range(1, self.dims[two]):
                p, dev = self.device(two, s)
                self.send(self.part.at[:, p], self.land2.at[s - 1], dev)

        def add_two():
            self.settle()
            def one_row(i, _):
                v = self.part[i, own2].astype(F32)
                for s in range(1, self.dims[two]):
                    v = v + self.land2[s - 1, i].astype(F32)
                self.part2[i] = v.astype(self.part2.dtype)
                return 0
            lax.fori_loop(0, nz, one_row, 0)
            for s in range(1, nz):
                p, dev = self.device(0, s)
                self.send(self.part2.at[p], self.land3.at[s - 1], dev)

        def add_three():
            self.settle()
            v = self.part2[z].astype(F32)
            for s in range(1, nz):
                v = v + self.land3[s - 1].astype(F32)
            self.total[z, y, x] = v.astype(self.total.dtype)
            spread(0, self.total.at[z, y, x])

        def spread(axis, ref):
            for s in range(1, self.dims[axis]):
                self.send(ref, ref, self.device(axis, s)[1])

        def wide_two():
            self.settle()
            spread(two, self.total.at[:, y, x])

        def wide_one():
            self.settle()
            spread(one, self.total.at[:, :, x] if one == 2 else self.total.at[:, y])

        return [start, pair_add, add_one, add_two, add_three, wide_two, wide_one, self.settle]


def buffers(dims, rows, width, dtype, first):
    nz, ny, nx = dims
    na, nb = (nx, ny) if first == "x" else (ny, nx)
    tail = (rows, width)
    shapes = [
        (nz, ny, nx) + tail, (nz, ny, nx) + tail, (max(na - 1, 1), nz, nb) + tail, (nz, nb) + tail,
        (max(nb - 1, 1), nz) + tail, (nz,) + tail, (max(nz - 1, 1),) + tail,
    ]
    copies = 2 + 2 * (na + nb + nz - 3)
    return [pltpu.VMEM(s, dtype) for s in shapes] + [pltpu.SemaphoreType.DMA((2, copies))]


def reduce_kernel(dims, views, firsts, *refs):
    count = len(firsts)
    sources = refs[: len(views)]
    totals = refs[len(views) : len(views) + count]
    scratch = refs[len(views) + count :]
    index, side = lax.axis_index("dp"), lax.axis_index("tensor")
    nz, ny, nx = dims
    place = (index // (ny * nx), lax.rem(index // nx, ny), lax.rem(index, nx), side, index)
    barrier = pltpu.get_barrier_semaphore()
    peers = [(index, 1 - side)]
    probe = Piece(dims, "x", None, None, None, [None] * 7, None, place)
    for axis in range(3):
        for s in range(1, dims[axis]):
            peers.append(probe.device(axis, s)[1])
    for peer in peers:
        pl.semaphore_signal(barrier, inc=1, device_id=peer, device_id_type=pl.DeviceIdType.MESH)
    pl.semaphore_wait(barrier, len(peers))
    plans = []
    at = 0
    for source, view in zip(sources, views):
        for near, far in view(source):
            plans.append(Piece(dims, firsts[at], near, far, totals[at], scratch[8 * at : 8 * at + 7], scratch[8 * at + 7], place).steps())
            at += 1
    slots = len(plans[0]) + (count + 1) // 2 - 1
    for slot in range(slots):
        for i, plan in enumerate(plans):
            if 0 <= slot - i // 2 < len(plan):
                plan[slot - i // 2]()


def all_reduce(dims, grads, small):
    g_down, g_up, g_qkv, g_out = grads
    nz, ny, nx = dims
    parts = nz * ny * nx
    ff = g_down.shape[0] // 2
    half = ff // 2
    rows_d, rows_u, rows_o = half // parts, D // parts, D // 2 // parts
    cut = 640
    down = g_down.reshape(2, 2, nz, ny, nx, rows_d, D)
    up = g_up.reshape(nz, ny, nx, rows_u, 2 * ff)
    qkv = g_qkv.reshape(nz, ny, nx, rows_u, 3 * D)
    out = g_out.reshape(2, nz, ny, nx, rows_o, D)
    cols = lambda r, a, n: r.at[:, :, :, :, a : a + n]
    wide = 3 * D // 2
    views = [
        lambda r: [(r.at[0, 0], r.at[1, 0]), (r.at[0, 1], r.at[1, 1])],
        lambda r: [(cols(r, 0, half), cols(r, ff, half)), (cols(r, half, half), cols(r, ff + half, half))],
        lambda r: [(cols(r, 0, cut), cols(r, wide, cut)), (cols(r, cut, wide - cut), cols(r, wide + cut, wide - cut))],
        lambda r: [(r.at[0], r.at[1])],
        lambda r: [(r.at[0], r.at[1])],
    ]
    sizes = [(rows_d, D, BF16)] * 2 + [(rows_u, half, BF16)] * 2 + [(rows_u, cut, BF16), (rows_u, wide - cut, BF16), (rows_o, D, BF16)]
    sizes.append(small.shape[-2:] + (F32,))
    firsts = ["x", "y"] * 3 + ["y", "x"]
    scratch = []
    for (r, w, t), first in zip(sizes, firsts):
        scratch += buffers(dims, r, w, t, first)
    totals = pl.pallas_call(
        functools.partial(reduce_kernel, dims, views, firsts),
        in_specs=[pl.BlockSpec(memory_space=pl.ANY)] * 5,
        out_specs=[pl.BlockSpec(memory_space=pltpu.VMEM)] * len(sizes),
        out_shape=[jax.ShapeDtypeStruct((nz, ny, nx, r, w), t) for r, w, t in sizes],
        scratch_shapes=scratch,
        compiler_params=pltpu.CompilerParams(collective_id=0, has_side_effects=True, vmem_limit_bytes=60 * 2**20),
        name="all_reduce",
    )(down, up, qkv, out, small)
    flat = [t.reshape(-1, t.shape[-1]) for t in totals]
    return (
        jnp.concatenate(flat[:2], axis=0).astype(F32),
        jnp.concatenate(flat[2:4], axis=1).astype(F32),
        jnp.concatenate(flat[4:6], axis=1).astype(F32),
        flat[6].astype(F32),
        flat[7].reshape(-1),
    )


class Route:
    def __init__(self, dims, first, near, far, mine, pair, total, out, bufs, sems):
        self.dims, self.first, self.near, self.far = dims, first, near, far
        self.mine, self.pair, self.total, self.out = mine, pair, total, out
        self.land, self.land2, self.land3 = bufs
        self.sems = sems
        self.count = 0
        self.flight = []

    def launch(self, make):
        slot = self.count
        self.count += 1
        make(slot).start()
        self.flight.append(lambda: make(slot))

    def remote(self, src, dst, where):
        self.launch(
            lambda slot: pltpu.make_async_remote_copy(
                src_ref=src(), dst_ref=dst(), send_sem=self.sems.at[0, slot], recv_sem=self.sems.at[1, slot],
                device_id=where(), device_id_type=pl.DeviceIdType.MESH,
            )
        )

    def local(self, src, dst):
        self.launch(lambda slot: pltpu.make_async_copy(src(), dst(), self.sems.at[0, slot]))

    def settle(self):
        for make in self.flight:
            make().wait()
        self.flight = []

    def steps(self, place):
        z, y, x, side, index = place
        nz, ny, nx = self.dims
        plain = self.first == "x"
        one, two = (2, 1) if plain else (1, 2)
        own = (z, y, x)

        def peer(axis, shift):
            return lax.rem(own[axis] + shift, self.dims[axis])

        def device(axis, shift):
            at = list(own)
            at[axis] = peer(axis, shift)
            return ((at[0] * ny + at[1]) * nx + at[2], side)

        def row(ref, i):
            return ref[i, :, x] if plain else ref[i, y]

        def start():
            if self.near is not None:
                self.local(lambda: self.near(), lambda: self.mine())
            self.remote(lambda: self.far(), lambda: self.pair(), lambda: (index, 1 - side))

        def pair_add():
            self.settle()
            mine, pair = self.mine(), self.pair()

            def body(i, _):
                mine[i] = (mine[i].astype(F32) + pair[i].astype(F32)).astype(mine.dtype)
                return 0

            lax.fori_loop(0, nz, body, 0)
            for s in range(1, self.dims[one]):
                self.remote(
                    lambda s=s: self.mine().at[:, :, peer(one, s)] if plain else self.mine().at[:, peer(one, s)],
                    lambda s=s: self.land().at[s - 1],
                    lambda s=s: device(one, s),
                )

        def add_one():
            self.settle()
            mine, land = self.mine(), self.land()

            def body(i, _):
                v = row(mine, i).astype(F32)
                for s in range(1, self.dims[one]):
                    v = v + land[s - 1, i].astype(F32)
                if plain:
                    mine[i, :, x] = v.astype(mine.dtype)
                else:
                    mine[i, y] = v.astype(mine.dtype)
                return 0

            lax.fori_loop(0, nz, body, 0)
            for s in range(1, self.dims[two]):
                self.remote(
                    lambda s=s: self.mine().at[:, peer(two, s), x] if plain else self.mine().at[:, y, peer(two, s)],
                    lambda s=s: self.land2().at[s - 1],
                    lambda s=s: device(two, s),
                )

        def add_two():
            self.settle()
            mine, land = self.mine(), self.land2()

            def body(i, _):
                v = mine[i, y, x].astype(F32)
                for s in range(1, self.dims[two]):
                    v = v + land[s - 1, i].astype(F32)
                mine[i, y, x] = v.astype(mine.dtype)
                return 0

            lax.fori_loop(0, nz, body, 0)
            for s in range(1, nz):
                self.remote(
                    lambda s=s: self.mine().at[peer(0, s), y, x], lambda s=s: self.land3().at[s - 1], lambda s=s: device(0, s)
                )

        def spread(axis, view):
            for s in range(1, self.dims[axis]):
                self.remote(lambda: view(self.total()), lambda: view(self.total()), lambda s=s: device(axis, s))

        def add_three():
            self.settle()
            mine, land, total = self.mine(), self.land3(), self.total()
            v = mine[z, y, x].astype(F32)
            for s in range(1, nz):
                v = v + land[s - 1].astype(F32)
            total[z, y, x] = v.astype(total.dtype)
            spread(0, lambda t: t.at[z, y, x])

        def wide_two():
            self.settle()
            spread(two, lambda t: t.at[:, y, x])

        def wide_one():
            self.settle()
            spread(one, lambda t: t.at[:, :, x] if plain else t.at[:, y])

        def leave():
            self.settle()
            self.local(lambda: self.total(), lambda: self.out())

        return [start, pair_add, add_one, add_two, add_three, wide_two, wide_one, leave, self.settle]


def route_buffers(dims, rows, width, dtype, first):
    nz, ny, nx = dims
    na, nb = (nx, ny) if first == "x" else (ny, nx)
    tail = (rows, width)
    shapes = [(max(na - 1, 1), nz, nb) + tail, (max(nb - 1, 1), nz) + tail, (max(nz - 1, 1),) + tail]
    copies = 3 + 2 * (na + nb + nz - 3)
    return [pltpu.VMEM(s, dtype) for s in shapes] + [pltpu.SemaphoreType.DMA((2, copies))]


PAIRS = D // 128
BLOCK = 256


def tail_kernel(dims, table, late, schedule, count, *refs):
    (
        prefix_ref, q_ref, k_ref, v_ref, o_ref, g_ref, lse_ref, n1t_ref, w_ref, x_ref, gm_ref, gain_ref, svec_ref, swide_ref,
        down_ref, up_ref, outw_ref, ig_ref, odown_ref, oup_ref, oqkv_ref, oout_ref, osmall_ref,
        gproj, gqkv, bias, sums, small,
        mdown, mup, mout, pdown, pup, pout, pqkv, psmall, tdown, tup, tqkv, tout, tsmall,
    ) = refs[:41]
    scratch = refs[41:]
    pid = pl.program_id(0)
    index, side = lax.axis_index("dp"), lax.axis_index("tensor")
    nz, ny, nx = dims
    place = (index // (ny * nx), lax.rem(index // nx, ny), lax.rem(index, nx), side, index)
    half = D // 2

    @pl.when(pid == 0)
    def _():
        barrier = pltpu.get_barrier_semaphore()
        peers = [(index, 1 - side)]
        for axis in range(3):
            for s in range(1, dims[axis]):
                at = list(place[:3])
                at[axis] = lax.rem(at[axis] + s, dims[axis])
                peers.append(((at[0] * ny + at[1]) * nx + at[2], side))
        for peer in peers:
            pl.semaphore_signal(barrier, inc=1, device_id=peer, device_id_type=pl.DeviceIdType.MESH)
        pl.semaphore_wait(barrier, len(peers))
        sums[...] = jnp.zeros_like(sums)

    homes = {
        "down": (down_ref, mdown, pdown, tdown, odown_ref),
        "up": (up_ref, mup, pup, tup, oup_ref),
        "qkv": (gqkv, gqkv, pqkv, tqkv, oqkv_ref),
        "out": (outw_ref, mout, pout, tout, oout_ref),
        "small": (small, small, psmall, tsmall, osmall_ref),
    }
    plans = []
    for n, (name, lead, near, width, first) in enumerate(table):
        src, mine, pair, total, out = homes[name]
        bufs = scratch[4 * n : 4 * n + 4]
        cols = lambda r, a, width=width: r.at[:, :, :, :, a : a + width]
        if name == "down":
            views = dict(
                near=lambda s=src, l=lead, c=cols, a=near: c(s.at[0, l], a), far=lambda s=src, l=lead, c=cols, a=near: c(s.at[1, l], a),
                mine=lambda s=mine, l=lead, c=cols, a=near: c(s.at[l], a), pair=lambda s=pair, l=lead, c=cols, a=near: c(s.at[l], a),
                total=lambda s=total, l=lead, c=cols, a=near: c(s.at[l], a), out=lambda s=out, l=lead, c=cols, a=near: c(s.at[l], a),
            )
        elif name in ("up", "qkv"):
            size = lead
            views = dict(
                near=None if name == "qkv" else (lambda s=src, c=cols, a=near: c(s, a)),
                far=lambda s=src, c=cols, a=near, n=size: c(s, a + n), mine=lambda s=mine, c=cols, a=near: c(s, a),
                pair=lambda s=pair, c=cols, a=near: c(s, a), total=lambda s=total, c=cols, a=near: c(s, a),
                out=lambda s=out, c=cols, a=near: c(s, a),
            )
        else:
            views = dict(
                near=None if name == "small" else (lambda s=src: s.at[0]), far=lambda s=src: s.at[1],
                mine=(lambda s=mine: s.at[0]) if name == "small" else (lambda s=mine: s),
                pair=lambda s=pair: s, total=lambda s=total: s, out=lambda s=out: s,
            )
        bufs = [(lambda b=b: b) for b in bufs[:3]] + [bufs[3]]
        plans.append(Route(dims, first, bufs=bufs[:3], sems=bufs[3], **views).steps(place))

    def advance(step):
        for n, k in schedule.get(step, ()):
            plans[n][k]()

    for step in range(count):
        if schedule.get(step):
            pl.when(pid == step)(functools.partial(advance, step))

    @pl.when(pid < PAIRS)
    def _():
        column = lambda c: gproj.at[:, pl.ds(pl.multiple_of(head_block(pid, c) * 128, 128), 128)]
        attn_bwd_kernel(
            prefix_ref, q_ref, k_ref, v_ref, o_ref, g_ref, lse_ref, column(0), column(1), column(2),
            bias.at[:, pl.ds(pl.multiple_of(pid * 128, 128), 128)],
        )

    @pl.when(pid == PAIRS)
    def _():
        def body(c, _):
            at = pl.ds(pl.multiple_of(c * D, 128), D)
            part = nn(n1t_ref[...], gproj[:, at]).astype(BF16)
            gqkv[:, :, :, :, at] = part.reshape(gqkv.shape[:4] + (D,))
            return 0

        lax.fori_loop(0, 3, body, 0)

    @pl.when(pid > PAIRS)
    def _():
        rows = pl.ds(pl.multiple_of((pid - PAIRS - 1) * BLOCK, BLOCK), BLOCK)
        e = nt(gproj[rows, :], w_ref[...])
        xhat, inv = normed(x_ref[...].astype(F32))
        sums[0] += colsum(e * xhat)
        sums[1] += colsum(e)
        ig_ref[...] = gm_ref[...] + normed_back(e * gain_ref[...], xhat, inv)

    @pl.when(pid == count - 1)
    def _():
        small[...] = jnp.zeros_like(small)
        split = [bias[i : i + 1, :] for i in range(2)]
        split += [jnp.sum(svec_ref[i], axis=0, keepdims=True) for i in range(2)]
        split += [jnp.sum(swide_ref[i], axis=0, keepdims=True) for i in range(3)]
        shared = [jnp.sum(sums[i], axis=0, keepdims=True) for i in range(2)]
        shared += [jnp.sum(svec_ref[i], axis=0, keepdims=True) for i in range(2, 6)]
        for s in range(2):
            at = 0
            for v in [v[:, s * (v.shape[1] // 2) : (s + 1) * (v.shape[1] // 2)] for v in split] + shared:
                for c in range(v.shape[1] // 128):
                    p = at // 8
                    small[s, p // (ny * nx), p // nx % ny, p % nx, at % 8 : at % 8 + 1, :] = v[:, c * 128 : (c + 1) * 128]
                    at += 1
        for n, k in late:
            plans[n][k]()


def tail_stage(dims, prefix, qkv, attended, ga, lse, n1t, wqkv, tokens, gm, pre_gain, svec, swide, g_down, g_up, g_out):
    nz, ny, nx = dims
    parts = nz * ny * nx
    length = qkv.shape[0]
    ff = g_down.shape[0] // 2
    half = ff // 2
    rows = D // parts
    wide = 3 * D // 2
    small_rows = 8
    down = g_down.reshape(2, 2, nz, ny, nx, rows, D)
    up = g_up.reshape(nz, ny, nx, rows, 2 * ff)
    out = g_out.reshape(2, nz, ny, nx, rows // 2, D)
    table = []
    for a in (0, D // 2):
        table += [("down", 0, a, D // 2, "x"), ("down", 1, a, D // 2, "y")]
    for a in (0, half // 2):
        table += [("up", ff, a, half // 2, "x"), ("up", ff, half + a, half // 2, "y")]
    table += [("out", 0, 0, D, "y")]
    table += [("qkv", wide, 0, 384, "x"), ("qkv", wide, 640, 256, "y"), ("qkv", wide, 384, 256, "x"), ("qkv", wide, 896, 256, "y")]
    table += [("small", 0, 0, 128, "x")]
    groups = [(0, 1), (2, 3), (4, 5), (6, 7), (8,), (9, 10), (11, 12), (13,)]
    enter = [0, 1, 2, 3, 4, 5, 6, 7]
    count = PAIRS + 1 + length // BLOCK
    at_step = [0, 0, 1, 3, 5, 7, 7, 10]
    schedule, late = {}, []
    depth = 9
    for slot in range(enter[-1] + depth):
        for g, members in enumerate(groups):
            k = slot - enter[g]
            if not 0 <= k < depth:
                continue
            for n in members:
                if slot < len(at_step) - 1:
                    schedule.setdefault(at_step[slot], []).append((n, k))
                else:
                    late.append((n, k))
    sds = jax.ShapeDtypeStruct
    scratch = [
        pltpu.VMEM((length, 3 * D), BF16), pltpu.VMEM((nz, ny, nx, rows, 3 * D), BF16), pltpu.VMEM((8, D), F32),
        pltpu.VMEM((2, 8, D), F32), pltpu.VMEM((2, nz, ny, nx, small_rows, 128), F32),
    ]
    shapes = {
        "down": (2, nz, ny, nx, rows, D), "up": (nz, ny, nx, rows, ff), "out": (nz, ny, nx, rows // 2, D),
        "qkv": (nz, ny, nx, rows, wide), "small": (nz, ny, nx, small_rows, 128),
    }
    kinds = {n: F32 if n == "small" else BF16 for n in shapes}
    scratch += [pltpu.VMEM(shapes[n], kinds[n]) for n in ("down", "up", "out")]
    scratch += [pltpu.VMEM(shapes[n], kinds[n]) for n in ("down", "up", "out", "qkv", "small")]
    scratch += [pltpu.VMEM(shapes[n], kinds[n]) for n in ("down", "up", "qkv", "out", "small")]
    heights = {"down": rows, "up": rows, "qkv": rows, "out": rows // 2, "small": small_rows}
    for name, _, _, width, first in table:
        scratch += route_buffers(dims, heights[name], width, kinds[name], first)
    pair_at = lambda i: jnp.minimum(i, PAIRS - 1)
    block_at = lambda i: jnp.maximum(i - PAIRS - 1, 0)
    col = lambda c: pl.BlockSpec((length, 128), lambda i, c=c: (0, head_block(pair_at(i), c)))
    one = pl.BlockSpec((length, 128), lambda i: (0, pair_at(i)))
    block = pl.BlockSpec((BLOCK, D), lambda i: (block_at(i), 0))
    whole = lambda v: pl.BlockSpec(v.shape, lambda i, n=v.ndim: (0,) * n, pipeline_mode=pl.Buffered(1))
    hbm = pl.BlockSpec(memory_space=pl.ANY)
    gain = pre_gain.reshape(1, D)
    order = ("down", "up", "qkv", "out", "small")
    results = pl.pallas_call(
        functools.partial(tail_kernel, dims, table, late, schedule, count),
        grid=(count,),
        in_specs=[
            pl.BlockSpec(memory_space=pltpu.SMEM), col(0), col(1), col(2), one, one,
            pl.BlockSpec((1, 8, length), lambda i: (pair_at(i), 0, 0)), whole(n1t), whole(wqkv), block, block, whole(gain),
            whole(svec), whole(swide), hbm, hbm, hbm,
        ],
        out_specs=[block] + [hbm] * 5,
        out_shape=[sds((length, D), F32)] + [sds(shapes[n], kinds[n]) for n in order],
        scratch_shapes=scratch,
        compiler_params=pltpu.CompilerParams(collective_id=1, has_side_effects=True, vmem_limit_bytes=63 * 2**20),
        name="tail_stage",
    )(prefix, qkv, qkv, qkv, attended, ga, lse, n1t, wqkv, tokens, gm, gain, svec, swide, down, up, out)
    input_grad, t_down, t_up, t_qkv, t_out, t_small = results
    return (
        input_grad, t_down.reshape(ff, D).astype(F32), t_up.reshape(D, ff).astype(F32), t_qkv.reshape(D, wide).astype(F32),
        t_out.reshape(D // 2, D).astype(F32), t_small.reshape(-1),
    )


def pack_small(dims, g_qv, g_vec, g_wide, g_pre):
    half, ff_half = D // 2, g_wide.shape[1] // 2
    shared = jnp.concatenate([g_pre.reshape(-1), g_vec[2:].reshape(-1)])
    rows = -(-(4 * half + 3 * ff_half + 6 * D) // (128 * 8 * math.prod(dims))) * 8
    pad = jnp.zeros((rows * 128 * math.prod(dims) - (4 * half + 3 * ff_half + 6 * D),), F32)
    pack = lambda i: jnp.concatenate(
        [v[j, i * n : (i + 1) * n] for v, m, n in ((g_qv, 2, half), (g_vec, 2, half), (g_wide, 3, ff_half)) for j in range(m)] + [shared, pad]
    )
    return jnp.stack([pack(0), pack(1)]).reshape((2,) + dims + (rows, 128))


def swap(value):
    return lax.ppermute(value, "tensor", ((0, 1), (1, 0)))


def body(
    dims, tokens, grad_out, prefix, pre_gain, pre_bias, qkv_weight, qv_bias, sub_gain, sub_bias, out_weight, out_bias,
    ffn_gain, ffn_bias, up_weight, up_bias, inner_gain, inner_bias, down_weight, down_bias,
):
    side = lax.axis_index("tensor")
    local = lax.dynamic_slice_in_dim(prefix, side, 1)
    both = lambda v, axis: jnp.concatenate([v, swap(v)], axis=axis)
    half, ff_half = D // 2, up_bias.shape[0]
    wqkv = both(qkv_weight.reshape(D, 3 * half), 1)
    wo = both(out_weight, 0)
    wu = both(up_weight, 1)
    wd = both(down_weight, 0)
    near = jnp.concatenate([qv_bias.reshape(-1), sub_gain, sub_bias, up_bias, inner_gain, inner_bias])
    far = swap(near)
    cut = lambda start, size: jnp.concatenate([near[start : start + size], far[start : start + size]])
    zero = jnp.zeros((half,), F32)
    bias = jnp.concatenate([p for v in (near, far) for p in (v[:half], zero, v[half : 2 * half])])
    sgain, sbias = [cut(i * half, half) for i in (2, 3)]
    ub, ig, ib = [cut(4 * half + i * ff_half, ff_half) for i in range(3)]
    vecs = jnp.stack([sgain, sbias, out_bias, ffn_gain, ffn_bias, down_bias])
    wides = jnp.stack([ub, ig, ib])
    n1, qkv, attended, lse, out, gm, ga, svec, swide, g_down, g_up, g_out = front(
        tokens, grad_out, local, pre_gain, pre_bias, wqkv, bias, vecs, wides, wo, wu, wd
    )
    if D // 2 % (16 * math.prod(dims) // 2) == 0 and D // math.prod(dims) % 16 == 0:
        input_grad, g_down, g_up, g_qkv, g_out, small = tail_stage(
            dims, local, qkv, attended, ga, lse, n1.T, wqkv, tokens, gm, pre_gain, svec, swide, g_down, g_up, g_out
        )
    else:
        input_grad, g_pre, g_qkv, g_qv = back(local, tokens, pre_gain, wqkv, n1, qkv, attended, lse, gm, ga)
        small = pack_small(dims, g_qv, jnp.sum(svec, 1), jnp.sum(swide, 1), g_pre)
        g_down, g_up, g_qkv, g_out, small = all_reduce(dims, (g_down, g_up, g_qkv, g_out), small)
    r = lambda i: small[i * half : (i + 1) * half]
    w = lambda i: small[4 * half + i * ff_half : 4 * half + (i + 1) * ff_half]
    base = 4 * half + 3 * ff_half
    f = lambda i: small[base + i * D : base + (i + 1) * D]
    return (
        out, input_grad, f(0), f(1), g_qkv.reshape(D, 3, half), small[: 2 * half].reshape(2, half), r(2), r(3), g_out,
        f(2), f(3), f(4), g_up, w(0), w(1), w(2), g_down, f(5),
    )


def solution(mesh):
    rows = P(("dp", "tensor"), None)
    wide, tall, vec, whole = P(None, "tensor"), P("tensor", None), P("tensor"), P()
    cube = P(None, None, "tensor")
    return jax.shard_map(
        functools.partial(body, grid_of(mesh.shape["dp"])),
        mesh=mesh,
        in_specs=(
            rows, rows, P("dp"), whole, whole, cube, wide, vec, vec, tall, whole, whole, whole, wide, vec, vec, vec, tall, whole,
        ),
        out_specs=(
            rows, rows, whole, whole, cube, wide, vec, vec, tall, whole, whole, whole, wide, vec, vec, vec, tall, whole,
        ),
        check_vma=False,
    )
```

```python
import functools
import math

import jax
import jax.numpy as jnp
from jax import lax
from jax.sharding import PartitionSpec as P
from jax.experimental import pallas as pl
from jax.experimental.pallas import tpu as pltpu

D = 768
HEAD_DIM = 64
PREFIX_MAX = 512
EPS = 1e-05
F32 = jnp.float32
BF16 = jnp.bfloat16
QB = 512


def nn(a, b):
    return lax.dot_general(a, b, (((1,), (0,)), ((), ())), preferred_element_type=F32)


def nt(a, b):
    return lax.dot_general(a, b, (((1,), (1,)), ((), ())), preferred_element_type=F32)


def tn(a, b):
    return lax.dot_general(a, b, (((0,), (0,)), ((), ())), preferred_element_type=F32)


def halves(v):
    left = lax.broadcasted_iota(jnp.int32, v.shape, 1) < HEAD_DIM
    zero = jnp.zeros_like(v)
    return jnp.where(left, v, zero), jnp.where(left, zero, v)


def spans(start, length, block):
    last = min(length, max(start + block, PREFIX_MAX))
    out = []
    if start:
        out.append((0, start, False))
    out.append((start, last, True))
    return out


def masked(scores, key_start, query_start, prefix):
    key_pos = key_start + lax.broadcasted_iota(jnp.int32, scores.shape, 0)
    query_pos = query_start + lax.broadcasted_iota(jnp.int32, scores.shape, 1)
    seen = key_pos <= query_pos
    if key_start < PREFIX_MAX:
        seen = seen | (key_pos < prefix)
    return jnp.where(seen, scores, -1e30)


def head_block(i, c):
    each = D // 256
    return i // each * 3 * each + c * each + lax.rem(i, each)


def attn_fwd_kernel(prefix_ref, q_ref, k_ref, v_ref, o_ref, lse_ref):
    length = q_ref.shape[0]
    prefix = prefix_ref[0]
    keys = halves(k_ref[...])
    value_t = v_ref[...].T
    for start in range(0, length, QB):
        query = q_ref[start : start + QB, :] * jnp.asarray(HEAD_DIM**-0.5, BF16)
        parts = []
        for head in range(2):
            scores = []
            for first, last, mask in spans(start, length, QB):
                s = nt(keys[head][first:last], query)
                scores.append(masked(s, first, start, prefix) if mask else s)
            peak = functools.reduce(jnp.maximum, [jnp.max(s, axis=0, keepdims=True) for s in scores])
            total = jnp.zeros_like(peak)
            mixed = jnp.zeros((HEAD_DIM, QB), F32)
            rows = slice(head * HEAD_DIM, (head + 1) * HEAD_DIM)
            for s, (first, last, _) in zip(scores, spans(start, length, QB)):
                w = jnp.exp(s - peak)
                total = total + jnp.sum(w, axis=0, keepdims=True)
                mixed = mixed + nn(value_t[rows, first:last], w.astype(BF16))
            parts.append(mixed / total)
            lse_ref[0, head : head + 1, start : start + QB] = peak + jnp.log(total)
        o_ref[start : start + QB, :] = jnp.concatenate(parts, axis=0).T


def attn_fwd(prefix, qkv):
    length = qkv.shape[0]
    pairs = D // 128
    col = lambda c: pl.BlockSpec((length, 128), lambda i, c=c: (0, head_block(i, c)))
    return pl.pallas_call(
        attn_fwd_kernel,
        grid=(pairs,),
        in_specs=[pl.BlockSpec(memory_space=pltpu.SMEM), col(0), col(1), col(2)],
        out_specs=[
            pl.BlockSpec((length, 128), lambda i: (0, i)),
            pl.BlockSpec((1, 8, length), lambda i: (i, 0, 0)),
        ],
        out_shape=[
            jax.ShapeDtypeStruct((length, D), F32),
            jax.ShapeDtypeStruct((pairs, 8, length), F32),
        ],
        name="attn_fwd",
    )(prefix, qkv, qkv, qkv)


def attn_bwd_kernel(prefix_ref, q_ref, k_ref, v_ref, o_ref, g_ref, lse_ref, dq_ref, dk_ref, dv_ref, bias_ref):
    length = q_ref.shape[0]
    prefix = prefix_ref[0]
    scale = HEAD_DIM**-0.5
    keys = halves(k_ref[...])
    values = halves(v_ref[...])
    key_t = k_ref[...].T
    delta_t = (o_ref[...] * g_ref[...].astype(F32)).T
    dk = [jnp.zeros((b - a, 128), F32) for a, b in zip(range(0, length, QB), range(QB, length + 1, QB))]
    dv = list(dk)
    qsum = jnp.zeros((8, 128), F32)
    for start in range(0, length, QB):
        cols = slice(start, start + QB)
        query = q_ref[cols, :] * jnp.asarray(scale, BF16)
        query_half = halves(query)
        grad = g_ref[cols, :]
        grad_half = halves(grad)
        parts = []
        for head in range(2):
            rows = slice(head * HEAD_DIM, (head + 1) * HEAD_DIM)
            lse = lse_ref[0, head : head + 1, cols]
            delta = jnp.sum(delta_t[rows, cols], axis=0, keepdims=True)
            dq = jnp.zeros((HEAD_DIM, QB), F32)
            for first in range(0, length, QB):
                live = [s for s in spans(start, length, QB) if s[0] <= first < s[1]]
                if not live:
                    continue
                last = first + QB
                s = nt(keys[head][first:last], query)
                if live[0][2]:
                    s = masked(s, first, start, prefix)
                w = jnp.exp(s - lse)
                dp = nt(values[head][first:last], grad)
                ds = (w * (dp - delta)).astype(BF16)
                b = first // QB
                dv[b] = dv[b] + nn(w.astype(BF16), grad_half[head])
                dk[b] = dk[b] + nn(ds, query_half[head])
                dq = dq + nn(key_t[rows, first:last], ds)
            parts.append(dq)
        dq = jnp.concatenate(parts, axis=0).T * scale
        qsum = qsum + jnp.sum(dq.reshape(QB // 8, 8, 128), axis=0)
        dq_ref[cols, :] = dq.astype(BF16)
    vsum = jnp.zeros((8, 128), F32)
    for b in range(length // QB):
        cols = slice(b * QB, (b + 1) * QB)
        dk_ref[cols, :] = dk[b].astype(BF16)
        dv_ref[cols, :] = dv[b].astype(BF16)
        vsum = vsum + jnp.sum(dv[b].reshape(QB // 8, 8, 128), axis=0)
    bias_ref[0:1, :] = jnp.sum(qsum, axis=0, keepdims=True)
    bias_ref[1:2, :] = jnp.sum(vsum, axis=0, keepdims=True)


def attn_bwd(prefix, qkv, attended, grad_attended, lse):
    length = qkv.shape[0]
    pairs = D // 128
    col = lambda c: pl.BlockSpec((length, 128), lambda i, c=c: (0, head_block(i, c)))
    one = pl.BlockSpec((length, 128), lambda i: (0, i))
    return pl.pallas_call(
        attn_bwd_kernel,
        grid=(pairs,),
        in_specs=[
            pl.BlockSpec(memory_space=pltpu.SMEM), col(0), col(1), col(2), one, one,
            pl.BlockSpec((1, 8, length), lambda i: (i, 0, 0)),
        ],
        out_specs=[one, one, one, pl.BlockSpec((8, 128), lambda i: (0, i))],
        out_shape=[jax.ShapeDtypeStruct((length, D), BF16)] * 3 + [jax.ShapeDtypeStruct((8, D), F32)],
        name="attn_bwd",
    )(prefix, qkv, qkv, qkv, attended, grad_attended, lse)


def normed(v):
    centre = v - jnp.mean(v, axis=-1, keepdims=True)
    inv = lax.rsqrt(jnp.mean(centre * centre, axis=-1, keepdims=True) + EPS)
    return centre * inv, inv


def normed_back(e, xhat, inv):
    return inv * (e - jnp.mean(e, axis=-1, keepdims=True) - xhat * jnp.mean(e * xhat, axis=-1, keepdims=True))


def colsum(v):
    rows, cols = v.shape
    return jnp.sum(v.reshape(rows // 8, 8, cols), axis=0)


def mid_kernel(
    x_ref, att_ref, g_ref, vec_ref, wide_ref, near_wo, far_wo, near_wu, far_wu, near_wd, far_wd,
    out_ref, n2_ref, n3_ref, n4_ref, gh_ref, gm_ref, gml_ref, ga_ref, svec_ref, swide_ref,
    act_ref, slope_ref, wo_ref, wu_ref, wd_ref, sem,
):
    first = pl.program_id(0) == 0
    half, ff_half = near_wo.shape[0], near_wu.shape[1]
    moves = (
        (near_wo, wo_ref.at[:half]), (far_wo, wo_ref.at[half:]), (near_wu, wu_ref.at[:, :ff_half]), (far_wu, wu_ref.at[:, ff_half:]),
        (near_wd, wd_ref.at[:ff_half]), (far_wd, wd_ref.at[ff_half:]),
    )
    moves = [pltpu.make_async_copy(a, b, sem.at[i]) for i, (a, b) in enumerate(moves)]

    def arrive(some):
        @pl.when(first)
        def _():
            for copy in some:
                copy.wait()

    @pl.when(first)
    def _():
        for copy in moves:
            copy.start()
        svec_ref[...] = jnp.zeros_like(svec_ref)
        swide_ref[...] = jnp.zeros_like(swide_ref)

    sub_gain, sub_bias, out_bias, ffn_gain, ffn_bias, down_bias = [vec_ref[i : i + 1, :] for i in range(6)]
    up_bias, inner_gain, inner_bias = [wide_ref[i : i + 1, :] for i in range(3)]
    xhat2, inv2 = normed(att_ref[...])
    n2 = (xhat2 * sub_gain + sub_bias).astype(BF16)
    n2_ref[...] = n2
    arrive(moves[:2])
    middle = x_ref[...].astype(F32) + nn(n2, wo_ref[...]) + out_bias
    xhat3, inv3 = normed(middle)
    n3 = (xhat3 * ffn_gain + ffn_bias).astype(BF16)
    n3_ref[...] = n3
    arrive(moves[2:4])
    hidden = nn(n3, wu_ref[...]) + up_bias
    half = 0.5 + 0.5 * lax.erf(hidden * (2.0**-0.5))
    act_ref[...] = hidden * half
    slope_ref[...] = half + hidden * (jnp.exp(-0.5 * hidden * hidden) * 0.3989422804014327)
    xhat4, inv4 = normed(act_ref[...])
    n4 = (xhat4 * inner_gain + inner_bias).astype(BF16)
    n4_ref[...] = n4
    act_ref[...] = xhat4
    arrive(moves[4:])
    out_ref[...] = (middle + nn(n4, wd_ref[...]) + down_bias).astype(BF16)
    g = g_ref[...]
    e = nt(g, wd_ref[...])
    xhat4 = act_ref[...]
    swide_ref[1] += colsum(e * xhat4)
    swide_ref[2] += colsum(e)
    gh = normed_back(e * inner_gain, xhat4, inv4) * slope_ref[...]
    swide_ref[0] += colsum(gh)
    ghl = gh.astype(BF16)
    gh_ref[...] = ghl
    gf = g.astype(F32)
    e = nt(ghl, wu_ref[...])
    svec_ref[3] += colsum(e * xhat3)
    svec_ref[4] += colsum(e)
    gm = gf + normed_back(e * ffn_gain, xhat3, inv3)
    svec_ref[2] += colsum(gm)
    svec_ref[5] += colsum(gf)
    gm_ref[...] = gm
    gml = gm.astype(BF16)
    gml_ref[...] = gml
    e = nt(gml, wo_ref[...])
    svec_ref[0] += colsum(e * xhat2)
    svec_ref[1] += colsum(e)
    ga_ref[...] = normed_back(e * sub_gain, xhat2, inv2).astype(BF16)


def middle_stage(x, att, g, vecs, wides, wo, wu, wd, block=256):
    rows = x.shape[0]
    ff = 2 * wu[0].shape[1]
    row = lambda n: pl.BlockSpec((block, n), lambda i: (i, 0))
    whole = lambda s: pl.BlockSpec(s, lambda i: (0,) * len(s), pipeline_mode=pl.Buffered(1))
    sds = jax.ShapeDtypeStruct
    return pl.pallas_call(
        mid_kernel,
        grid=(rows // block,),
        in_specs=[row(D), row(D), row(D), whole(vecs.shape), whole(wides.shape)] + [pl.BlockSpec(memory_space=pl.ANY)] * 6,
        out_specs=[row(D), row(D), row(D), row(ff), row(ff), row(D), row(D), row(D), whole((6, 8, D)), whole((3, 8, ff))],
        out_shape=[
            sds((rows, D), BF16), sds((rows, D), BF16), sds((rows, D), BF16), sds((rows, ff), BF16), sds((rows, ff), BF16),
            sds((rows, D), F32), sds((rows, D), BF16), sds((rows, D), BF16), sds((6, 8, D), F32), sds((3, 8, ff), F32),
        ],
        scratch_shapes=[pltpu.VMEM((block, ff), F32), pltpu.VMEM((block, ff), F32), pltpu.VMEM((D, D), BF16), pltpu.VMEM((D, ff), BF16), pltpu.VMEM((ff, D), BF16), pltpu.SemaphoreType.DMA((6,))],
        compiler_params=pltpu.CompilerParams(vmem_limit_bytes=62 * 2**20),
        name="middle_stage",
    )(x, att, g, vecs, wides, *wo, *wu, *wd)


def front(tokens, grad_out, prefix, qkv, vecs, wides, wo, wu, wd):
    attended, lse = attn_fwd(prefix, qkv)
    out, n2, n3, n4, gh, gm, gml, ga, svec, swide = middle_stage(tokens, attended, grad_out, vecs, wides, wo, wu, wd)
    g_down = tn(n4, grad_out).astype(BF16)
    g_up = tn(n3, gh).astype(BF16)
    g_out = tn(n2, gml).astype(BF16)
    return attended, lse, out, gm, ga, svec, swide, g_down, g_up, g_out


def back(prefix, tokens, pre_gain, wqkv, n1, qkv, attended, lse, gm, ga):
    xhat1, inv1 = normed(tokens.astype(F32))
    dq, dk, dv, dbias = attn_bwd(prefix, qkv, attended, ga, lse)
    h = D // 2
    gproj = jnp.concatenate([v[:, s] for s in (slice(0, h), slice(h, D)) for v in (dq, dk, dv)], axis=1)
    g_qkv = tn(n1, gproj).astype(BF16)
    e = nt(gproj, wqkv)
    g_pre = jnp.stack([jnp.sum(e * xhat1, axis=0), jnp.sum(e, axis=0)])
    input_grad = gm + normed_back(e * pre_gain, xhat1, inv1)
    return input_grad, g_pre, g_qkv, dbias


def grid_of(count):
    side = 1
    while 2 * side**3 < count:
        side += 1
    return (2 * side, side, side) if 2 * side**3 == count else (count, 1, 1)


class Piece:
    def __init__(self, dims, first, near, far, total, bufs, sems, place):
        self.dims, self.first, self.near, self.far, self.total = dims, first, near, far, total
        self.mine, self.pair, self.land, self.part, self.land2, self.part2, self.land3 = bufs
        self.sems, self.place = sems, place
        self.count = 0
        self.flight = []

    def send(self, src, dst, where):
        copy = pltpu.make_async_remote_copy(
            src_ref=src, dst_ref=dst, send_sem=self.sems.at[0, self.count], recv_sem=self.sems.at[1, self.count],
            device_id=where, device_id_type=pl.DeviceIdType.MESH,
        )
        self.count += 1
        copy.start()
        self.flight.append(copy)

    def settle(self):
        for copy in self.flight:
            copy.wait()
        self.flight = []

    def device(self, axis, shift):
        at = list(self.place[:3])
        at[axis] = lax.rem(at[axis] + shift, self.dims[axis])
        nz, ny, nx = self.dims
        return at[axis], ((at[0] * ny + at[1]) * nx + at[2], self.place[3])

    def steps(self):
        z, y, x = self.place[:3]
        nz, ny, nx = self.dims
        one, two = (2, 1) if self.first == "x" else (1, 2)
        pick1 = lambda ref, p: ref.at[:, :, p] if one == 2 else ref.at[:, p]
        own1, own2 = (x, y) if one == 2 else (y, x)

        def start():
            local = pltpu.make_async_copy(self.near, self.mine, self.sems.at[0, self.count])
            self.count += 1
            local.start()
            self.send(self.far, self.pair, (self.place[4], 1 - self.place[3]))
            self.flight.append(local)

        def pair_add():
            self.settle()
            def one_row(i, _):
                self.mine[i] = (self.mine[i].astype(F32) + self.pair[i].astype(F32)).astype(self.mine.dtype)
                return 0
            lax.fori_loop(0, nz, one_row, 0)
            for s in range(1, self.dims[one]):
                p, dev = self.device(one, s)
                self.send(pick1(self.mine, p), self.land.at[s - 1], dev)

        def add_one():
            self.settle()
            def one_row(i, _):
                v = (self.mine[i, :, x] if one == 2 else self.mine[i, y]).astype(F32)
                for s in range(1, self.dims[one]):
                    v = v + self.land[s - 1, i].astype(F32)
                self.part[i] = v.astype(self.part.dtype)
                return 0
            lax.fori_loop(0, nz, one_row, 0)
            for s in range(1, self.dims[two]):
                p, dev = self.device(two, s)
                self.send(self.part.at[:, p], self.land2.at[s - 1], dev)

        def add_two():
            self.settle()
            def one_row(i, _):
                v = self.part[i, own2].astype(F32)
                for s in range(1, self.dims[two]):
                    v = v + self.land2[s - 1, i].astype(F32)
                self.part2[i] = v.astype(self.part2.dtype)
                return 0
            lax.fori_loop(0, nz, one_row, 0)
            for s in range(1, nz):
                p, dev = self.device(0, s)
                self.send(self.part2.at[p], self.land3.at[s - 1], dev)

        def add_three():
            self.settle()
            v = self.part2[z].astype(F32)
            for s in range(1, nz):
                v = v + self.land3[s - 1].astype(F32)
            self.total[z, y, x] = v.astype(self.total.dtype)
            spread(0, self.total.at[z, y, x])

        def spread(axis, ref):
            for s in range(1, self.dims[axis]):
                self.send(ref, ref, self.device(axis, s)[1])

        def wide_two():
            self.settle()
            spread(two, self.total.at[:, y, x])

        def wide_one():
            self.settle()
            spread(one, self.total.at[:, :, x] if one == 2 else self.total.at[:, y])

        return [start, pair_add, add_one, add_two, add_three, wide_two, wide_one, self.settle]


def buffers(dims, rows, width, dtype, first):
    nz, ny, nx = dims
    na, nb = (nx, ny) if first == "x" else (ny, nx)
    tail = (rows, width)
    shapes = [
        (nz, ny, nx) + tail, (nz, ny, nx) + tail, (max(na - 1, 1), nz, nb) + tail, (nz, nb) + tail,
        (max(nb - 1, 1), nz) + tail, (nz,) + tail, (max(nz - 1, 1),) + tail,
    ]
    copies = 2 + 2 * (na + nb + nz - 3)
    return [pltpu.VMEM(s, dtype) for s in shapes] + [pltpu.SemaphoreType.DMA((2, copies))]


def reduce_kernel(dims, views, firsts, *refs):
    count = len(firsts)
    sources = refs[: len(views)]
    totals = refs[len(views) : len(views) + count]
    scratch = refs[len(views) + count :]
    index, side = lax.axis_index("dp"), lax.axis_index("tensor")
    nz, ny, nx = dims
    place = (index // (ny * nx), lax.rem(index // nx, ny), lax.rem(index, nx), side, index)
    barrier = pltpu.get_barrier_semaphore()
    peers = [(index, 1 - side)]
    probe = Piece(dims, "x", None, None, None, [None] * 7, None, place)
    for axis in range(3):
        for s in range(1, dims[axis]):
            peers.append(probe.device(axis, s)[1])
    for peer in peers:
        pl.semaphore_signal(barrier, inc=1, device_id=peer, device_id_type=pl.DeviceIdType.MESH)
    pl.semaphore_wait(barrier, len(peers))
    plans = []
    at = 0
    for source, view in zip(sources, views):
        for near, far in view(source):
            plans.append(Piece(dims, firsts[at], near, far, totals[at], scratch[8 * at : 8 * at + 7], scratch[8 * at + 7], place).steps())
            at += 1
    slots = len(plans[0]) + (count + 1) // 2 - 1
    for slot in range(slots):
        for i, plan in enumerate(plans):
            if 0 <= slot - i // 2 < len(plan):
                plan[slot - i // 2]()


def all_reduce(dims, grads, small):
    g_down, g_up, g_qkv, g_out = grads
    nz, ny, nx = dims
    parts = nz * ny * nx
    ff = g_down.shape[0] // 2
    half = ff // 2
    rows_d, rows_u, rows_o = half // parts, D // parts, D // 2 // parts
    cut = 640
    down = g_down.reshape(2, 2, nz, ny, nx, rows_d, D)
    up = g_up.reshape(nz, ny, nx, rows_u, 2 * ff)
    qkv = g_qkv.reshape(nz, ny, nx, rows_u, 3 * D)
    out = g_out.reshape(2, nz, ny, nx, rows_o, D)
    cols = lambda r, a, n: r.at[:, :, :, :, a : a + n]
    wide = 3 * D // 2
    views = [
        lambda r: [(r.at[0, 0], r.at[1, 0]), (r.at[0, 1], r.at[1, 1])],
        lambda r: [(cols(r, 0, half), cols(r, ff, half)), (cols(r, half, half), cols(r, ff + half, half))],
        lambda r: [(cols(r, 0, cut), cols(r, wide, cut)), (cols(r, cut, wide - cut), cols(r, wide + cut, wide - cut))],
        lambda r: [(r.at[0], r.at[1])],
        lambda r: [(r.at[0], r.at[1])],
    ]
    sizes = [(rows_d, D, BF16)] * 2 + [(rows_u, half, BF16)] * 2 + [(rows_u, cut, BF16), (rows_u, wide - cut, BF16), (rows_o, D, BF16)]
    sizes.append(small.shape[-2:] + (F32,))
    firsts = ["x", "y"] * 3 + ["y", "x"]
    scratch = []
    for (r, w, t), first in zip(sizes, firsts):
        scratch += buffers(dims, r, w, t, first)
    totals = pl.pallas_call(
        functools.partial(reduce_kernel, dims, views, firsts),
        in_specs=[pl.BlockSpec(memory_space=pl.ANY)] * 5,
        out_specs=[pl.BlockSpec(memory_space=pltpu.VMEM)] * len(sizes),
        out_shape=[jax.ShapeDtypeStruct((nz, ny, nx, r, w), t) for r, w, t in sizes],
        scratch_shapes=scratch,
        compiler_params=pltpu.CompilerParams(collective_id=0, has_side_effects=True, vmem_limit_bytes=60 * 2**20),
        name="all_reduce",
    )(down, up, qkv, out, small)
    flat = [t.reshape(-1, t.shape[-1]) for t in totals]
    return (
        jnp.concatenate(flat[:2], axis=0).astype(F32),
        jnp.concatenate(flat[2:4], axis=1).astype(F32),
        jnp.concatenate(flat[4:6], axis=1).astype(F32),
        flat[6].astype(F32),
        flat[7].reshape(-1),
    )


class Route:
    def __init__(self, dims, first, near, far, mine, pair, total, out, bufs, sems):
        self.dims, self.first, self.near, self.far = dims, first, near, far
        self.mine, self.pair, self.total, self.out = mine, pair, total, out
        self.land, self.land2, self.land3 = bufs
        self.sems = sems
        self.count = 0
        self.flight = []

    def launch(self, make):
        slot = self.count
        self.count += 1
        make(slot).start()
        self.flight.append(lambda: make(slot))

    def remote(self, src, dst, where):
        self.launch(
            lambda slot: pltpu.make_async_remote_copy(
                src_ref=src(), dst_ref=dst(), send_sem=self.sems.at[0, slot], recv_sem=self.sems.at[1, slot],
                device_id=where(), device_id_type=pl.DeviceIdType.MESH,
            )
        )

    def local(self, src, dst):
        self.launch(lambda slot: pltpu.make_async_copy(src(), dst(), self.sems.at[0, slot]))

    def settle(self):
        for make in self.flight:
            make().wait()
        self.flight = []

    def steps(self, place):
        z, y, x, side, index = place
        nz, ny, nx = self.dims
        plain = self.first == "x"
        one, two = (2, 1) if plain else (1, 2)
        own = (z, y, x)

        def peer(axis, shift):
            return lax.rem(own[axis] + shift, self.dims[axis])

        def device(axis, shift):
            at = list(own)
            at[axis] = peer(axis, shift)
            return ((at[0] * ny + at[1]) * nx + at[2], side)

        def row(ref, i):
            return ref[i, :, x] if plain else ref[i, y]

        def start():
            if self.near is not None:
                self.local(lambda: self.near(), lambda: self.mine())
            self.remote(lambda: self.far(), lambda: self.pair(), lambda: (index, 1 - side))

        def pair_add():
            self.settle()
            mine, pair = self.mine(), self.pair()

            def body(i, _):
                mine[i] = (mine[i].astype(F32) + pair[i].astype(F32)).astype(mine.dtype)
                return 0

            lax.fori_loop(0, nz, body, 0)
            for s in range(1, self.dims[one]):
                self.remote(
                    lambda s=s: self.mine().at[:, :, peer(one, s)] if plain else self.mine().at[:, peer(one, s)],
                    lambda s=s: self.land().at[s - 1],
                    lambda s=s: device(one, s),
                )

        def add_one():
            self.settle()
            mine, land = self.mine(), self.land()

            def body(i, _):
                v = row(mine, i).astype(F32)
                for s in range(1, self.dims[one]):
                    v = v + land[s - 1, i].astype(F32)
                if plain:
                    mine[i, :, x] = v.astype(mine.dtype)
                else:
                    mine[i, y] = v.astype(mine.dtype)
                return 0

            lax.fori_loop(0, nz, body, 0)
            for s in range(1, self.dims[two]):
                self.remote(
                    lambda s=s: self.mine().at[:, peer(two, s), x] if plain else self.mine().at[:, y, peer(two, s)],
                    lambda s=s: self.land2().at[s - 1],
                    lambda s=s: device(two, s),
                )

        def add_two():
            self.settle()
            mine, land = self.mine(), self.land2()

            def body(i, _):
                v = mine[i, y, x].astype(F32)
                for s in range(1, self.dims[two]):
                    v = v + land[s - 1, i].astype(F32)
                mine[i, y, x] = v.astype(mine.dtype)
                return 0

            lax.fori_loop(0, nz, body, 0)
            for s in range(1, nz):
                self.remote(
                    lambda s=s: self.mine().at[peer(0, s), y, x], lambda s=s: self.land3().at[s - 1], lambda s=s: device(0, s)
                )

        def spread(axis, view):
            for s in range(1, self.dims[axis]):
                self.remote(lambda: view(self.total()), lambda: view(self.total()), lambda s=s: device(axis, s))

        def add_three():
            self.settle()
            mine, land, total = self.mine(), self.land3(), self.total()
            v = mine[z, y, x].astype(F32)
            for s in range(1, nz):
                v = v + land[s - 1].astype(F32)
            total[z, y, x] = v.astype(total.dtype)
            spread(0, lambda t: t.at[z, y, x])

        def wide_two():
            self.settle()
            spread(two, lambda t: t.at[:, y, x])

        def wide_one():
            self.settle()
            spread(one, lambda t: t.at[:, :, x] if plain else t.at[:, y])

        def leave():
            self.settle()
            self.local(lambda: self.total(), lambda: self.out())

        return [start, pair_add, add_one, add_two, add_three, wide_two, wide_one, leave, self.settle]


def route_buffers(dims, rows, width, dtype, first):
    nz, ny, nx = dims
    na, nb = (nx, ny) if first == "x" else (ny, nx)
    tail = (rows, width)
    shapes = [(max(na - 1, 1), nz, nb) + tail, (max(nb - 1, 1), nz) + tail, (max(nz - 1, 1),) + tail]
    copies = 3 + 2 * (na + nb + nz - 3)
    return [pltpu.VMEM(s, dtype) for s in shapes] + [pltpu.SemaphoreType.DMA((2, copies))]


PAIRS = D // 128
BLOCK = 256


def tail_kernel(dims, table, late, schedule, count, *refs):
    (
        prefix_ref, q_ref, k_ref, v_ref, o_ref, g_ref, lse_ref, n1t_ref, w_ref, x_ref, gm_ref, gain_ref, svec_ref, swide_ref,
        down_ref, up_ref, outw_ref, ig_ref, odown_ref, oup_ref, oqkv_ref, oout_ref, osmall_ref,
        gproj, gqkv, bias, sums, small,
        mdown, mup, mout, pdown, pup, pout, pqkv, psmall, tdown, tup, tqkv, tout, tsmall,
    ) = refs[:41]
    scratch = refs[41:]
    pid = pl.program_id(0)
    index, side = lax.axis_index("dp"), lax.axis_index("tensor")
    nz, ny, nx = dims
    place = (index // (ny * nx), lax.rem(index // nx, ny), lax.rem(index, nx), side, index)
    half = D // 2

    @pl.when(pid == 0)
    def _():
        barrier = pltpu.get_barrier_semaphore()
        peers = [(index, 1 - side)]
        for axis in range(3):
            for s in range(1, dims[axis]):
                at = list(place[:3])
                at[axis] = lax.rem(at[axis] + s, dims[axis])
                peers.append(((at[0] * ny + at[1]) * nx + at[2], side))
        for peer in peers:
            pl.semaphore_signal(barrier, inc=1, device_id=peer, device_id_type=pl.DeviceIdType.MESH)
        pl.semaphore_wait(barrier, len(peers))
        sums[...] = jnp.zeros_like(sums)

    homes = {
        "down": (down_ref, mdown, pdown, tdown, odown_ref),
        "up": (up_ref, mup, pup, tup, oup_ref),
        "qkv": (gqkv, gqkv, pqkv, tqkv, oqkv_ref),
        "out": (outw_ref, mout, pout, tout, oout_ref),
        "small": (small, small, psmall, tsmall, osmall_ref),
    }
    plans = []
    for n, (name, lead, near, width, first) in enumerate(table):
        src, mine, pair, total, out = homes[name]
        bufs = scratch[4 * n : 4 * n + 4]
        cols = lambda r, a, width=width: r.at[:, :, :, :, a : a + width]
        if name == "down":
            views = dict(
                near=lambda s=src, l=lead, c=cols, a=near: c(s.at[0, l], a), far=lambda s=src, l=lead, c=cols, a=near: c(s.at[1, l], a),
                mine=lambda s=mine, l=lead, c=cols, a=near: c(s.at[l], a), pair=lambda s=pair, l=lead, c=cols, a=near: c(s.at[l], a),
                total=lambda s=total, l=lead, c=cols, a=near: c(s.at[l], a), out=lambda s=out, l=lead, c=cols, a=near: c(s.at[l], a),
            )
        elif name in ("up", "qkv"):
            size = lead
            views = dict(
                near=None if name == "qkv" else (lambda s=src, c=cols, a=near: c(s, a)),
                far=lambda s=src, c=cols, a=near, n=size: c(s, a + n), mine=lambda s=mine, c=cols, a=near: c(s, a),
                pair=lambda s=pair, c=cols, a=near: c(s, a), total=lambda s=total, c=cols, a=near: c(s, a),
                out=lambda s=out, c=cols, a=near: c(s, a),
            )
            if name == "qkv":
                views["out"] = lambda s=out, c=cols, a=near: c(s.at[a // (D // 2)], a % (D // 2))
        elif name == "out":
            views = dict(
                near=lambda s=src, c=cols, a=near: c(s.at[0], a), far=lambda s=src, c=cols, a=near: c(s.at[1], a),
                mine=lambda s=mine, c=cols, a=near: c(s, a), pair=lambda s=pair, c=cols, a=near: c(s, a),
                total=lambda s=total, c=cols, a=near: c(s, a), out=lambda s=out, c=cols, a=near: c(s, a),
            )
        else:
            views = dict(
                near=None, far=lambda s=src: s.at[1], mine=lambda s=mine: s.at[0],
                pair=lambda s=pair: s, total=lambda s=total: s, out=lambda s=out: s,
            )
        bufs = [(lambda b=b: b) for b in bufs[:3]] + [bufs[3]]
        plans.append(Route(dims, first, bufs=bufs[:3], sems=bufs[3], **views).steps(place))

    def advance(step):
        for n, k in schedule.get(step, ()):
            plans[n][k]()

    for step in range(count):
        if schedule.get(step):
            pl.when(pid == step)(functools.partial(advance, step))

    @pl.when(pid < PAIRS)
    def _():
        column = lambda c: gproj.at[:, pl.ds(pl.multiple_of(head_block(pid, c) * 128, 128), 128)]
        attn_bwd_kernel(
            prefix_ref, q_ref, k_ref, v_ref, o_ref, g_ref, lse_ref, column(0), column(1), column(2),
            bias.at[:, pl.ds(pl.multiple_of(pid * 128, 128), 128)],
        )

    @pl.when(pid == PAIRS)
    def _():
        def body(c, _):
            at = pl.ds(pl.multiple_of(c * D, 128), D)
            part = nn(n1t_ref[...], gproj[:, at]).astype(BF16)
            gqkv[:, :, :, :, at] = part.reshape(gqkv.shape[:4] + (D,))
            return 0

        lax.fori_loop(0, 3, body, 0)

    @pl.when(pid > PAIRS)
    def _():
        rows = pl.ds(pl.multiple_of((pid - PAIRS - 1) * BLOCK, BLOCK), BLOCK)
        e = nt(gproj[rows, :], w_ref[...])
        xhat, inv = normed(x_ref[...].astype(F32))
        sums[0] += colsum(e * xhat)
        sums[1] += colsum(e)
        ig_ref[...] = gm_ref[...] + normed_back(e * gain_ref[...], xhat, inv)

    @pl.when(pid == count - 1)
    def _():
        small[...] = jnp.zeros_like(small)
        split = [bias[i : i + 1, :] for i in range(2)]
        split += [jnp.sum(svec_ref[i], axis=0, keepdims=True) for i in range(2)]
        split += [jnp.sum(swide_ref[i], axis=0, keepdims=True) for i in range(3)]
        shared = [jnp.sum(sums[i], axis=0, keepdims=True) for i in range(2)]
        shared += [jnp.sum(svec_ref[i], axis=0, keepdims=True) for i in range(2, 6)]
        for s in range(2):
            at = 0
            for v in [v[:, s * (v.shape[1] // 2) : (s + 1) * (v.shape[1] // 2)] for v in split] + shared:
                for c in range(v.shape[1] // 128):
                    p = at // 8
                    small[s, p // (ny * nx), p // nx % ny, p % nx, at % 8 : at % 8 + 1, :] = v[:, c * 128 : (c + 1) * 128]
                    at += 1
        for n, k in late:
            plans[n][k]()


def tail_stage(dims, prefix, qkv, attended, ga, lse, n1t, wqkv, tokens, gm, pre_gain, svec, swide, g_down, g_up, g_out):
    nz, ny, nx = dims
    parts = nz * ny * nx
    length = qkv.shape[0]
    ff = g_down.shape[0] // 2
    half = ff // 2
    rows = D // parts
    wide = 3 * D // 2
    small_rows = 8
    down = g_down.reshape(2, 2, nz, ny, nx, rows, D)
    up = g_up.reshape(nz, ny, nx, rows, 2 * ff)
    out = g_out.reshape(2, nz, ny, nx, rows // 2, D)
    table = []
    for a in (0, D // 2):
        table += [("down", 0, a, D // 2, "x"), ("down", 1, a, D // 2, "y")]
    for a in (0, half // 2):
        table += [("up", ff, a, half // 2, "x"), ("up", ff, half + a, half // 2, "y")]
    third = D // 2
    table += [("out", 0, 0, third, "x"), ("out", 0, third, third, "y")]
    table += [("qkv", wide, 0, third, "x"), ("qkv", wide, 2 * third, third, "y")]
    table += [("qkv", wide, third, 256, "x"), ("qkv", wide, third + 256, 128, "y")]
    table += [("small", 0, 0, 128, "x")]
    groups = [(0, 1), (2, 3), (4, 5), (6, 7), (8, 9), (10, 11), (12, 13), (14,)]
    enter = [0, 1, 2, 3, 4, 5, 6, 7]
    count = PAIRS + 1 + length // BLOCK
    at_step = [0, 0, 1, 3, 5, 7, 7, 10]
    schedule, late = {}, []
    depth = 9
    for slot in range(enter[-1] + depth):
        for g, members in enumerate(groups):
            k = slot - enter[g]
            if not 0 <= k < depth:
                continue
            for n in members:
                if slot < len(at_step) - 1:
                    schedule.setdefault(at_step[slot], []).append((n, k))
                else:
                    late.append((n, k))
    sds = jax.ShapeDtypeStruct
    scratch = [
        pltpu.VMEM((length, 3 * D), BF16), pltpu.VMEM((nz, ny, nx, rows, 3 * D), BF16), pltpu.VMEM((8, D), F32),
        pltpu.VMEM((2, 8, D), F32), pltpu.VMEM((2, nz, ny, nx, small_rows, 128), F32),
    ]
    shapes = {
        "down": (2, nz, ny, nx, rows, D), "up": (nz, ny, nx, rows, ff), "out": (nz, ny, nx, rows // 2, D),
        "qkv": (nz, ny, nx, rows, wide), "small": (nz, ny, nx, small_rows, 128),
    }
    landed = {n: (3,) + v[:4] + (wide // 3,) if n == "qkv" else v for n, v in shapes.items()}
    kinds = {n: F32 if n == "small" else BF16 for n in shapes}
    scratch += [pltpu.VMEM(shapes[n], kinds[n]) for n in ("down", "up", "out")]
    scratch += [pltpu.VMEM(shapes[n], kinds[n]) for n in ("down", "up", "out", "qkv", "small")]
    scratch += [pltpu.VMEM(shapes[n], kinds[n]) for n in ("down", "up", "qkv", "out", "small")]
    heights = {"down": rows, "up": rows, "qkv": rows, "out": rows // 2, "small": small_rows}
    for name, _, _, width, first in table:
        scratch += route_buffers(dims, heights[name], width, kinds[name], first)
    pair_at = lambda i: jnp.minimum(i, PAIRS - 1)
    block_at = lambda i: jnp.maximum(i - PAIRS - 1, 0)
    col = lambda c: pl.BlockSpec((length, 128), lambda i, c=c: (0, head_block(pair_at(i), c)))
    one = pl.BlockSpec((length, 128), lambda i: (0, pair_at(i)))
    block = pl.BlockSpec((BLOCK, D), lambda i: (block_at(i), 0))
    whole = lambda v: pl.BlockSpec(v.shape, lambda i, n=v.ndim: (0,) * n, pipeline_mode=pl.Buffered(1))
    hbm = pl.BlockSpec(memory_space=pl.ANY)
    gain = pre_gain.reshape(1, D)
    order = ("down", "up", "qkv", "out", "small")
    results = pl.pallas_call(
        functools.partial(tail_kernel, dims, table, late, schedule, count),
        grid=(count,),
        in_specs=[
            pl.BlockSpec(memory_space=pltpu.SMEM), col(0), col(1), col(2), one, one,
            pl.BlockSpec((1, 8, length), lambda i: (pair_at(i), 0, 0)), whole(n1t), whole(wqkv), block, block, whole(gain),
            whole(svec), whole(swide), hbm, hbm, hbm,
        ],
        out_specs=[block] + [hbm] * 5,
        out_shape=[sds((length, D), F32)] + [sds(landed[n], kinds[n]) for n in order],
        scratch_shapes=scratch,
        compiler_params=pltpu.CompilerParams(collective_id=1, has_side_effects=True, vmem_limit_bytes=63 * 2**20),
        name="tail_stage",
    )(prefix, qkv, qkv, qkv, attended, ga, lse, n1t, wqkv, tokens, gm, gain, svec, swide, down, up, out)
    input_grad, t_down, t_up, t_qkv, t_out, t_small = results
    return (
        input_grad, t_down.reshape(ff, D).astype(F32), t_up.reshape(D, ff).astype(F32), t_qkv.reshape(3, D, wide // 3).astype(F32),
        t_out.reshape(D // 2, D).astype(F32), t_small.reshape(-1),
    )


def head_kernel(
    x_ref, gain_ref, bias_ref, w_ref, wo_ref, sub_gain, sub_bias, up_bias, inner_gain, inner_bias, qv_ref,
    out_bias, ffn_gain, ffn_bias, down_bias,
    qkv_ref, n1t_ref, wall_ref, far_wo, vec_ref, wide_ref,
    near_sem, send_sem, recv_sem, norm_ref, far_small, far_wide, far_qv,
):
    index, side = lax.axis_index("dp"), lax.axis_index("tensor")
    other = (index, 1 - side)
    mesh_id = pl.DeviceIdType.MESH
    barrier = pltpu.get_barrier_semaphore()
    pl.semaphore_signal(barrier, inc=1, device_id=other, device_id_type=mesh_id)
    half = D // 2
    wide = 3 * half
    here = [pltpu.make_async_copy(w_ref.at[c], wall_ref.at[:, c * half : (c + 1) * half], near_sem.at[c]) for c in range(3)]
    for copy in here:
        copy.start()
    pl.semaphore_wait(barrier, 1)
    away = [(w_ref.at[c], wall_ref.at[:, wide + c * half : wide + (c + 1) * half]) for c in range(3)]
    away += [(qv_ref, far_qv), (sub_gain, far_small.at[0]), (sub_bias, far_small.at[1])]
    away += [(up_bias, far_wide.at[0]), (inner_gain, far_wide.at[1]), (inner_bias, far_wide.at[2]), (wo_ref, far_wo)]
    away = [
        pltpu.make_async_remote_copy(
            src_ref=a, dst_ref=b, send_sem=send_sem.at[i], recv_sem=recv_sem.at[i], device_id=other, device_id_type=mesh_id
        )
        for i, (a, b) in enumerate(away)
    ]
    for copy in away:
        copy.start()
    length = x_ref.shape[0]
    block = 256

    def norm(i, _):
        rows = pl.ds(pl.multiple_of(i * block, block), block)
        xhat, _ = normed(x_ref[rows, :].astype(F32))
        n1 = (xhat * gain_ref[...] + bias_ref[...]).astype(BF16)
        norm_ref[rows, :] = n1
        n1t_ref[:, rows] = n1.T
        return 0

    lax.fori_loop(0, length // block, norm, 0)

    def product(first, biases):
        weight = wall_ref[:, first : first + wide]
        bias = jnp.concatenate([biases[0:1, :], jnp.zeros((1, half), F32), biases[1:2, :]], axis=1)

        def rows(i, _):
            at = pl.ds(pl.multiple_of(i * block, block), block)
            qkv_ref[at, first : first + wide] = (nn(norm_ref[at, :], weight) + bias).astype(BF16)
            return 0

        lax.fori_loop(0, length // block, rows, 0)

    for copy in here:
        copy.wait()
    product(0, qv_ref[...])
    for copy in away:
        copy.wait()
    product(wide, far_qv[...])
    vec_ref[0:1, :] = jnp.concatenate([sub_gain[...], far_small[0]], axis=1)
    vec_ref[1:2, :] = jnp.concatenate([sub_bias[...], far_small[1]], axis=1)
    for i, v in enumerate((out_bias, ffn_gain, ffn_bias, down_bias)):
        vec_ref[i + 2 : i + 3, :] = v[...]
    for i, v in enumerate((up_bias, inner_gain, inner_bias)):
        wide_ref[i : i + 1, :] = jnp.concatenate([v[...], far_wide[i]], axis=1)


def head_stage(tokens, pre_gain, pre_bias, w3, wo, sub_gain, sub_bias, up_bias, inner_gain, inner_bias, qv_bias, *rest):
    length = tokens.shape[0]
    row = lambda v: v.reshape(1, -1)
    ff_half = up_bias.shape[0]
    half = D // 2
    sds = jax.ShapeDtypeStruct
    vmem, hbm = pl.BlockSpec(memory_space=pltpu.VMEM), pl.BlockSpec(memory_space=pl.ANY)
    return pl.pallas_call(
        head_kernel,
        in_specs=[vmem] * 3 + [hbm] * 2 + [vmem] * 10,
        out_specs=[vmem] * 3 + [hbm] + [vmem] * 2,
        out_shape=[
            sds((length, 3 * D), BF16), sds((D, length), BF16), sds((D, 3 * D), BF16), sds(wo.shape, BF16),
            sds((6, D), F32), sds((3, 2 * ff_half), F32),
        ],
        scratch_shapes=[
            pltpu.SemaphoreType.DMA((3,)), pltpu.SemaphoreType.DMA((10,)), pltpu.SemaphoreType.DMA((10,)),
            pltpu.VMEM((length, D), BF16), pltpu.VMEM((2, 1, half), F32), pltpu.VMEM((3, 1, ff_half), F32), pltpu.VMEM((2, half), F32),
        ],
        compiler_params=pltpu.CompilerParams(collective_id=2, has_side_effects=True, vmem_limit_bytes=40 * 2**20),
        name="head_stage",
    )(
        tokens, row(pre_gain), row(pre_bias), w3, wo, row(sub_gain), row(sub_bias), row(up_bias), row(inner_gain), row(inner_bias),
        qv_bias, *[row(v) for v in rest],
    )


def pack_small(dims, g_qv, g_vec, g_wide, g_pre):
    half, ff_half = D // 2, g_wide.shape[1] // 2
    shared = jnp.concatenate([g_pre.reshape(-1), g_vec[2:].reshape(-1)])
    rows = -(-(4 * half + 3 * ff_half + 6 * D) // (128 * 8 * math.prod(dims))) * 8
    pad = jnp.zeros((rows * 128 * math.prod(dims) - (4 * half + 3 * ff_half + 6 * D),), F32)
    pack = lambda i: jnp.concatenate(
        [v[j, i * n : (i + 1) * n] for v, m, n in ((g_qv, 2, half), (g_vec, 2, half), (g_wide, 3, ff_half)) for j in range(m)] + [shared, pad]
    )
    return jnp.stack([pack(0), pack(1)]).reshape((2,) + dims + (rows, 128))


def swap(value):
    return lax.ppermute(value, "tensor", ((0, 1), (1, 0)))


def body(
    dims, tokens, grad_out, prefix, pre_gain, pre_bias, qkv_weight, qv_bias, sub_gain, sub_bias, out_weight, out_bias,
    ffn_gain, ffn_bias, up_weight, up_bias, inner_gain, inner_bias, down_weight, down_bias,
):
    side = lax.axis_index("tensor")
    local = lax.dynamic_slice_in_dim(prefix, side, 1)
    half, ff_half = D // 2, up_bias.shape[0]
    wu, wd = (up_weight, swap(up_weight)), (down_weight, swap(down_weight))
    qkv, n1t, wqkv, far_wo, vecs, wides = head_stage(
        tokens, pre_gain, pre_bias, qkv_weight.transpose(1, 0, 2), out_weight, sub_gain, sub_bias, up_bias, inner_gain, inner_bias,
        qv_bias, out_bias, ffn_gain, ffn_bias, down_bias,
    )
    attended, lse, out, gm, ga, svec, swide, g_down, g_up, g_out = front(
        tokens, grad_out, local, qkv, vecs, wides, (out_weight, far_wo), wu, wd
    )
    if D // math.prod(dims) % 16 == 0:
        input_grad, g_down, g_up, g_qkv, g_out, small = tail_stage(
            dims, local, qkv, attended, ga, lse, n1t, wqkv, tokens, gm, pre_gain, svec, swide, g_down, g_up, g_out
        )
    else:
        input_grad, g_pre, g_qkv, g_qv = back(local, tokens, pre_gain, wqkv, n1t.T, qkv, attended, lse, gm, ga)
        small = pack_small(dims, g_qv, jnp.sum(svec, 1), jnp.sum(swide, 1), g_pre)
        g_down, g_up, g_qkv, g_out, small = all_reduce(dims, (g_down, g_up, g_qkv, g_out), small)
        g_qkv = g_qkv.reshape(D, 3, half).transpose(1, 0, 2)
    r = lambda i: small[i * half : (i + 1) * half]
    w = lambda i: small[4 * half + i * ff_half : 4 * half + (i + 1) * ff_half]
    base = 4 * half + 3 * ff_half
    f = lambda i: small[base + i * D : base + (i + 1) * D]
    return (
        out, input_grad, f(0), f(1), g_qkv.transpose(1, 0, 2), small[: 2 * half].reshape(2, half), r(2), r(3), g_out,
        f(2), f(3), f(4), g_up, w(0), w(1), w(2), g_down, f(5),
    )


def solution(mesh):
    rows = P(("dp", "tensor"), None)
    wide, tall, vec, whole = P(None, "tensor"), P("tensor", None), P("tensor"), P()
    cube = P(None, None, "tensor")
    return jax.shard_map(
        functools.partial(body, grid_of(mesh.shape["dp"])),
        mesh=mesh,
        in_specs=(
            rows, rows, P("dp"), whole, whole, cube, wide, vec, vec, tall, whole, whole, whole, wide, vec, vec, vec, tall, whole,
        ),
        out_specs=(
            rows, rows, whole, whole, cube, wide, vec, vec, tall, whole, whole, whole, wide, vec, vec, vec, tall, whole,
        ),
        check_vma=False,
    )
```

```python
import functools
import math

import jax
import jax.numpy as jnp
from jax import lax
from jax.sharding import PartitionSpec as P
from jax.experimental import pallas as pl
from jax.experimental.pallas import tpu as pltpu

D = 768
HEAD_DIM = 64
PREFIX_MAX = 512
EPS = 1e-05
F32 = jnp.float32
BF16 = jnp.bfloat16
QB = 512
VMEM = 67043328


def nn(a, b):
    return lax.dot_general(a, b, (((1,), (0,)), ((), ())), preferred_element_type=F32)


def nt(a, b):
    return lax.dot_general(a, b, (((1,), (1,)), ((), ())), preferred_element_type=F32)


def tn(a, b):
    return lax.dot_general(a, b, (((0,), (0,)), ((), ())), preferred_element_type=F32)


def halves(v):
    left = lax.broadcasted_iota(jnp.int32, v.shape, 1) < HEAD_DIM
    zero = jnp.zeros_like(v)
    return jnp.where(left, v, zero), jnp.where(left, zero, v)


def spans(start, length, block):
    last = min(length, max(start + block, PREFIX_MAX))
    out = []
    if start:
        out.append((0, start, False))
    out.append((start, last, True))
    return out


def masked(scores, key_start, query_start, prefix):
    key_pos = key_start + lax.broadcasted_iota(jnp.int32, scores.shape, 0)
    query_pos = query_start + lax.broadcasted_iota(jnp.int32, scores.shape, 1)
    seen = key_pos <= query_pos
    if key_start < PREFIX_MAX:
        seen = seen | (key_pos < prefix)
    return jnp.where(seen, scores, -1e30)


def head_block(i, c):
    each = D // 256
    return i // each * 3 * each + c * each + lax.rem(i, each)


def attn_fwd_kernel(prefix_ref, q_ref, k_ref, v_ref, wu_ref, wd_ref, o_ref, lse_ref, far_wu, far_wd, send_sem, recv_sem):
    pid = pl.program_id(0)
    other = (lax.axis_index("dp"), 1 - lax.axis_index("tensor"))

    def exchange(i, src, dst):
        return pltpu.make_async_remote_copy(
            src_ref=src, dst_ref=dst, send_sem=send_sem.at[i], recv_sem=recv_sem.at[i], device_id=other,
            device_id_type=pl.DeviceIdType.MESH,
        )

    @pl.when(pid == 0)
    def _():
        barrier = pltpu.get_barrier_semaphore()
        pl.semaphore_signal(barrier, inc=1, device_id=other, device_id_type=pl.DeviceIdType.MESH)
        pl.semaphore_wait(barrier, 1)
        exchange(0, wu_ref, far_wu).start()
        exchange(1, wd_ref, far_wd).start()

    length = q_ref.shape[0]
    prefix = prefix_ref[lax.axis_index("tensor")]
    keys = halves(k_ref[...])
    value_t = v_ref[...].T
    for start in range(0, length, QB):
        query = q_ref[start : start + QB, :] * jnp.asarray(HEAD_DIM**-0.5, BF16)
        parts = []
        for head in range(2):
            scores = []
            for first, last, mask in spans(start, length, QB):
                s = nt(keys[head][first:last], query)
                scores.append(masked(s, first, start, prefix) if mask else s)
            peak = functools.reduce(jnp.maximum, [jnp.max(s, axis=0, keepdims=True) for s in scores])
            total = jnp.zeros_like(peak)
            mixed = jnp.zeros((HEAD_DIM, QB), F32)
            rows = slice(head * HEAD_DIM, (head + 1) * HEAD_DIM)
            for s, (first, last, _) in zip(scores, spans(start, length, QB)):
                w = jnp.exp(s - peak)
                total = total + jnp.sum(w, axis=0, keepdims=True)
                mixed = mixed + nn(value_t[rows, first:last], w.astype(BF16))
            parts.append(mixed / total)
            lse_ref[0, head : head + 1, start : start + QB] = peak + jnp.log(total)
        o_ref[start : start + QB, :] = jnp.concatenate(parts, axis=0).T

    @pl.when(pid == pl.num_programs(0) - 1)
    def _():
        exchange(0, wu_ref, far_wu).wait()
        exchange(1, wd_ref, far_wd).wait()


def attn_fwd(prefix, qkv, wu, wd):
    length = qkv.shape[0]
    pairs = D // 128
    col = lambda c: pl.BlockSpec((length, 128), lambda i, c=c: (0, head_block(i, c)))
    hbm = pl.BlockSpec(memory_space=pl.ANY)
    return pl.pallas_call(
        attn_fwd_kernel,
        grid=(pairs,),
        in_specs=[pl.BlockSpec(memory_space=pltpu.SMEM), col(0), col(1), col(2), hbm, hbm],
        out_specs=[
            pl.BlockSpec((length, 128), lambda i: (0, i)),
            pl.BlockSpec((1, 8, length), lambda i: (i, 0, 0)),
            hbm,
            hbm,
        ],
        out_shape=[
            jax.ShapeDtypeStruct((length, D), F32),
            jax.ShapeDtypeStruct((pairs, 8, length), F32),
            jax.ShapeDtypeStruct(wu.shape, BF16),
            jax.ShapeDtypeStruct(wd.shape, BF16),
        ],
        scratch_shapes=[pltpu.SemaphoreType.DMA((2,))] * 2,
        compiler_params=pltpu.CompilerParams(collective_id=4, has_side_effects=True, vmem_limit_bytes=VMEM),
        name="attn_fwd",
    )(prefix, qkv, qkv, qkv, wu, wd)


def attn_bwd_kernel(prefix_ref, q_ref, k_ref, v_ref, o_ref, g_ref, lse_ref, dq_ref, dk_ref, dv_ref, bias_ref):
    length = q_ref.shape[0]
    prefix = prefix_ref[lax.axis_index("tensor")]
    scale = HEAD_DIM**-0.5
    keys = halves(k_ref[...])
    values = halves(v_ref[...])
    key_t = k_ref[...].T
    delta_t = (o_ref[...] * g_ref[...].astype(F32)).T
    dk = [jnp.zeros((b - a, 128), F32) for a, b in zip(range(0, length, QB), range(QB, length + 1, QB))]
    dv = list(dk)
    qsum = jnp.zeros((8, 128), F32)
    for start in range(0, length, QB):
        cols = slice(start, start + QB)
        query = q_ref[cols, :] * jnp.asarray(scale, BF16)
        query_half = halves(query)
        grad = g_ref[cols, :]
        grad_half = halves(grad)
        parts = []
        for head in range(2):
            rows = slice(head * HEAD_DIM, (head + 1) * HEAD_DIM)
            lse = lse_ref[0, head : head + 1, cols]
            delta = jnp.sum(delta_t[rows, cols], axis=0, keepdims=True)
            dq = jnp.zeros((HEAD_DIM, QB), F32)
            for first in range(0, length, QB):
                live = [s for s in spans(start, length, QB) if s[0] <= first < s[1]]
                if not live:
                    continue
                last = first + QB
                s = nt(keys[head][first:last], query)
                if live[0][2]:
                    s = masked(s, first, start, prefix)
                w = jnp.exp(s - lse)
                dp = nt(values[head][first:last], grad)
                ds = (w * (dp - delta)).astype(BF16)
                b = first // QB
                dv[b] = dv[b] + nn(w.astype(BF16), grad_half[head])
                dk[b] = dk[b] + nn(ds, query_half[head])
                dq = dq + nn(key_t[rows, first:last], ds)
            parts.append(dq)
        dq = jnp.concatenate(parts, axis=0).T * scale
        qsum = qsum + jnp.sum(dq.reshape(QB // 8, 8, 128), axis=0)
        dq_ref[cols, :] = dq.astype(BF16)
    vsum = jnp.zeros((8, 128), F32)
    for b in range(length // QB):
        cols = slice(b * QB, (b + 1) * QB)
        dk_ref[cols, :] = dk[b].astype(BF16)
        dv_ref[cols, :] = dv[b].astype(BF16)
        vsum = vsum + jnp.sum(dv[b].reshape(QB // 8, 8, 128), axis=0)
    bias_ref[0:1, :] = jnp.sum(qsum, axis=0, keepdims=True)
    bias_ref[1:2, :] = jnp.sum(vsum, axis=0, keepdims=True)


def attn_bwd(prefix, qkv, attended, grad_attended, lse):
    length = qkv.shape[0]
    pairs = D // 128
    col = lambda c: pl.BlockSpec((length, 128), lambda i, c=c: (0, head_block(i, c)))
    one = pl.BlockSpec((length, 128), lambda i: (0, i))
    return pl.pallas_call(
        attn_bwd_kernel,
        grid=(pairs,),
        in_specs=[
            pl.BlockSpec(memory_space=pltpu.SMEM), col(0), col(1), col(2), one, one,
            pl.BlockSpec((1, 8, length), lambda i: (i, 0, 0)),
        ],
        out_specs=[one, one, one, pl.BlockSpec((8, 128), lambda i: (0, i))],
        out_shape=[jax.ShapeDtypeStruct((length, D), BF16)] * 3 + [jax.ShapeDtypeStruct((8, D), F32)],
        name="attn_bwd",
    )(prefix, qkv, qkv, qkv, attended, grad_attended, lse)


def normed(v):
    centre = v - jnp.mean(v, axis=-1, keepdims=True)
    inv = lax.rsqrt(jnp.mean(centre * centre, axis=-1, keepdims=True) + EPS)
    return centre * inv, inv


def normed_back(e, xhat, inv):
    return inv * (e - jnp.mean(e, axis=-1, keepdims=True) - xhat * jnp.mean(e * xhat, axis=-1, keepdims=True))


def colsum(v):
    rows, cols = v.shape
    return jnp.sum(v.reshape(rows // 8, 8, cols), axis=0)


def mid_kernel(
    x_ref, att_ref, g_ref, vec_ref, wide_ref, near_wo, far_wo, near_wu, far_wu, near_wd, far_wd,
    out_ref, n2_ref, n3_ref, n4_ref, gh_ref, gm_ref, gml_ref, ga_ref, svec_ref, swide_ref,
    act_ref, slope_ref, wo_ref, wu_ref, wd_ref, sem,
):
    first = pl.program_id(0) == 0
    half, ff_half = near_wo.shape[0], near_wu.shape[1]
    moves = (
        (near_wo, wo_ref.at[:half]), (far_wo, wo_ref.at[half:]), (near_wu, wu_ref.at[:, :ff_half]), (far_wu, wu_ref.at[:, ff_half:]),
        (near_wd, wd_ref.at[:ff_half]), (far_wd, wd_ref.at[ff_half:]),
    )
    moves = [pltpu.make_async_copy(a, b, sem.at[i]) for i, (a, b) in enumerate(moves)]

    def arrive(some):
        @pl.when(first)
        def _():
            for copy in some:
                copy.wait()

    @pl.when(first)
    def _():
        for copy in moves:
            copy.start()
        svec_ref[...] = jnp.zeros_like(svec_ref)
        swide_ref[...] = jnp.zeros_like(swide_ref)

    sub_gain, sub_bias, out_bias, ffn_gain, ffn_bias, down_bias = [vec_ref[i : i + 1, :] for i in range(6)]
    up_bias, inner_gain, inner_bias = [wide_ref[i : i + 1, :] for i in range(3)]
    xhat2, inv2 = normed(att_ref[...])
    n2 = (xhat2 * sub_gain + sub_bias).astype(BF16)
    n2_ref[...] = n2.T
    arrive(moves[:2])
    middle = x_ref[...].astype(F32) + nn(n2, wo_ref[...]) + out_bias
    xhat3, inv3 = normed(middle)
    n3 = (xhat3 * ffn_gain + ffn_bias).astype(BF16)
    n3_ref[...] = n3.T
    arrive(moves[2:4])
    hidden = nn(n3, wu_ref[...]) + up_bias
    half = 0.5 + 0.5 * lax.erf(hidden * (2.0**-0.5))
    act_ref[...] = hidden * half
    slope_ref[...] = half + hidden * (jnp.exp(-0.5 * hidden * hidden) * 0.3989422804014327)
    xhat4, inv4 = normed(act_ref[...])
    n4 = (xhat4 * inner_gain + inner_bias).astype(BF16)
    n4_ref[...] = n4
    act_ref[...] = xhat4
    arrive(moves[4:])
    out_ref[...] = (middle + nn(n4, wd_ref[...]) + down_bias).astype(BF16)
    g = g_ref[...]
    e = nt(g, wd_ref[...])
    xhat4 = act_ref[...]
    swide_ref[1] += colsum(e * xhat4)
    swide_ref[2] += colsum(e)
    gh = normed_back(e * inner_gain, xhat4, inv4) * slope_ref[...]
    swide_ref[0] += colsum(gh)
    ghl = gh.astype(BF16)
    gh_ref[...] = ghl
    gf = g.astype(F32)
    e = nt(ghl, wu_ref[...])
    svec_ref[3] += colsum(e * xhat3)
    svec_ref[4] += colsum(e)
    gm = gf + normed_back(e * ffn_gain, xhat3, inv3)
    svec_ref[2] += colsum(gm)
    svec_ref[5] += colsum(gf)
    gm_ref[...] = gm
    gml = gm.astype(BF16)
    gml_ref[...] = gml
    e = nt(gml, wo_ref[...])
    svec_ref[0] += colsum(e * xhat2)
    svec_ref[1] += colsum(e)
    ga_ref[...] = normed_back(e * sub_gain, xhat2, inv2).astype(BF16)


def middle_stage(x, att, g, vecs, wides, wo, wu, wd, block=256):
    rows = x.shape[0]
    ff = 2 * wu[0].shape[1]
    row = lambda n: pl.BlockSpec((block, n), lambda i: (i, 0))
    turned = pl.BlockSpec((D, block), lambda i: (0, i))
    whole = lambda s: pl.BlockSpec(s, lambda i: (0,) * len(s), pipeline_mode=pl.Buffered(1))
    sds = jax.ShapeDtypeStruct
    return pl.pallas_call(
        mid_kernel,
        grid=(rows // block,),
        in_specs=[row(D), row(D), row(D), whole(vecs.shape), whole(wides.shape)] + [pl.BlockSpec(memory_space=pl.ANY)] * 6,
        out_specs=[row(D), turned, turned, row(ff), row(ff), row(D), row(D), row(D), whole((6, 8, D)), whole((3, 8, ff))],
        out_shape=[
            sds((rows, D), BF16), sds((D, rows), BF16), sds((D, rows), BF16), sds((rows, ff), BF16), sds((rows, ff), BF16),
            sds((rows, D), F32), sds((rows, D), BF16), sds((rows, D), BF16), sds((6, 8, D), F32), sds((3, 8, ff), F32),
        ],
        scratch_shapes=[pltpu.VMEM((block, ff), F32), pltpu.VMEM((block, ff), F32), pltpu.VMEM((D, D), BF16), pltpu.VMEM((D, ff), BF16), pltpu.VMEM((ff, D), BF16), pltpu.SemaphoreType.DMA((6,))],
        compiler_params=pltpu.CompilerParams(vmem_limit_bytes=VMEM),
        name="middle_stage",
    )(x, att, g, vecs, wides, *wo, *wu, *wd)


def back(prefix, tokens, pre_gain, wqkv, n1, qkv, attended, lse, gm, ga):
    xhat1, inv1 = normed(tokens.astype(F32))
    dq, dk, dv, dbias = attn_bwd(prefix, qkv, attended, ga, lse)
    h = D // 2
    gproj = jnp.concatenate([v[:, s] for s in (slice(0, h), slice(h, D)) for v in (dq, dk, dv)], axis=1)
    g_qkv = tn(n1, gproj).astype(BF16)
    e = nt(gproj, wqkv)
    g_pre = jnp.stack([jnp.sum(e * xhat1, axis=0), jnp.sum(e, axis=0)])
    input_grad = gm + normed_back(e * pre_gain, xhat1, inv1)
    return input_grad, g_pre, g_qkv, dbias


def grid_of(count):
    side = 1
    while 2 * side**3 < count:
        side += 1
    return (2 * side, side, side) if 2 * side**3 == count else (count, 1, 1)


class Piece:
    def __init__(self, dims, first, near, far, total, bufs, sems, place):
        self.dims, self.first, self.near, self.far, self.total = dims, first, near, far, total
        self.mine, self.pair, self.land, self.part, self.land2, self.part2, self.land3 = bufs
        self.sems, self.place = sems, place
        self.count = 0
        self.flight = []

    def send(self, src, dst, where):
        copy = pltpu.make_async_remote_copy(
            src_ref=src, dst_ref=dst, send_sem=self.sems.at[0, self.count], recv_sem=self.sems.at[1, self.count],
            device_id=where, device_id_type=pl.DeviceIdType.MESH,
        )
        self.count += 1
        copy.start()
        self.flight.append(copy)

    def settle(self):
        for copy in self.flight:
            copy.wait()
        self.flight = []

    def device(self, axis, shift):
        at = list(self.place[:3])
        at[axis] = lax.rem(at[axis] + shift, self.dims[axis])
        nz, ny, nx = self.dims
        return at[axis], ((at[0] * ny + at[1]) * nx + at[2], self.place[3])

    def steps(self):
        z, y, x = self.place[:3]
        nz, ny, nx = self.dims
        one, two = (2, 1) if self.first == "x" else (1, 2)
        pick1 = lambda ref, p: ref.at[:, :, p] if one == 2 else ref.at[:, p]
        own1, own2 = (x, y) if one == 2 else (y, x)

        def start():
            local = pltpu.make_async_copy(self.near, self.mine, self.sems.at[0, self.count])
            self.count += 1
            local.start()
            self.send(self.far, self.pair, (self.place[4], 1 - self.place[3]))
            self.flight.append(local)

        def pair_add():
            self.settle()
            def one_row(i, _):
                self.mine[i] = (self.mine[i].astype(F32) + self.pair[i].astype(F32)).astype(self.mine.dtype)
                return 0
            lax.fori_loop(0, nz, one_row, 0)
            for s in range(1, self.dims[one]):
                p, dev = self.device(one, s)
                self.send(pick1(self.mine, p), self.land.at[s - 1], dev)

        def add_one():
            self.settle()
            def one_row(i, _):
                v = (self.mine[i, :, x] if one == 2 else self.mine[i, y]).astype(F32)
                for s in range(1, self.dims[one]):
                    v = v + self.land[s - 1, i].astype(F32)
                self.part[i] = v.astype(self.part.dtype)
                return 0
            lax.fori_loop(0, nz, one_row, 0)
            for s in range(1, self.dims[two]):
                p, dev = self.device(two, s)
                self.send(self.part.at[:, p], self.land2.at[s - 1], dev)

        def add_two():
            self.settle()
            def one_row(i, _):
                v = self.part[i, own2].astype(F32)
                for s in range(1, self.dims[two]):
                    v = v + self.land2[s - 1, i].astype(F32)
                self.part2[i] = v.astype(self.part2.dtype)
                return 0
            lax.fori_loop(0, nz, one_row, 0)
            for s in range(1, nz):
                p, dev = self.device(0, s)
                self.send(self.part2.at[p], self.land3.at[s - 1], dev)

        def add_three():
            self.settle()
            v = self.part2[z].astype(F32)
            for s in range(1, nz):
                v = v + self.land3[s - 1].astype(F32)
            self.total[z, y, x] = v.astype(self.total.dtype)
            spread(0, self.total.at[z, y, x])

        def spread(axis, ref):
            for s in range(1, self.dims[axis]):
                self.send(ref, ref, self.device(axis, s)[1])

        def wide_two():
            self.settle()
            spread(two, self.total.at[:, y, x])

        def wide_one():
            self.settle()
            spread(one, self.total.at[:, :, x] if one == 2 else self.total.at[:, y])

        return [start, pair_add, add_one, add_two, add_three, wide_two, wide_one, self.settle]


def buffers(dims, rows, width, dtype, first):
    nz, ny, nx = dims
    na, nb = (nx, ny) if first == "x" else (ny, nx)
    tail = (rows, width)
    shapes = [
        (nz, ny, nx) + tail, (nz, ny, nx) + tail, (max(na - 1, 1), nz, nb) + tail, (nz, nb) + tail,
        (max(nb - 1, 1), nz) + tail, (nz,) + tail, (max(nz - 1, 1),) + tail,
    ]
    copies = 2 + 2 * (na + nb + nz - 3)
    return [pltpu.VMEM(s, dtype) for s in shapes] + [pltpu.SemaphoreType.DMA((2, copies))]


def reduce_kernel(dims, views, firsts, *refs):
    count = len(firsts)
    sources = refs[: len(views)]
    totals = refs[len(views) : len(views) + count]
    scratch = refs[len(views) + count :]
    index, side = lax.axis_index("dp"), lax.axis_index("tensor")
    nz, ny, nx = dims
    place = (index // (ny * nx), lax.rem(index // nx, ny), lax.rem(index, nx), side, index)
    barrier = pltpu.get_barrier_semaphore()
    peers = [(index, 1 - side)]
    probe = Piece(dims, "x", None, None, None, [None] * 7, None, place)
    for axis in range(3):
        for s in range(1, dims[axis]):
            peers.append(probe.device(axis, s)[1])
    for peer in peers:
        pl.semaphore_signal(barrier, inc=1, device_id=peer, device_id_type=pl.DeviceIdType.MESH)
    pl.semaphore_wait(barrier, len(peers))
    plans = []
    at = 0
    for source, view in zip(sources, views):
        for near, far in view(source):
            plans.append(Piece(dims, firsts[at], near, far, totals[at], scratch[8 * at : 8 * at + 7], scratch[8 * at + 7], place).steps())
            at += 1
    slots = len(plans[0]) + (count + 1) // 2 - 1
    for slot in range(slots):
        for i, plan in enumerate(plans):
            if 0 <= slot - i // 2 < len(plan):
                plan[slot - i // 2]()


def all_reduce(dims, grads, small):
    g_down, g_up, g_qkv, g_out = grads
    nz, ny, nx = dims
    parts = nz * ny * nx
    ff = g_down.shape[0] // 2
    half = ff // 2
    rows_d, rows_u, rows_o = half // parts, D // parts, D // 2 // parts
    cut = 640
    down = g_down.reshape(2, 2, nz, ny, nx, rows_d, D)
    up = g_up.reshape(nz, ny, nx, rows_u, 2 * ff)
    qkv = g_qkv.reshape(nz, ny, nx, rows_u, 3 * D)
    out = g_out.reshape(2, nz, ny, nx, rows_o, D)
    cols = lambda r, a, n: r.at[:, :, :, :, a : a + n]
    wide = 3 * D // 2
    views = [
        lambda r: [(r.at[0, 0], r.at[1, 0]), (r.at[0, 1], r.at[1, 1])],
        lambda r: [(cols(r, 0, half), cols(r, ff, half)), (cols(r, half, half), cols(r, ff + half, half))],
        lambda r: [(cols(r, 0, cut), cols(r, wide, cut)), (cols(r, cut, wide - cut), cols(r, wide + cut, wide - cut))],
        lambda r: [(r.at[0], r.at[1])],
        lambda r: [(r.at[0], r.at[1])],
    ]
    sizes = [(rows_d, D, BF16)] * 2 + [(rows_u, half, BF16)] * 2 + [(rows_u, cut, BF16), (rows_u, wide - cut, BF16), (rows_o, D, BF16)]
    sizes.append(small.shape[-2:] + (F32,))
    firsts = ["x", "y"] * 3 + ["y", "x"]
    scratch = []
    for (r, w, t), first in zip(sizes, firsts):
        scratch += buffers(dims, r, w, t, first)
    totals = pl.pallas_call(
        functools.partial(reduce_kernel, dims, views, firsts),
        in_specs=[pl.BlockSpec(memory_space=pl.ANY)] * 5,
        out_specs=[pl.BlockSpec(memory_space=pltpu.VMEM)] * len(sizes),
        out_shape=[jax.ShapeDtypeStruct((nz, ny, nx, r, w), t) for r, w, t in sizes],
        scratch_shapes=scratch,
        compiler_params=pltpu.CompilerParams(collective_id=0, has_side_effects=True, vmem_limit_bytes=60 * 2**20),
        name="all_reduce",
    )(down, up, qkv, out, small)
    flat = [t.reshape(-1, t.shape[-1]) for t in totals]
    return (
        jnp.concatenate(flat[:2], axis=0).astype(F32),
        jnp.concatenate(flat[2:4], axis=1).astype(F32),
        jnp.concatenate(flat[4:6], axis=1).astype(F32),
        flat[6].astype(F32),
        flat[7].reshape(-1),
    )


class Route:
    def __init__(self, dims, first, near, far, mine, pair, total, bufs, sems):
        self.dims, self.first, self.near, self.far = dims, first, near, far
        self.mine, self.pair, self.total = mine, pair, total
        self.land, self.land2, self.land3 = bufs
        self.sems = sems
        self.count = 0
        self.flight = []

    def launch(self, make):
        slot = self.count
        self.count += 1
        make(slot).start()
        self.flight.append(lambda: make(slot))

    def remote(self, src, dst, where):
        self.launch(
            lambda slot: pltpu.make_async_remote_copy(
                src_ref=src(), dst_ref=dst(), send_sem=self.sems.at[0, slot], recv_sem=self.sems.at[1, slot],
                device_id=where(), device_id_type=pl.DeviceIdType.MESH,
            )
        )

    def local(self, src, dst):
        self.launch(lambda slot: pltpu.make_async_copy(src(), dst(), self.sems.at[0, slot]))

    def settle(self):
        for make in self.flight:
            make().wait()
        self.flight = []

    def steps(self, place):
        z, y, x, side, index = place
        nz, ny, nx = self.dims
        plain = self.first == "x"
        one, two = (2, 1) if plain else (1, 2)
        own = (z, y, x)

        def peer(axis, shift):
            return lax.rem(own[axis] + shift, self.dims[axis])

        def device(axis, shift):
            at = list(own)
            at[axis] = peer(axis, shift)
            return ((at[0] * ny + at[1]) * nx + at[2], side)

        def row(ref, i):
            return ref[i, :, x] if plain else ref[i, y]

        def start():
            if self.near is not None:
                self.local(lambda: self.near(), lambda: self.mine())
            self.remote(lambda: self.far(), lambda: self.pair(), lambda: (index, 1 - side))

        def pair_add():
            self.settle()
            mine, pair = self.mine(), self.pair()

            def body(i, _):
                mine[i] = (mine[i].astype(F32) + pair[i].astype(F32)).astype(mine.dtype)
                return 0

            lax.fori_loop(0, nz, body, 0)
            for s in range(1, self.dims[one]):
                self.remote(
                    lambda s=s: self.mine().at[:, :, peer(one, s)] if plain else self.mine().at[:, peer(one, s)],
                    lambda s=s: self.land().at[s - 1],
                    lambda s=s: device(one, s),
                )

        def add_one():
            self.settle()
            mine, land = self.mine(), self.land()

            def body(i, _):
                v = row(mine, i).astype(F32)
                for s in range(1, self.dims[one]):
                    v = v + land[s - 1, i].astype(F32)
                if plain:
                    mine[i, :, x] = v.astype(mine.dtype)
                else:
                    mine[i, y] = v.astype(mine.dtype)
                return 0

            lax.fori_loop(0, nz, body, 0)
            for s in range(1, self.dims[two]):
                self.remote(
                    lambda s=s: self.mine().at[:, peer(two, s), x] if plain else self.mine().at[:, y, peer(two, s)],
                    lambda s=s: self.land2().at[s - 1],
                    lambda s=s: device(two, s),
                )

        def add_two():
            self.settle()
            mine, land = self.mine(), self.land2()

            def body(i, _):
                v = mine[i, y, x].astype(F32)
                for s in range(1, self.dims[two]):
                    v = v + land[s - 1, i].astype(F32)
                mine[i, y, x] = v.astype(mine.dtype)
                return 0

            lax.fori_loop(0, nz, body, 0)
            for s in range(1, nz):
                self.remote(
                    lambda s=s: self.mine().at[peer(0, s), y, x], lambda s=s: self.land3().at[s - 1], lambda s=s: device(0, s)
                )

        def spread(axis, view, source):
            for s in range(1, self.dims[axis]):
                self.remote(lambda: view(source()), lambda: view(self.total()), lambda s=s: device(axis, s))

        def add_three():
            self.settle()
            mine, land = self.mine(), self.land3()
            v = mine[z, y, x].astype(F32)
            for s in range(1, nz):
                v = v + land[s - 1].astype(F32)
            mine[z, y, x] = v.astype(mine.dtype)
            self.local(lambda: self.mine().at[z, y, x], lambda: self.total().at[z, y, x])
            spread(0, lambda t: t.at[z, y, x], self.mine)

        def wide_two():
            self.settle()
            spread(two, lambda t: t.at[:, y, x], self.total)

        def wide_one():
            self.settle()
            spread(one, lambda t: t.at[:, :, x] if plain else t.at[:, y], self.total)

        return [start, pair_add, add_one, add_two, add_three, wide_two, wide_one, self.settle]


def route_buffers(dims, rows, width, dtype, first):
    nz, ny, nx = dims
    na, nb = (nx, ny) if first == "x" else (ny, nx)
    tail = (rows, width)
    shapes = [(max(na - 1, 1), nz, nb) + tail, (max(nb - 1, 1), nz) + tail, (max(nz - 1, 1),) + tail]
    copies = 3 + 2 * (na + nb + nz - 3)
    return [pltpu.VMEM(s, dtype) for s in shapes] + [pltpu.SemaphoreType.DMA((2, copies))]


PAIRS = D // 128
BLOCK = 256


def greet(dims, place):
    z, y, x, side, index = place
    barrier = pltpu.get_barrier_semaphore()
    peers = [(index, 1 - side)]
    for axis in range(3):
        for s in range(1, dims[axis]):
            at = [z, y, x]
            at[axis] = lax.rem(at[axis] + s, dims[axis])
            peers.append(((at[0] * dims[1] + at[1]) * dims[2] + at[2], side))
    for peer in peers:
        pl.semaphore_signal(barrier, inc=1, device_id=peer, device_id_type=pl.DeviceIdType.MESH)
    pl.semaphore_wait(barrier, len(peers))


def place_of(dims):
    index, side = lax.axis_index("dp"), lax.axis_index("tensor")
    _, ny, nx = dims
    return (index // (ny * nx), lax.rem(index // nx, ny), lax.rem(index, nx), side, index)


def columns(ref, start, width):
    return ref.at[..., start : start + width]


STRIPS = 4
FIRST_PAIR = STRIPS + 1
QKV_STEP = FIRST_PAIR + PAIRS
TAIL_SLOTS = (0, 0, 4, 6, 8, 10, 12, 13)


def tail_kernel(dims, table, late, schedule, count, *refs):
    (
        prefix_ref, q_ref, k_ref, v_ref, o_ref, g_ref, lse_ref, n1t_ref, w_ref, x_ref, gm_ref, gain_ref, svec_ref, swide_ref,
        gh_ref, n2t_ref, n3t_ref, gml_ref, down_ref, ig_ref, odown_ref, oup_ref, oqkv_ref, oout_ref, osmall_ref,
        gproj, gqkv, gup, gout, bias, sums, small, mdown, pdown, pup, pout, pqkv, psmall,
    ) = refs[:38]
    scratch = refs[38:]
    pid = pl.program_id(0)
    _, ny, nx = dims
    place = place_of(dims)

    @pl.when(pid == 0)
    def _():
        greet(dims, place)
        sums[...] = jnp.zeros_like(sums)

    homes = {
        "up": (gup, pup, oup_ref),
        "qkv": (gqkv, pqkv, oqkv_ref),
        "out": (gout, pout, oout_ref),
        "small": (small, psmall, osmall_ref),
    }
    plans = []
    for n, (name, lead, start, width, first) in enumerate(table):
        bufs = scratch[4 * n : 4 * n + 4]
        cut = lambda r, at=start, width=width: columns(r, at, width)
        if name == "down":
            views = [down_ref.at[0, lead], down_ref.at[1, lead], mdown.at[lead], pdown.at[lead], odown_ref.at[lead]]
            views = [lambda v=v, cut=cut: cut(v) for v in views]
        else:
            src, pair, total = homes[name]
            near = lambda s=src, cut=cut: cut(s)
            far = lambda s=src, at=start + lead, width=width: columns(s, at, width)
            if name in ("out", "small"):
                near, far = [lambda s=src, i=i, cut=cut: cut(s.at[i]) for i in (0, 1)]
            done = lambda t=total, cut=cut: cut(t)
            if name == "qkv":
                third = D // 2
                done = lambda t=total, at=start, width=width: columns(t.at[at // third], at % third, width)
            views = [None, far, near, lambda p=pair, cut=cut: cut(p), done]
        plans.append(Route(dims, first, *views, [(lambda b=b: b) for b in bufs[:3]], bufs[3]).steps(place))

    def advance(step):
        for n, k in schedule.get(step, ()):
            plans[n][k]()

    for step in range(count):
        if schedule.get(step):
            pl.when(pid == step)(functools.partial(advance, step))

    @pl.when(pid < STRIPS)
    def _():
        width = gh_ref.shape[1]
        at = pl.ds(pl.multiple_of(pid * width, width), width)
        gup[:, :, :, :, at] = nn(n3t_ref[...], gh_ref[...]).astype(BF16).reshape(gup.shape[:4] + (width,))

    @pl.when(pid == STRIPS)
    def _():
        gout[...] = nn(n2t_ref[...], gml_ref[...]).reshape(gout.shape).astype(BF16)

    @pl.when((pid >= FIRST_PAIR) & (pid < QKV_STEP))
    def _():
        i = pid - FIRST_PAIR
        column = lambda c: gproj.at[:, pl.ds(pl.multiple_of(head_block(i, c) * 128, 128), 128)]
        attn_bwd_kernel(
            prefix_ref, q_ref, k_ref, v_ref, o_ref, g_ref, lse_ref, column(0), column(1), column(2),
            bias.at[:, pl.ds(pl.multiple_of(i * 128, 128), 128)],
        )

    @pl.when(pid == QKV_STEP)
    def _():
        def body(c, _):
            at = pl.ds(pl.multiple_of(c * D, 128), D)
            part = nn(n1t_ref[...], gproj[:, at]).astype(BF16)
            gqkv[:, :, :, :, at] = part.reshape(gqkv.shape[:4] + (D,))
            return 0

        lax.fori_loop(0, 3, body, 0)

    @pl.when(pid > QKV_STEP)
    def _():
        rows = pl.ds(pl.multiple_of((pid - QKV_STEP - 1) * BLOCK, BLOCK), BLOCK)
        e = nt(gproj[rows, :], w_ref[...])
        xhat, inv = normed(x_ref[...].astype(F32))
        sums[0] += colsum(e * xhat)
        sums[1] += colsum(e)
        ig_ref[...] = gm_ref[...] + normed_back(e * gain_ref[...].reshape(1, D), xhat, inv)

    @pl.when(pid == count - 1)
    def _():
        small[...] = jnp.zeros_like(small)
        split = [bias[i : i + 1, :] for i in range(2)]
        split += [jnp.sum(svec_ref[i], axis=0, keepdims=True) for i in range(2)]
        split += [jnp.sum(swide_ref[i], axis=0, keepdims=True) for i in range(3)]
        shared = [jnp.sum(sums[i], axis=0, keepdims=True) for i in range(2)]
        shared += [jnp.sum(svec_ref[i], axis=0, keepdims=True) for i in range(2, 6)]
        for s in range(2):
            at = 0
            for v in [v[:, s * (v.shape[1] // 2) : (s + 1) * (v.shape[1] // 2)] for v in split] + shared:
                for c in range(v.shape[1] // 128):
                    p = at // 8
                    small[s, p // (ny * nx), p // nx % ny, p % nx, at % 8 : at % 8 + 1, :] = v[:, c * 128 : (c + 1) * 128]
                    at += 1
        for n, k in late:
            plans[n][k]()


def tail_stage(dims, prefix, qkv, attended, ga, lse, n1t, wqkv, tokens, gm, pre_gain, svec, swide, gh, n2t, n3t, gml, g_down):
    nz, ny, nx = dims
    parts = nz * ny * nx
    length = qkv.shape[0]
    ff = gh.shape[1] // 2
    half, third = ff // 2, D // 2
    rows = D // parts
    wide = 3 * D // 2
    small_rows = 8
    down = g_down.reshape(2, 2, nz, ny, nx, rows, D)
    table = []
    for a in (0, D // 2):
        table += [("down", 0, a, D // 2, "x"), ("down", 1, a, D // 2, "y")]
    for a in (0, half // 2):
        table += [("up", ff, a, half // 2, "x"), ("up", ff, half + a, half // 2, "y")]
    table += [("out", 0, 0, third, "x"), ("out", 0, third, third, "y")]
    table += [("qkv", wide, 0, third, "x"), ("qkv", wide, 2 * third, third, "y")]
    table += [("qkv", wide, third, 256, "x"), ("qkv", wide, third + 256, 128, "y")]
    table += [("small", 0, 0, 128, "x")]
    groups = [((0, 1), 0), ((2, 3), 1), ((4, 5), 2), ((6, 7), 3), ((8, 9), 4), ((10, 11), 6), ((12, 13), 7), ((14,), 8)]
    depth = 8
    count = QKV_STEP + 1 + length // BLOCK
    schedule, late = {}, []
    for slot in range(groups[-1][1] + depth):
        for members, enter in groups:
            k = slot - enter
            if 0 <= k < depth:
                where = schedule.setdefault(TAIL_SLOTS[slot], []) if slot < len(TAIL_SLOTS) else late
                where.extend((n, k) for n in members)
    sds = jax.ShapeDtypeStruct
    box = (nz, ny, nx)
    shapes = {
        "down": (2, *box, rows, D), "up": (*box, rows, ff), "qkv": (*box, rows, wide), "out": (*box, rows // 2, D),
        "small": (*box, small_rows, 128),
    }
    kinds = {n: F32 if n == "small" else BF16 for n in shapes}
    landed = dict(shapes, qkv=(3, *box, rows, third))
    scratch = [
        pltpu.VMEM((length, 3 * D), BF16), pltpu.VMEM((*box, rows, 3 * D), BF16), pltpu.VMEM((*box, rows, 2 * ff), BF16),
        pltpu.VMEM((2, *box, rows // 2, D), BF16), pltpu.VMEM((8, D), F32), pltpu.VMEM((2, 8, D), F32),
        pltpu.VMEM((2, *box, small_rows, 128), F32), pltpu.VMEM(shapes["down"], BF16),
    ]
    scratch += [pltpu.VMEM(shapes[n], kinds[n]) for n in ("down", "up", "out", "qkv", "small")]
    heights = {"down": rows, "up": rows, "qkv": rows, "out": rows // 2, "small": small_rows}
    for name, _, _, width, first in table:
        scratch += route_buffers(dims, heights[name], width, kinds[name], first)
    pair_at = lambda i: jnp.clip(i - FIRST_PAIR, 0, PAIRS - 1)
    block_at = lambda i: jnp.maximum(i - QKV_STEP - 1, 0)
    col = lambda c: pl.BlockSpec((length, 128), lambda i, c=c: (0, head_block(pair_at(i), c)))
    one = pl.BlockSpec((length, 128), lambda i: (0, pair_at(i)))
    block = pl.BlockSpec((BLOCK, D), lambda i: (block_at(i), 0))
    strip = pl.BlockSpec((length, 2 * ff // STRIPS), lambda i: (0, jnp.minimum(i, STRIPS - 1)))
    whole = lambda v: pl.BlockSpec(v.shape, lambda i, n=v.ndim: (0,) * n, pipeline_mode=pl.Buffered(1))
    hbm = pl.BlockSpec(memory_space=pl.ANY)
    return pl.pallas_call(
        functools.partial(tail_kernel, dims, table, late, schedule, count),
        grid=(count,),
        in_specs=[
            pl.BlockSpec(memory_space=pltpu.SMEM), col(0), col(1), col(2), one, one,
            pl.BlockSpec((1, 8, length), lambda i: (pair_at(i), 0, 0)), whole(n1t), whole(wqkv), block, block, whole(pre_gain),
            whole(svec), whole(swide), strip, whole(n2t), whole(n3t), whole(gml), hbm,
        ],
        out_specs=[block] + [hbm] * 5,
        out_shape=[sds((length, D), F32)] + [sds(landed[n], kinds[n]) for n in ("down", "up", "qkv", "out", "small")],
        scratch_shapes=scratch,
        compiler_params=pltpu.CompilerParams(collective_id=1, has_side_effects=True, vmem_limit_bytes=VMEM),
        name="tail_stage",
    )(
        prefix, qkv, qkv, qkv, attended, ga, lse, n1t, wqkv, tokens, gm, pre_gain, svec, swide, gh, n2t, n3t, gml, down,
    )


def unpack_kernel(ig_ref, down_ref, up_ref, qkv_ref, out_ref, small_ref, oig, odown, oup, oqkv, oout, *vectors):
    oig[...] = ig_ref[...]
    odown[...] = down_ref[...].astype(F32)
    oup[...] = up_ref[...].astype(F32)
    oqkv[...] = qkv_ref[...].astype(F32)
    oout[...] = out_ref[...].astype(F32).reshape(oout.shape)

    @pl.when(pl.program_id(0) == 0)
    def _():
        at = 0
        for ref in vectors:
            for row in range(ref.shape[0] if ref.ndim == 2 else 1):
                for c in range(ref.shape[-1] // 128):
                    lanes = pl.ds(c * 128, 128)
                    if ref.ndim == 2:
                        ref[row, lanes] = small_ref[at, :]
                    else:
                        ref[lanes] = small_ref[at, :]
                    at += 1


def unpack(input_grad, down, up, qkv, out, small, ff):
    steps = 8
    half = D // 2
    down, up, qkv = down.reshape(ff, D), up.reshape(D, ff), qkv.reshape(3 * D, half)
    out = out.reshape((-1,) + out.shape[-2:])
    small = small.reshape(-1, 128)
    block = lambda v: pl.BlockSpec((v.shape[0] // steps,) + v.shape[1:], lambda i, n=v.ndim: (i,) + (0,) * (n - 1))
    whole = lambda s: pl.BlockSpec(s, lambda i: (0,) * len(s), pipeline_mode=pl.Buffered(1))
    sds = lambda s: jax.ShapeDtypeStruct(s, F32)
    vectors = [(2, half), (half,), (half,), (ff,), (ff,), (ff,)] + [(D,)] * 6
    shapes = [input_grad.shape, (ff, D), (D, ff), (3 * D, half), (half, D)]
    return pl.pallas_call(
        unpack_kernel,
        grid=(steps,),
        in_specs=[block(v) for v in (input_grad, down, up, qkv, out)] + [whole(small.shape)],
        out_specs=[block(sds(s)) for s in shapes] + [whole(s) for s in vectors],
        out_shape=[sds(s) for s in shapes + vectors],
        compiler_params=pltpu.CompilerParams(vmem_limit_bytes=VMEM),
        name="unpack",
    )(input_grad, down, up, qkv, out, small)


def head_kernel(
    x_ref, gain_ref, bias_ref, w_ref, wo_ref, sub_gain, sub_bias, up_bias, inner_gain, inner_bias, qv_ref,
    out_bias, ffn_gain, ffn_bias, down_bias,
    qkv_ref, n1t_ref, wall_ref, far_wo, vec_ref, wide_ref,
    near_sem, send_sem, recv_sem, norm_ref, far_sg, far_sb, far_ub, far_ig, far_ib, far_qv,
):
    index, side = lax.axis_index("dp"), lax.axis_index("tensor")
    other = (index, 1 - side)
    mesh_id = pl.DeviceIdType.MESH
    barrier = pltpu.get_barrier_semaphore()
    pl.semaphore_signal(barrier, inc=1, device_id=other, device_id_type=mesh_id)
    half = D // 2
    wide = 3 * half
    here = [pltpu.make_async_copy(w_ref.at[c], wall_ref.at[:, c * half : (c + 1) * half], near_sem.at[c]) for c in range(3)]
    for copy in here:
        copy.start()
    pl.semaphore_wait(barrier, 1)
    away = [(w_ref.at[c], wall_ref.at[:, wide + c * half : wide + (c + 1) * half]) for c in range(3)]
    away += [(qv_ref, far_qv), (sub_gain, far_sg), (sub_bias, far_sb)]
    away += [(up_bias, far_ub), (inner_gain, far_ig), (inner_bias, far_ib), (wo_ref, far_wo)]
    away = [
        pltpu.make_async_remote_copy(
            src_ref=a, dst_ref=b, send_sem=send_sem.at[i], recv_sem=recv_sem.at[i], device_id=other, device_id_type=mesh_id
        )
        for i, (a, b) in enumerate(away)
    ]
    for copy in away:
        copy.start()
    length = x_ref.shape[0]
    block = 256
    line = lambda ref: ref[...].reshape(1, -1)
    gain, bias = line(gain_ref), line(bias_ref)

    def norm(i, _):
        rows = pl.ds(pl.multiple_of(i * block, block), block)
        xhat, _ = normed(x_ref[rows, :].astype(F32))
        n1 = (xhat * gain + bias).astype(BF16)
        norm_ref[rows, :] = n1
        n1t_ref[:, rows] = n1.T
        return 0

    lax.fori_loop(0, length // block, norm, 0)

    def product(first, biases):
        weight = wall_ref[:, first : first + wide]
        bias = jnp.concatenate([biases[0:1, :], jnp.zeros((1, half), F32), biases[1:2, :]], axis=1)

        def rows(i, _):
            at = pl.ds(pl.multiple_of(i * block, block), block)
            qkv_ref[at, first : first + wide] = (nn(norm_ref[at, :], weight) + bias).astype(BF16)
            return 0

        lax.fori_loop(0, length // block, rows, 0)

    for copy in here:
        copy.wait()
    product(0, qv_ref[...])
    for copy in away:
        copy.wait()
    product(wide, far_qv[...])
    both = lambda near, far: jnp.concatenate([line(near), line(far)], axis=1)
    vec_ref[0:1, :] = both(sub_gain, far_sg)
    vec_ref[1:2, :] = both(sub_bias, far_sb)
    for i, v in enumerate((out_bias, ffn_gain, ffn_bias, down_bias)):
        vec_ref[i + 2 : i + 3, :] = line(v)
    for i, (near, far) in enumerate(((up_bias, far_ub), (inner_gain, far_ig), (inner_bias, far_ib))):
        wide_ref[i : i + 1, :] = both(near, far)


def head_stage(tokens, pre_gain, pre_bias, w3, wo, sub_gain, sub_bias, up_bias, inner_gain, inner_bias, qv_bias, *rest):
    length = tokens.shape[0]
    ff_half = up_bias.shape[0]
    half = D // 2
    sds = jax.ShapeDtypeStruct
    vmem, hbm = pl.BlockSpec(memory_space=pltpu.VMEM), pl.BlockSpec(memory_space=pl.ANY)
    return pl.pallas_call(
        head_kernel,
        in_specs=[vmem] * 3 + [hbm] * 2 + [vmem] * 10,
        out_specs=[vmem] * 3 + [hbm] + [vmem] * 2,
        out_shape=[
            sds((length, 3 * D), BF16), sds((D, length), BF16), sds((D, 3 * D), BF16), sds(wo.shape, BF16),
            sds((6, D), F32), sds((3, 2 * ff_half), F32),
        ],
        scratch_shapes=[
            pltpu.SemaphoreType.DMA((3,)), pltpu.SemaphoreType.DMA((10,)), pltpu.SemaphoreType.DMA((10,)),
            pltpu.VMEM((length, D), BF16), *[pltpu.VMEM((half,), F32)] * 2,
            *[pltpu.VMEM((ff_half,), F32)] * 3, pltpu.VMEM((2, half), F32),
        ],
        compiler_params=pltpu.CompilerParams(collective_id=2, has_side_effects=True, vmem_limit_bytes=VMEM),
        name="head_stage",
    )(tokens, pre_gain, pre_bias, w3, wo, sub_gain, sub_bias, up_bias, inner_gain, inner_bias, qv_bias, *rest)


def pack_small(dims, g_qv, g_vec, g_wide, g_pre):
    half, ff_half = D // 2, g_wide.shape[1] // 2
    shared = jnp.concatenate([g_pre.reshape(-1), g_vec[2:].reshape(-1)])
    rows = -(-(4 * half + 3 * ff_half + 6 * D) // (128 * 8 * math.prod(dims))) * 8
    pad = jnp.zeros((rows * 128 * math.prod(dims) - (4 * half + 3 * ff_half + 6 * D),), F32)
    pack = lambda i: jnp.concatenate(
        [v[j, i * n : (i + 1) * n] for v, m, n in ((g_qv, 2, half), (g_vec, 2, half), (g_wide, 3, ff_half)) for j in range(m)] + [shared, pad]
    )
    return jnp.stack([pack(0), pack(1)]).reshape((2,) + dims + (rows, 128))


def body(
    dims, tokens, grad_out, prefix, pre_gain, pre_bias, qkv_weight, qv_bias, sub_gain, sub_bias, out_weight, out_bias,
    ffn_gain, ffn_bias, up_weight, up_bias, inner_gain, inner_bias, down_weight, down_bias,
):
    half, ff_half = D // 2, up_bias.shape[0]
    qkv, n1t, wqkv, wo_far, vecs, wides = head_stage(
        tokens, pre_gain, pre_bias, qkv_weight.transpose(1, 0, 2), out_weight, sub_gain, sub_bias, up_bias, inner_gain, inner_bias,
        qv_bias, out_bias, ffn_gain, ffn_bias, down_bias,
    )
    attended, lse, wu_far, wd_far = attn_fwd(prefix, qkv, up_weight, down_weight)
    wo, wu, wd = (out_weight, wo_far), (up_weight, wu_far), (down_weight, wd_far)
    out, n2t, n3t, n4, gh, gm, gml, ga, svec, swide = middle_stage(tokens, attended, grad_out, vecs, wides, wo, wu, wd)
    g_down = tn(n4, grad_out).astype(BF16)
    if D // math.prod(dims) % 16 == 0:
        sums = tail_stage(
            dims, prefix, qkv, attended, ga, lse, n1t, wqkv, tokens, gm, pre_gain, svec, swide, gh, n2t, n3t, gml, g_down
        )
        input_grad, g_down, g_up, g_qkv, g_out, *vectors = unpack(*sums, ff_half)
        g_qv, g_sub_gain, g_sub_bias, g_up_bias, g_inner_gain, g_inner_bias = vectors[:6]
        g_pre_gain, g_pre_bias, g_out_bias, g_ffn_gain, g_ffn_bias, g_down_bias = vectors[6:]
        g_qkv = g_qkv.reshape(3, D, half)
    else:
        g_up, g_out = nn(n3t, gh).astype(BF16), nn(n2t, gml).astype(BF16)
        input_grad, g_pre, g_qkv, g_qv = back(prefix, tokens, pre_gain, wqkv, n1t.T, qkv, attended, lse, gm, ga)
        small = pack_small(dims, g_qv, jnp.sum(svec, 1), jnp.sum(swide, 1), g_pre)
        g_down, g_up, g_qkv, g_out, small = all_reduce(dims, (g_down, g_up, g_qkv, g_out), small)
        g_qkv = g_qkv.reshape(D, 3, half).transpose(1, 0, 2)
        g_qv = small[: 2 * half].reshape(2, half)
        g_sub_gain, g_sub_bias = [small[i * half : (i + 1) * half] for i in (2, 3)]
        g_up_bias, g_inner_gain, g_inner_bias = [small[4 * half + i * ff_half : 4 * half + (i + 1) * ff_half] for i in range(3)]
        base = 4 * half + 3 * ff_half
        g_pre_gain, g_pre_bias, g_out_bias, g_ffn_gain, g_ffn_bias, g_down_bias = [
            small[base + i * D : base + (i + 1) * D] for i in range(6)
        ]
    return (
        out, input_grad, g_pre_gain, g_pre_bias, g_qkv.transpose(1, 0, 2), g_qv, g_sub_gain, g_sub_bias, g_out, g_out_bias,
        g_ffn_gain, g_ffn_bias, g_up, g_up_bias, g_inner_gain, g_inner_bias, g_down, g_down_bias,
    )


def solution(mesh):
    rows = P(("dp", "tensor"), None)
    wide, tall, vec, whole = P(None, "tensor"), P("tensor", None), P("tensor"), P()
    cube = P(None, None, "tensor")
    return jax.shard_map(
        functools.partial(body, grid_of(mesh.shape["dp"])),
        mesh=mesh,
        in_specs=(
            rows, rows, P("dp"), whole, whole, cube, wide, vec, vec, tall, whole, whole, whole, wide, vec, vec, vec, tall, whole,
        ),
        out_specs=(
            rows, rows, whole, whole, cube, wide, vec, vec, tall, whole, whole, whole, wide, vec, vec, vec, tall, whole,
        ),
        check_vma=False,
    )
```

```python
import functools
import math

import jax
import jax.numpy as jnp
from jax import lax
from jax.sharding import PartitionSpec as P
from jax.experimental import pallas as pl
from jax.experimental.pallas import tpu as pltpu

D = 768
HEAD_DIM = 64
PREFIX_MAX = 512
EPS = 1e-05
F32 = jnp.float32
BF16 = jnp.bfloat16
QB = 512
VMEM = 67043328


def nn(a, b):
    return lax.dot_general(a, b, (((1,), (0,)), ((), ())), preferred_element_type=F32)


def nt(a, b):
    return lax.dot_general(a, b, (((1,), (1,)), ((), ())), preferred_element_type=F32)


def tn(a, b):
    return lax.dot_general(a, b, (((0,), (0,)), ((), ())), preferred_element_type=F32)


def halves(v):
    left = lax.broadcasted_iota(jnp.int32, v.shape, 1) < HEAD_DIM
    zero = jnp.zeros_like(v)
    return jnp.where(left, v, zero), jnp.where(left, zero, v)


def spans(start, length, block):
    last = min(length, max(start + block, PREFIX_MAX))
    out = []
    if start:
        out.append((0, start, False))
    out.append((start, last, True))
    return out


def masked(scores, key_start, query_start, prefix):
    key_pos = key_start + lax.broadcasted_iota(jnp.int32, scores.shape, 0)
    query_pos = query_start + lax.broadcasted_iota(jnp.int32, scores.shape, 1)
    seen = key_pos <= query_pos
    if key_start < PREFIX_MAX:
        seen = seen | (key_pos < prefix)
    return jnp.where(seen, scores, -1e30)


def head_block(i, c):
    each = D // 256
    return i // each * 3 * each + c * each + lax.rem(i, each)


def attn_fwd_kernel(prefix_ref, q_ref, k_ref, v_ref, wu_ref, wd_ref, o_ref, lse_ref, far_wu, far_wd, send_sem, recv_sem):
    pid = pl.program_id(0)
    other = (lax.axis_index("dp"), 1 - lax.axis_index("tensor"))

    def exchange(i, src, dst):
        return pltpu.make_async_remote_copy(
            src_ref=src, dst_ref=dst, send_sem=send_sem.at[i], recv_sem=recv_sem.at[i], device_id=other,
            device_id_type=pl.DeviceIdType.MESH,
        )

    @pl.when(pid == 0)
    def _():
        barrier = pltpu.get_barrier_semaphore()
        pl.semaphore_signal(barrier, inc=1, device_id=other, device_id_type=pl.DeviceIdType.MESH)
        pl.semaphore_wait(barrier, 1)
        exchange(0, wu_ref, far_wu).start()
        exchange(1, wd_ref, far_wd).start()

    length = q_ref.shape[0]
    prefix = prefix_ref[lax.axis_index("tensor")]
    keys = halves(k_ref[...])
    value_t = v_ref[...].T
    for start in range(0, length, QB):
        query = q_ref[start : start + QB, :] * jnp.asarray(HEAD_DIM**-0.5, BF16)
        parts = []
        for head in range(2):
            scores = []
            for first, last, mask in spans(start, length, QB):
                s = nt(keys[head][first:last], query)
                scores.append(masked(s, first, start, prefix) if mask else s)
            peak = functools.reduce(jnp.maximum, [jnp.max(s, axis=0, keepdims=True) for s in scores])
            total = jnp.zeros_like(peak)
            mixed = jnp.zeros((HEAD_DIM, QB), F32)
            rows = slice(head * HEAD_DIM, (head + 1) * HEAD_DIM)
            for s, (first, last, _) in zip(scores, spans(start, length, QB)):
                w = jnp.exp(s - peak)
                total = total + jnp.sum(w, axis=0, keepdims=True)
                mixed = mixed + nn(value_t[rows, first:last], w.astype(BF16))
            parts.append(mixed / total)
            lse_ref[0, head : head + 1, start : start + QB] = peak + jnp.log(total)
        o_ref[start : start + QB, :] = jnp.concatenate(parts, axis=0).T

    @pl.when(pid == pl.num_programs(0) - 1)
    def _():
        exchange(0, wu_ref, far_wu).wait()
        exchange(1, wd_ref, far_wd).wait()


def attn_fwd(prefix, qkv, wu, wd):
    length = qkv.shape[0]
    pairs = D // 128
    col = lambda c: pl.BlockSpec((length, 128), lambda i, c=c: (0, head_block(i, c)))
    hbm = pl.BlockSpec(memory_space=pl.ANY)
    return pl.pallas_call(
        attn_fwd_kernel,
        grid=(pairs,),
        in_specs=[pl.BlockSpec(memory_space=pltpu.SMEM), col(0), col(1), col(2), hbm, hbm],
        out_specs=[
            pl.BlockSpec((length, 128), lambda i: (0, i)),
            pl.BlockSpec((1, 8, length), lambda i: (i, 0, 0)),
            hbm,
            hbm,
        ],
        out_shape=[
            jax.ShapeDtypeStruct((length, D), F32),
            jax.ShapeDtypeStruct((pairs, 8, length), F32),
            jax.ShapeDtypeStruct(wu.shape, BF16),
            jax.ShapeDtypeStruct(wd.shape, BF16),
        ],
        scratch_shapes=[pltpu.SemaphoreType.DMA((2,))] * 2,
        compiler_params=pltpu.CompilerParams(collective_id=4, has_side_effects=True, vmem_limit_bytes=VMEM),
        name="attn_fwd",
    )(prefix, qkv, qkv, qkv, wu, wd)


def attn_bwd_kernel(prefix_ref, q_ref, k_ref, v_ref, o_ref, g_ref, lse_ref, dq_ref, dk_ref, dv_ref, bias_ref):
    length = q_ref.shape[0]
    prefix = prefix_ref[lax.axis_index("tensor")]
    scale = HEAD_DIM**-0.5
    keys = halves(k_ref[...])
    values = halves(v_ref[...])
    key_t = k_ref[...].T
    delta_t = (o_ref[...] * g_ref[...].astype(F32)).T
    dk = [jnp.zeros((b - a, 128), F32) for a, b in zip(range(0, length, QB), range(QB, length + 1, QB))]
    dv = list(dk)
    qsum = jnp.zeros((8, 128), F32)
    for start in range(0, length, QB):
        cols = slice(start, start + QB)
        query = q_ref[cols, :] * jnp.asarray(scale, BF16)
        query_half = halves(query)
        grad = g_ref[cols, :]
        grad_half = halves(grad)
        parts = []
        for head in range(2):
            rows = slice(head * HEAD_DIM, (head + 1) * HEAD_DIM)
            lse = lse_ref[0, head : head + 1, cols]
            delta = jnp.sum(delta_t[rows, cols], axis=0, keepdims=True)
            dq = jnp.zeros((HEAD_DIM, QB), F32)
            for first in range(0, length, QB):
                live = [s for s in spans(start, length, QB) if s[0] <= first < s[1]]
                if not live:
                    continue
                last = first + QB
                s = nt(keys[head][first:last], query)
                if live[0][2]:
                    s = masked(s, first, start, prefix)
                w = jnp.exp(s - lse)
                dp = nt(values[head][first:last], grad)
                ds = (w * (dp - delta)).astype(BF16)
                b = first // QB
                dv[b] = dv[b] + nn(w.astype(BF16), grad_half[head])
                dk[b] = dk[b] + nn(ds, query_half[head])
                dq = dq + nn(key_t[rows, first:last], ds)
            parts.append(dq)
        dq = jnp.concatenate(parts, axis=0).T * scale
        qsum = qsum + jnp.sum(dq.reshape(QB // 8, 8, 128), axis=0)
        dq_ref[cols, :] = dq.astype(BF16)
    vsum = jnp.zeros((8, 128), F32)
    for b in range(length // QB):
        cols = slice(b * QB, (b + 1) * QB)
        dk_ref[cols, :] = dk[b].astype(BF16)
        dv_ref[cols, :] = dv[b].astype(BF16)
        vsum = vsum + jnp.sum(dv[b].reshape(QB // 8, 8, 128), axis=0)
    bias_ref[0:1, :] = jnp.sum(qsum, axis=0, keepdims=True)
    bias_ref[1:2, :] = jnp.sum(vsum, axis=0, keepdims=True)


def attn_bwd(prefix, qkv, attended, grad_attended, lse):
    length = qkv.shape[0]
    pairs = D // 128
    col = lambda c: pl.BlockSpec((length, 128), lambda i, c=c: (0, head_block(i, c)))
    one = pl.BlockSpec((length, 128), lambda i: (0, i))
    return pl.pallas_call(
        attn_bwd_kernel,
        grid=(pairs,),
        in_specs=[
            pl.BlockSpec(memory_space=pltpu.SMEM), col(0), col(1), col(2), one, one,
            pl.BlockSpec((1, 8, length), lambda i: (i, 0, 0)),
        ],
        out_specs=[one, one, one, pl.BlockSpec((8, 128), lambda i: (0, i))],
        out_shape=[jax.ShapeDtypeStruct((length, D), BF16)] * 3 + [jax.ShapeDtypeStruct((8, D), F32)],
        name="attn_bwd",
    )(prefix, qkv, qkv, qkv, attended, grad_attended, lse)


def normed(v):
    centre = v - jnp.mean(v, axis=-1, keepdims=True)
    inv = lax.rsqrt(jnp.mean(centre * centre, axis=-1, keepdims=True) + EPS)
    return centre * inv, inv


def normed_back(e, xhat, inv):
    return inv * (e - jnp.mean(e, axis=-1, keepdims=True) - xhat * jnp.mean(e * xhat, axis=-1, keepdims=True))


def colsum(v):
    rows, cols = v.shape
    return jnp.sum(v.reshape(rows // 8, 8, cols), axis=0)


def mid_kernel(
    x_ref, att_ref, g_ref, vec_ref, wide_ref, near_wo, far_wo, near_wu, far_wu, near_wd, far_wd,
    out_ref, n2_ref, n3_ref, n4_ref, gh_ref, gm_ref, gml_ref, ga_ref, svec_ref, swide_ref,
    act_ref, slope_ref, wo_ref, wu_ref, wd_ref, sem,
):
    first = pl.program_id(0) == 0
    half, ff_half = near_wo.shape[0], near_wu.shape[1]
    moves = (
        (near_wo, wo_ref.at[:half]), (far_wo, wo_ref.at[half:]), (near_wu, wu_ref.at[:, :ff_half]), (far_wu, wu_ref.at[:, ff_half:]),
        (near_wd, wd_ref.at[:ff_half]), (far_wd, wd_ref.at[ff_half:]),
    )
    moves = [pltpu.make_async_copy(a, b, sem.at[i]) for i, (a, b) in enumerate(moves)]

    def arrive(some):
        @pl.when(first)
        def _():
            for copy in some:
                copy.wait()

    @pl.when(first)
    def _():
        for copy in moves:
            copy.start()
        svec_ref[...] = jnp.zeros_like(svec_ref)
        swide_ref[...] = jnp.zeros_like(swide_ref)

    sub_gain, sub_bias, out_bias, ffn_gain, ffn_bias, down_bias = [vec_ref[i : i + 1, :] for i in range(6)]
    up_bias, inner_gain, inner_bias = [wide_ref[i : i + 1, :] for i in range(3)]
    xhat2, inv2 = normed(att_ref[...])
    n2 = (xhat2 * sub_gain + sub_bias).astype(BF16)
    n2_ref[...] = n2.T
    arrive(moves[:2])
    middle = x_ref[...].astype(F32) + nn(n2, wo_ref[...]) + out_bias
    xhat3, inv3 = normed(middle)
    n3 = (xhat3 * ffn_gain + ffn_bias).astype(BF16)
    n3_ref[...] = n3.T
    arrive(moves[2:4])
    hidden = nn(n3, wu_ref[...]) + up_bias
    half = 0.5 + 0.5 * lax.erf(hidden * (2.0**-0.5))
    act_ref[...] = hidden * half
    slope_ref[...] = half + hidden * (jnp.exp(-0.5 * hidden * hidden) * 0.3989422804014327)
    xhat4, inv4 = normed(act_ref[...])
    n4 = (xhat4 * inner_gain + inner_bias).astype(BF16)
    n4_ref[...] = n4
    act_ref[...] = xhat4
    arrive(moves[4:])
    out_ref[...] = (middle + nn(n4, wd_ref[...]) + down_bias).astype(BF16)
    g = g_ref[...]
    e = nt(g, wd_ref[...])
    xhat4 = act_ref[...]
    swide_ref[1] += colsum(e * xhat4)
    swide_ref[2] += colsum(e)
    gh = normed_back(e * inner_gain, xhat4, inv4) * slope_ref[...]
    swide_ref[0] += colsum(gh)
    ghl = gh.astype(BF16)
    gh_ref[...] = ghl
    gf = g.astype(F32)
    e = nt(ghl, wu_ref[...])
    svec_ref[3] += colsum(e * xhat3)
    svec_ref[4] += colsum(e)
    gm = gf + normed_back(e * ffn_gain, xhat3, inv3)
    svec_ref[2] += colsum(gm)
    svec_ref[5] += colsum(gf)
    gm_ref[...] = gm
    gml = gm.astype(BF16)
    gml_ref[...] = gml
    e = nt(gml, wo_ref[...])
    svec_ref[0] += colsum(e * xhat2)
    svec_ref[1] += colsum(e)
    ga_ref[...] = normed_back(e * sub_gain, xhat2, inv2).astype(BF16)


def middle_stage(x, att, g, vecs, wides, wo, wu, wd, block=256):
    rows = x.shape[0]
    ff = 2 * wu[0].shape[1]
    row = lambda n: pl.BlockSpec((block, n), lambda i: (i, 0))
    turned = pl.BlockSpec((D, block), lambda i: (0, i))
    whole = lambda s: pl.BlockSpec(s, lambda i: (0,) * len(s), pipeline_mode=pl.Buffered(1))
    sds = jax.ShapeDtypeStruct
    return pl.pallas_call(
        mid_kernel,
        grid=(rows // block,),
        in_specs=[row(D), row(D), row(D), whole(vecs.shape), whole(wides.shape)] + [pl.BlockSpec(memory_space=pl.ANY)] * 6,
        out_specs=[row(D), turned, turned, row(ff), row(ff), row(D), row(D), row(D), whole((6, 8, D)), whole((3, 8, ff))],
        out_shape=[
            sds((rows, D), BF16), sds((D, rows), BF16), sds((D, rows), BF16), sds((rows, ff), BF16), sds((rows, ff), BF16),
            sds((rows, D), F32), sds((rows, D), BF16), sds((rows, D), BF16), sds((6, 8, D), F32), sds((3, 8, ff), F32),
        ],
        scratch_shapes=[pltpu.VMEM((block, ff), F32), pltpu.VMEM((block, ff), F32), pltpu.VMEM((D, D), BF16), pltpu.VMEM((D, ff), BF16), pltpu.VMEM((ff, D), BF16), pltpu.SemaphoreType.DMA((6,))],
        compiler_params=pltpu.CompilerParams(vmem_limit_bytes=VMEM),
        name="middle_stage",
    )(x, att, g, vecs, wides, *wo, *wu, *wd)


def back(prefix, tokens, pre_gain, wqkv, n1, qkv, attended, lse, gm, ga):
    xhat1, inv1 = normed(tokens.astype(F32))
    dq, dk, dv, dbias = attn_bwd(prefix, qkv, attended, ga, lse)
    h = D // 2
    gproj = jnp.concatenate([v[:, s] for s in (slice(0, h), slice(h, D)) for v in (dq, dk, dv)], axis=1)
    g_qkv = tn(n1, gproj).astype(BF16)
    e = nt(gproj, wqkv)
    g_pre = jnp.stack([jnp.sum(e * xhat1, axis=0), jnp.sum(e, axis=0)])
    input_grad = gm + normed_back(e * pre_gain, xhat1, inv1)
    return input_grad, g_pre, g_qkv, dbias


def grid_of(count):
    side = 1
    while 2 * side**3 < count:
        side += 1
    return (2 * side, side, side) if 2 * side**3 == count else (count, 1, 1)


class Piece:
    def __init__(self, dims, first, near, far, total, bufs, sems, place):
        self.dims, self.first, self.near, self.far, self.total = dims, first, near, far, total
        self.mine, self.pair, self.land, self.part, self.land2, self.part2, self.land3 = bufs
        self.sems, self.place = sems, place
        self.count = 0
        self.flight = []

    def send(self, src, dst, where):
        copy = pltpu.make_async_remote_copy(
            src_ref=src, dst_ref=dst, send_sem=self.sems.at[0, self.count], recv_sem=self.sems.at[1, self.count],
            device_id=where, device_id_type=pl.DeviceIdType.MESH,
        )
        self.count += 1
        copy.start()
        self.flight.append(copy)

    def settle(self):
        for copy in self.flight:
            copy.wait()
        self.flight = []

    def device(self, axis, shift):
        at = list(self.place[:3])
        at[axis] = lax.rem(at[axis] + shift, self.dims[axis])
        nz, ny, nx = self.dims
        return at[axis], ((at[0] * ny + at[1]) * nx + at[2], self.place[3])

    def steps(self):
        z, y, x = self.place[:3]
        nz, ny, nx = self.dims
        one, two = (2, 1) if self.first == "x" else (1, 2)
        pick1 = lambda ref, p: ref.at[:, :, p] if one == 2 else ref.at[:, p]
        own1, own2 = (x, y) if one == 2 else (y, x)

        def start():
            local = pltpu.make_async_copy(self.near, self.mine, self.sems.at[0, self.count])
            self.count += 1
            local.start()
            self.send(self.far, self.pair, (self.place[4], 1 - self.place[3]))
            self.flight.append(local)

        def pair_add():
            self.settle()
            def one_row(i, _):
                self.mine[i] = (self.mine[i].astype(F32) + self.pair[i].astype(F32)).astype(self.mine.dtype)
                return 0
            lax.fori_loop(0, nz, one_row, 0)
            for s in range(1, self.dims[one]):
                p, dev = self.device(one, s)
                self.send(pick1(self.mine, p), self.land.at[s - 1], dev)

        def add_one():
            self.settle()
            def one_row(i, _):
                v = (self.mine[i, :, x] if one == 2 else self.mine[i, y]).astype(F32)
                for s in range(1, self.dims[one]):
                    v = v + self.land[s - 1, i].astype(F32)
                self.part[i] = v.astype(self.part.dtype)
                return 0
            lax.fori_loop(0, nz, one_row, 0)
            for s in range(1, self.dims[two]):
                p, dev = self.device(two, s)
                self.send(self.part.at[:, p], self.land2.at[s - 1], dev)

        def add_two():
            self.settle()
            def one_row(i, _):
                v = self.part[i, own2].astype(F32)
                for s in range(1, self.dims[two]):
                    v = v + self.land2[s - 1, i].astype(F32)
                self.part2[i] = v.astype(self.part2.dtype)
                return 0
            lax.fori_loop(0, nz, one_row, 0)
            for s in range(1, nz):
                p, dev = self.device(0, s)
                self.send(self.part2.at[p], self.land3.at[s - 1], dev)

        def add_three():
            self.settle()
            v = self.part2[z].astype(F32)
            for s in range(1, nz):
                v = v + self.land3[s - 1].astype(F32)
            self.total[z, y, x] = v.astype(self.total.dtype)
            spread(0, self.total.at[z, y, x])

        def spread(axis, ref):
            for s in range(1, self.dims[axis]):
                self.send(ref, ref, self.device(axis, s)[1])

        def wide_two():
            self.settle()
            spread(two, self.total.at[:, y, x])

        def wide_one():
            self.settle()
            spread(one, self.total.at[:, :, x] if one == 2 else self.total.at[:, y])

        return [start, pair_add, add_one, add_two, add_three, wide_two, wide_one, self.settle]


def buffers(dims, rows, width, dtype, first):
    nz, ny, nx = dims
    na, nb = (nx, ny) if first == "x" else (ny, nx)
    tail = (rows, width)
    shapes = [
        (nz, ny, nx) + tail, (nz, ny, nx) + tail, (max(na - 1, 1), nz, nb) + tail, (nz, nb) + tail,
        (max(nb - 1, 1), nz) + tail, (nz,) + tail, (max(nz - 1, 1),) + tail,
    ]
    copies = 2 + 2 * (na + nb + nz - 3)
    return [pltpu.VMEM(s, dtype) for s in shapes] + [pltpu.SemaphoreType.DMA((2, copies))]


def reduce_kernel(dims, views, firsts, *refs):
    count = len(firsts)
    sources = refs[: len(views)]
    totals = refs[len(views) : len(views) + count]
    scratch = refs[len(views) + count :]
    index, side = lax.axis_index("dp"), lax.axis_index("tensor")
    nz, ny, nx = dims
    place = (index // (ny * nx), lax.rem(index // nx, ny), lax.rem(index, nx), side, index)
    barrier = pltpu.get_barrier_semaphore()
    peers = [(index, 1 - side)]
    probe = Piece(dims, "x", None, None, None, [None] * 7, None, place)
    for axis in range(3):
        for s in range(1, dims[axis]):
            peers.append(probe.device(axis, s)[1])
    for peer in peers:
        pl.semaphore_signal(barrier, inc=1, device_id=peer, device_id_type=pl.DeviceIdType.MESH)
    pl.semaphore_wait(barrier, len(peers))
    plans = []
    at = 0
    for source, view in zip(sources, views):
        for near, far in view(source):
            plans.append(Piece(dims, firsts[at], near, far, totals[at], scratch[8 * at : 8 * at + 7], scratch[8 * at + 7], place).steps())
            at += 1
    slots = len(plans[0]) + (count + 1) // 2 - 1
    for slot in range(slots):
        for i, plan in enumerate(plans):
            if 0 <= slot - i // 2 < len(plan):
                plan[slot - i // 2]()


def all_reduce(dims, grads, small):
    g_down, g_up, g_qkv, g_out = grads
    nz, ny, nx = dims
    parts = nz * ny * nx
    ff = g_down.shape[0] // 2
    half = ff // 2
    rows_d, rows_u, rows_o = half // parts, D // parts, D // 2 // parts
    cut = 640
    down = g_down.reshape(2, 2, nz, ny, nx, rows_d, D)
    up = g_up.reshape(nz, ny, nx, rows_u, 2 * ff)
    qkv = g_qkv.reshape(nz, ny, nx, rows_u, 3 * D)
    out = g_out.reshape(2, nz, ny, nx, rows_o, D)
    cols = lambda r, a, n: r.at[:, :, :, :, a : a + n]
    wide = 3 * D // 2
    views = [
        lambda r: [(r.at[0, 0], r.at[1, 0]), (r.at[0, 1], r.at[1, 1])],
        lambda r: [(cols(r, 0, half), cols(r, ff, half)), (cols(r, half, half), cols(r, ff + half, half))],
        lambda r: [(cols(r, 0, cut), cols(r, wide, cut)), (cols(r, cut, wide - cut), cols(r, wide + cut, wide - cut))],
        lambda r: [(r.at[0], r.at[1])],
        lambda r: [(r.at[0], r.at[1])],
    ]
    sizes = [(rows_d, D, BF16)] * 2 + [(rows_u, half, BF16)] * 2 + [(rows_u, cut, BF16), (rows_u, wide - cut, BF16), (rows_o, D, BF16)]
    sizes.append(small.shape[-2:] + (F32,))
    firsts = ["x", "y"] * 3 + ["y", "x"]
    scratch = []
    for (r, w, t), first in zip(sizes, firsts):
        scratch += buffers(dims, r, w, t, first)
    totals = pl.pallas_call(
        functools.partial(reduce_kernel, dims, views, firsts),
        in_specs=[pl.BlockSpec(memory_space=pl.ANY)] * 5,
        out_specs=[pl.BlockSpec(memory_space=pltpu.VMEM)] * len(sizes),
        out_shape=[jax.ShapeDtypeStruct((nz, ny, nx, r, w), t) for r, w, t in sizes],
        scratch_shapes=scratch,
        compiler_params=pltpu.CompilerParams(collective_id=0, has_side_effects=True, vmem_limit_bytes=60 * 2**20),
        name="all_reduce",
    )(down, up, qkv, out, small)
    flat = [t.reshape(-1, t.shape[-1]) for t in totals]
    return (
        jnp.concatenate(flat[:2], axis=0).astype(F32),
        jnp.concatenate(flat[2:4], axis=1).astype(F32),
        jnp.concatenate(flat[4:6], axis=1).astype(F32),
        flat[6].astype(F32),
        flat[7].reshape(-1),
    )


class Route:
    def __init__(self, dims, first, near, far, mine, pair, total, bufs, sems):
        self.dims, self.first, self.near, self.far = dims, first, near, far
        self.mine, self.pair, self.total = mine, pair, total
        self.land, self.land2, self.land3 = bufs
        self.sems = sems
        self.count = 0
        self.flight = []

    def launch(self, make):
        slot = self.count
        self.count += 1
        make(slot).start()
        self.flight.append(lambda: make(slot))

    def remote(self, src, dst, where):
        self.launch(
            lambda slot: pltpu.make_async_remote_copy(
                src_ref=src(), dst_ref=dst(), send_sem=self.sems.at[0, slot], recv_sem=self.sems.at[1, slot],
                device_id=where(), device_id_type=pl.DeviceIdType.MESH,
            )
        )

    def local(self, src, dst):
        self.launch(lambda slot: pltpu.make_async_copy(src(), dst(), self.sems.at[0, slot]))

    def settle(self):
        for make in self.flight:
            make().wait()
        self.flight = []

    def steps(self, place):
        z, y, x, side, index = place
        nz, ny, nx = self.dims
        plain = self.first == "x"
        one, two = (2, 1) if plain else (1, 2)
        own = (z, y, x)

        def peer(axis, shift):
            return lax.rem(own[axis] + shift, self.dims[axis])

        def device(axis, shift):
            at = list(own)
            at[axis] = peer(axis, shift)
            return ((at[0] * ny + at[1]) * nx + at[2], side)

        def row(ref, i):
            return ref[i, :, x] if plain else ref[i, y]

        def start():
            if self.near is not None:
                self.local(lambda: self.near(), lambda: self.mine())
            self.remote(lambda: self.far(), lambda: self.pair(), lambda: (index, 1 - side))

        def pair_add():
            self.settle()
            mine, pair = self.mine(), self.pair()

            def body(i, _):
                mine[i] = (mine[i].astype(F32) + pair[i].astype(F32)).astype(mine.dtype)
                return 0

            lax.fori_loop(0, nz, body, 0)
            for s in range(1, self.dims[one]):
                self.remote(
                    lambda s=s: self.mine().at[:, :, peer(one, s)] if plain else self.mine().at[:, peer(one, s)],
                    lambda s=s: self.land().at[s - 1],
                    lambda s=s: device(one, s),
                )

        def add_one():
            self.settle()
            mine, land = self.mine(), self.land()

            def body(i, _):
                v = row(mine, i).astype(F32)
                for s in range(1, self.dims[one]):
                    v = v + land[s - 1, i].astype(F32)
                if plain:
                    mine[i, :, x] = v.astype(mine.dtype)
                else:
                    mine[i, y] = v.astype(mine.dtype)
                return 0

            lax.fori_loop(0, nz, body, 0)
            for s in range(1, self.dims[two]):
                self.remote(
                    lambda s=s: self.mine().at[:, peer(two, s), x] if plain else self.mine().at[:, y, peer(two, s)],
                    lambda s=s: self.land2().at[s - 1],
                    lambda s=s: device(two, s),
                )

        def add_two():
            self.settle()
            mine, land = self.mine(), self.land2()

            def body(i, _):
                v = mine[i, y, x].astype(F32)
                for s in range(1, self.dims[two]):
                    v = v + land[s - 1, i].astype(F32)
                mine[i, y, x] = v.astype(mine.dtype)
                return 0

            lax.fori_loop(0, nz, body, 0)
            for s in range(1, nz):
                self.remote(
                    lambda s=s: self.mine().at[peer(0, s), y, x], lambda s=s: self.land3().at[s - 1], lambda s=s: device(0, s)
                )

        def spread(axis, view, source):
            for s in range(1, self.dims[axis]):
                self.remote(lambda: view(source()), lambda: view(self.total()), lambda s=s: device(axis, s))

        def add_three():
            self.settle()
            mine, land = self.mine(), self.land3()
            v = mine[z, y, x].astype(F32)
            for s in range(1, nz):
                v = v + land[s - 1].astype(F32)
            mine[z, y, x] = v.astype(mine.dtype)
            self.local(lambda: self.mine().at[z, y, x], lambda: self.total().at[z, y, x])
            spread(0, lambda t: t.at[z, y, x], self.mine)

        def wide_two():
            self.settle()
            spread(two, lambda t: t.at[:, y, x], self.total)

        def wide_one():
            self.settle()
            spread(one, lambda t: t.at[:, :, x] if plain else t.at[:, y], self.total)

        return [start, pair_add, add_one, add_two, add_three, wide_two, wide_one, self.settle]


def route_buffers(dims, rows, width, dtype, first):
    nz, ny, nx = dims
    na, nb = (nx, ny) if first == "x" else (ny, nx)
    tail = (rows, width)
    shapes = [(max(na - 1, 1), nz, nb) + tail, (max(nb - 1, 1), nz) + tail, (max(nz - 1, 1),) + tail]
    copies = 3 + 2 * (na + nb + nz - 3)
    return [pltpu.VMEM(s, dtype) for s in shapes] + [pltpu.SemaphoreType.DMA((2, copies))]


PAIRS = D // 128
BLOCK = 256


def greet(dims, place):
    z, y, x, side, index = place
    barrier = pltpu.get_barrier_semaphore()
    peers = [(index, 1 - side)]
    for axis in range(3):
        for s in range(1, dims[axis]):
            at = [z, y, x]
            at[axis] = lax.rem(at[axis] + s, dims[axis])
            peers.append(((at[0] * dims[1] + at[1]) * dims[2] + at[2], side))
    for peer in peers:
        pl.semaphore_signal(barrier, inc=1, device_id=peer, device_id_type=pl.DeviceIdType.MESH)
    pl.semaphore_wait(barrier, len(peers))


def place_of(dims):
    index, side = lax.axis_index("dp"), lax.axis_index("tensor")
    _, ny, nx = dims
    return (index // (ny * nx), lax.rem(index // nx, ny), lax.rem(index, nx), side, index)


def columns(ref, start, width):
    return ref.at[..., start : start + width]


STRIPS = 4
FIRST_PAIR = STRIPS + 1
QKV_STEP = FIRST_PAIR + PAIRS
ORDER = (
    (0, 3, 1, 2),
    (0, 3),
    (),
    (2,),
    (5, 0, 6, 7),
    (1, 3, 6, 4, 0, 2, 8),
    (9, 0, 1, 3, 5, 4, 9, 2),
    (0, 7, 3, 1, 5, 8, 2),
    (0, 4, 5),
    (2, 3, 1, 7, 6, 5),
    (1, 4, 3, 2),
    (5, 4, 1),
    (10, 4, 11, 9, 7, 6, 8, 10, 11, 13, 12, 8, 9, 12, 13, 7),
    (8, 10, 11, 6, 1, 4, 5, 9),
    (7, 8, 11, 10),
    (12, 6, 13),
    (
        11, 14, 8, 9, 10, 7, 14, 11, 12, 6, 13, 10, 0, 5, 12, 8, 14, 11, 2, 12, 13, 10, 7, 14, 6, 14, 13, 14, 9, 12, 14,
        13, 10, 9, 11, 4, 3, 12, 13, 14,
    ),
)


def tail_kernel(dims, table, late, schedule, count, *refs):
    (
        prefix_ref, q_ref, k_ref, v_ref, o_ref, g_ref, lse_ref, n1t_ref, w_ref, x_ref, gm_ref, gain_ref, svec_ref, swide_ref,
        gh_ref, n2t_ref, n3t_ref, gml_ref, down_ref, ig_ref, odown_ref, oup_ref, oqkv_ref, oout_ref, osmall_ref,
        gproj, gqkv, gup, gout, bias, sums, small, mdown, pdown, pup, pout, pqkv, psmall,
    ) = refs[:38]
    scratch = refs[38:]
    pid = pl.program_id(0)
    _, ny, nx = dims
    place = place_of(dims)

    @pl.when(pid == 0)
    def _():
        greet(dims, place)
        sums[...] = jnp.zeros_like(sums)

    homes = {
        "up": (gup, pup, oup_ref),
        "qkv": (gqkv, pqkv, oqkv_ref),
        "out": (gout, pout, oout_ref),
        "small": (small, psmall, osmall_ref),
    }
    plans = []
    for n, (name, lead, start, width, first) in enumerate(table):
        bufs = scratch[4 * n : 4 * n + 4]
        cut = lambda r, at=start, width=width: columns(r, at, width)
        if name == "down":
            views = [down_ref.at[0, lead], down_ref.at[1, lead], mdown.at[lead], pdown.at[lead], odown_ref.at[lead]]
            views = [lambda v=v, cut=cut: cut(v) for v in views]
        else:
            src, pair, total = homes[name]
            near = lambda s=src, cut=cut: cut(s)
            far = lambda s=src, at=start + lead, width=width: columns(s, at, width)
            if name in ("out", "small"):
                near, far = [lambda s=src, i=i, cut=cut: cut(s.at[i]) for i in (0, 1)]
            done = lambda t=total, cut=cut: cut(t)
            if name == "qkv":
                third = D // 2
                done = lambda t=total, at=start, width=width: columns(t.at[at // third], at % third, width)
            views = [None, far, near, lambda p=pair, cut=cut: cut(p), done]
        plans.append(Route(dims, first, *views, [(lambda b=b: b) for b in bufs[:3]], bufs[3]).steps(place))

    def advance(step):
        for n, k in schedule.get(step, ()):
            plans[n][k]()

    for step in range(count):
        if schedule.get(step):
            pl.when(pid == step)(functools.partial(advance, step))

    @pl.when(pid < STRIPS)
    def _():
        width = gh_ref.shape[1]
        at = pl.ds(pl.multiple_of(pid * width, width), width)
        gup[:, :, :, :, at] = nn(n3t_ref[...], gh_ref[...]).astype(BF16).reshape(gup.shape[:4] + (width,))

    @pl.when(pid == STRIPS)
    def _():
        gout[...] = nn(n2t_ref[...], gml_ref[...]).reshape(gout.shape).astype(BF16)

    @pl.when((pid >= FIRST_PAIR) & (pid < QKV_STEP))
    def _():
        i = pid - FIRST_PAIR
        column = lambda c: gproj.at[:, pl.ds(pl.multiple_of(head_block(i, c) * 128, 128), 128)]
        attn_bwd_kernel(
            prefix_ref, q_ref, k_ref, v_ref, o_ref, g_ref, lse_ref, column(0), column(1), column(2),
            bias.at[:, pl.ds(pl.multiple_of(i * 128, 128), 128)],
        )

    @pl.when(pid == QKV_STEP)
    def _():
        def body(c, _):
            at = pl.ds(pl.multiple_of(c * D, 128), D)
            part = nn(n1t_ref[...], gproj[:, at]).astype(BF16)
            gqkv[:, :, :, :, at] = part.reshape(gqkv.shape[:4] + (D,))
            return 0

        lax.fori_loop(0, 3, body, 0)

    @pl.when(pid > QKV_STEP)
    def _():
        rows = pl.ds(pl.multiple_of((pid - QKV_STEP - 1) * BLOCK, BLOCK), BLOCK)
        e = nt(gproj[rows, :], w_ref[...])
        xhat, inv = normed(x_ref[...].astype(F32))
        sums[0] += colsum(e * xhat)
        sums[1] += colsum(e)
        ig_ref[...] = gm_ref[...] + normed_back(e * gain_ref[...].reshape(1, D), xhat, inv)

    @pl.when(pid == count - 1)
    def _():
        small[...] = jnp.zeros_like(small)
        split = [bias[i : i + 1, :] for i in range(2)]
        split += [jnp.sum(svec_ref[i], axis=0, keepdims=True) for i in range(2)]
        split += [jnp.sum(swide_ref[i], axis=0, keepdims=True) for i in range(3)]
        shared = [jnp.sum(sums[i], axis=0, keepdims=True) for i in range(2)]
        shared += [jnp.sum(svec_ref[i], axis=0, keepdims=True) for i in range(2, 6)]
        for s in range(2):
            at = 0
            for v in [v[:, s * (v.shape[1] // 2) : (s + 1) * (v.shape[1] // 2)] for v in split] + shared:
                for c in range(v.shape[1] // 128):
                    p = at // 8
                    small[s, p // (ny * nx), p // nx % ny, p % nx, at % 8 : at % 8 + 1, :] = v[:, c * 128 : (c + 1) * 128]
                    at += 1
        for n, k in late:
            plans[n][k]()


def tail_stage(dims, prefix, qkv, attended, ga, lse, n1t, wqkv, tokens, gm, pre_gain, svec, swide, gh, n2t, n3t, gml, g_down):
    nz, ny, nx = dims
    parts = nz * ny * nx
    length = qkv.shape[0]
    ff = gh.shape[1] // 2
    half, third = ff // 2, D // 2
    rows = D // parts
    wide = 3 * D // 2
    small_rows = 8
    down = g_down.reshape(2, 2, nz, ny, nx, rows, D)
    table = []
    for a in (0, D // 2):
        table += [("down", 0, a, D // 2, "x"), ("down", 1, a, D // 2, "y")]
    for a in (0, half // 2):
        table += [("up", ff, a, half // 2, "x"), ("up", ff, half + a, half // 2, "y")]
    table += [("out", 0, 0, third, "x"), ("out", 0, third, third, "y")]
    table += [("qkv", wide, 0, third, "x"), ("qkv", wide, 2 * third, third, "y")]
    table += [("qkv", wide, third, 256, "x"), ("qkv", wide, third + 256, 128, "y")]
    table += [("small", 0, 0, 128, "x")]
    count = QKV_STEP + 1 + length // BLOCK
    phase = [0] * len(table)
    steps = []
    for pieces in ORDER:
        steps.append([])
        for n in pieces:
            steps[-1].append((n, phase[n]))
            phase[n] += 1
    schedule, late = dict(enumerate(steps[:count])), steps[count]
    sds = jax.ShapeDtypeStruct
    box = (nz, ny, nx)
    shapes = {
        "down": (2, *box, rows, D), "up": (*box, rows, ff), "qkv": (*box, rows, wide), "out": (*box, rows // 2, D),
        "small": (*box, small_rows, 128),
    }
    kinds = {n: F32 if n == "small" else BF16 for n in shapes}
    landed = dict(shapes, qkv=(3, *box, rows, third))
    scratch = [
        pltpu.VMEM((length, 3 * D), BF16), pltpu.VMEM((*box, rows, 3 * D), BF16), pltpu.VMEM((*box, rows, 2 * ff), BF16),
        pltpu.VMEM((2, *box, rows // 2, D), BF16), pltpu.VMEM((8, D), F32), pltpu.VMEM((2, 8, D), F32),
        pltpu.VMEM((2, *box, small_rows, 128), F32), pltpu.VMEM(shapes["down"], BF16),
    ]
    scratch += [pltpu.VMEM(shapes[n], kinds[n]) for n in ("down", "up", "out", "qkv", "small")]
    heights = {"down": rows, "up": rows, "qkv": rows, "out": rows // 2, "small": small_rows}
    for name, _, _, width, first in table:
        scratch += route_buffers(dims, heights[name], width, kinds[name], first)
    pair_at = lambda i: jnp.clip(i - FIRST_PAIR, 0, PAIRS - 1)
    block_at = lambda i: jnp.maximum(i - QKV_STEP - 1, 0)
    col = lambda c: pl.BlockSpec((length, 128), lambda i, c=c: (0, head_block(pair_at(i), c)))
    one = pl.BlockSpec((length, 128), lambda i: (0, pair_at(i)))
    block = pl.BlockSpec((BLOCK, D), lambda i: (block_at(i), 0))
    strip = pl.BlockSpec((length, 2 * ff // STRIPS), lambda i: (0, jnp.minimum(i, STRIPS - 1)))
    whole = lambda v: pl.BlockSpec(v.shape, lambda i, n=v.ndim: (0,) * n, pipeline_mode=pl.Buffered(1))
    hbm = pl.BlockSpec(memory_space=pl.ANY)
    return pl.pallas_call(
        functools.partial(tail_kernel, dims, table, late, schedule, count),
        grid=(count,),
        in_specs=[
            pl.BlockSpec(memory_space=pltpu.SMEM), col(0), col(1), col(2), one, one,
            pl.BlockSpec((1, 8, length), lambda i: (pair_at(i), 0, 0)), whole(n1t), whole(wqkv), block, block, whole(pre_gain),
            whole(svec), whole(swide), strip, whole(n2t), whole(n3t), whole(gml), hbm,
        ],
        out_specs=[block] + [hbm] * 5,
        out_shape=[sds((length, D), F32)] + [sds(landed[n], kinds[n]) for n in ("down", "up", "qkv", "out", "small")],
        scratch_shapes=scratch,
        compiler_params=pltpu.CompilerParams(collective_id=1, has_side_effects=True, vmem_limit_bytes=VMEM),
        name="tail_stage",
    )(
        prefix, qkv, qkv, qkv, attended, ga, lse, n1t, wqkv, tokens, gm, pre_gain, svec, swide, gh, n2t, n3t, gml, down,
    )


def unpack_kernel(ig_ref, down_ref, up_ref, qkv_ref, out_ref, small_ref, oig, odown, oup, oqkv, oout, *vectors):
    oig[...] = ig_ref[...]
    odown[...] = down_ref[...].astype(F32)
    oup[...] = up_ref[...].astype(F32)
    oqkv[...] = qkv_ref[...].astype(F32)
    oout[...] = out_ref[...].astype(F32).reshape(oout.shape)

    @pl.when(pl.program_id(0) == 0)
    def _():
        at = 0
        for ref in vectors:
            for row in range(ref.shape[0] if ref.ndim == 2 else 1):
                for c in range(ref.shape[-1] // 128):
                    lanes = pl.ds(c * 128, 128)
                    if ref.ndim == 2:
                        ref[row, lanes] = small_ref[at, :]
                    else:
                        ref[lanes] = small_ref[at, :]
                    at += 1


def unpack(input_grad, down, up, qkv, out, small, ff):
    steps = 8
    half = D // 2
    down, up, qkv = down.reshape(ff, D), up.reshape(D, ff), qkv.reshape(3 * D, half)
    out = out.reshape((-1,) + out.shape[-2:])
    small = small.reshape(-1, 128)
    block = lambda v: pl.BlockSpec((v.shape[0] // steps,) + v.shape[1:], lambda i, n=v.ndim: (i,) + (0,) * (n - 1))
    whole = lambda s: pl.BlockSpec(s, lambda i: (0,) * len(s), pipeline_mode=pl.Buffered(1))
    sds = lambda s: jax.ShapeDtypeStruct(s, F32)
    vectors = [(2, half), (half,), (half,), (ff,), (ff,), (ff,)] + [(D,)] * 6
    shapes = [input_grad.shape, (ff, D), (D, ff), (3 * D, half), (half, D)]
    return pl.pallas_call(
        unpack_kernel,
        grid=(steps,),
        in_specs=[block(v) for v in (input_grad, down, up, qkv, out)] + [whole(small.shape)],
        out_specs=[block(sds(s)) for s in shapes] + [whole(s) for s in vectors],
        out_shape=[sds(s) for s in shapes + vectors],
        compiler_params=pltpu.CompilerParams(vmem_limit_bytes=VMEM),
        name="unpack",
    )(input_grad, down, up, qkv, out, small)


def head_kernel(
    x_ref, gain_ref, bias_ref, w_ref, wo_ref, sub_gain, sub_bias, up_bias, inner_gain, inner_bias, qv_ref,
    out_bias, ffn_gain, ffn_bias, down_bias,
    qkv_ref, n1t_ref, wall_ref, far_wo, vec_ref, wide_ref,
    near_sem, send_sem, recv_sem, norm_ref, far_sg, far_sb, far_ub, far_ig, far_ib, far_qv,
):
    index, side = lax.axis_index("dp"), lax.axis_index("tensor")
    other = (index, 1 - side)
    mesh_id = pl.DeviceIdType.MESH
    barrier = pltpu.get_barrier_semaphore()
    pl.semaphore_signal(barrier, inc=1, device_id=other, device_id_type=mesh_id)
    half = D // 2
    wide = 3 * half
    here = [pltpu.make_async_copy(w_ref.at[c], wall_ref.at[:, c * half : (c + 1) * half], near_sem.at[c]) for c in range(3)]
    for copy in here:
        copy.start()
    pl.semaphore_wait(barrier, 1)
    away = [(w_ref.at[c], wall_ref.at[:, wide + c * half : wide + (c + 1) * half]) for c in range(3)]
    away += [(qv_ref, far_qv), (sub_gain, far_sg), (sub_bias, far_sb)]
    away += [(up_bias, far_ub), (inner_gain, far_ig), (inner_bias, far_ib), (wo_ref, far_wo)]
    away = [
        pltpu.make_async_remote_copy(
            src_ref=a, dst_ref=b, send_sem=send_sem.at[i], recv_sem=recv_sem.at[i], device_id=other, device_id_type=mesh_id
        )
        for i, (a, b) in enumerate(away)
    ]
    for copy in away:
        copy.start()
    length = x_ref.shape[0]
    block = 256
    line = lambda ref: ref[...].reshape(1, -1)
    gain, bias = line(gain_ref), line(bias_ref)

    def norm(i, _):
        rows = pl.ds(pl.multiple_of(i * block, block), block)
        xhat, _ = normed(x_ref[rows, :].astype(F32))
        n1 = (xhat * gain + bias).astype(BF16)
        norm_ref[rows, :] = n1
        n1t_ref[:, rows] = n1.T
        return 0

    lax.fori_loop(0, length // block, norm, 0)

    def product(first, biases):
        weight = wall_ref[:, first : first + wide]
        bias = jnp.concatenate([biases[0:1, :], jnp.zeros((1, half), F32), biases[1:2, :]], axis=1)

        def rows(i, _):
            at = pl.ds(pl.multiple_of(i * block, block), block)
            qkv_ref[at, first : first + wide] = (nn(norm_ref[at, :], weight) + bias).astype(BF16)
            return 0

        lax.fori_loop(0, length // block, rows, 0)

    for copy in here:
        copy.wait()
    product(0, qv_ref[...])
    for copy in away:
        copy.wait()
    product(wide, far_qv[...])
    both = lambda near, far: jnp.concatenate([line(near), line(far)], axis=1)
    vec_ref[0:1, :] = both(sub_gain, far_sg)
    vec_ref[1:2, :] = both(sub_bias, far_sb)
    for i, v in enumerate((out_bias, ffn_gain, ffn_bias, down_bias)):
        vec_ref[i + 2 : i + 3, :] = line(v)
    for i, (near, far) in enumerate(((up_bias, far_ub), (inner_gain, far_ig), (inner_bias, far_ib))):
        wide_ref[i : i + 1, :] = both(near, far)


def head_stage(tokens, pre_gain, pre_bias, w3, wo, sub_gain, sub_bias, up_bias, inner_gain, inner_bias, qv_bias, *rest):
    length = tokens.shape[0]
    ff_half = up_bias.shape[0]
    half = D // 2
    sds = jax.ShapeDtypeStruct
    vmem, hbm = pl.BlockSpec(memory_space=pltpu.VMEM), pl.BlockSpec(memory_space=pl.ANY)
    return pl.pallas_call(
        head_kernel,
        in_specs=[vmem] * 3 + [hbm] * 2 + [vmem] * 10,
        out_specs=[vmem] * 3 + [hbm] + [vmem] * 2,
        out_shape=[
            sds((length, 3 * D), BF16), sds((D, length), BF16), sds((D, 3 * D), BF16), sds(wo.shape, BF16),
            sds((6, D), F32), sds((3, 2 * ff_half), F32),
        ],
        scratch_shapes=[
            pltpu.SemaphoreType.DMA((3,)), pltpu.SemaphoreType.DMA((10,)), pltpu.SemaphoreType.DMA((10,)),
            pltpu.VMEM((length, D), BF16), *[pltpu.VMEM((half,), F32)] * 2,
            *[pltpu.VMEM((ff_half,), F32)] * 3, pltpu.VMEM((2, half), F32),
        ],
        compiler_params=pltpu.CompilerParams(collective_id=2, has_side_effects=True, vmem_limit_bytes=VMEM),
        name="head_stage",
    )(tokens, pre_gain, pre_bias, w3, wo, sub_gain, sub_bias, up_bias, inner_gain, inner_bias, qv_bias, *rest)


def pack_small(dims, g_qv, g_vec, g_wide, g_pre):
    half, ff_half = D // 2, g_wide.shape[1] // 2
    shared = jnp.concatenate([g_pre.reshape(-1), g_vec[2:].reshape(-1)])
    rows = -(-(4 * half + 3 * ff_half + 6 * D) // (128 * 8 * math.prod(dims))) * 8
    pad = jnp.zeros((rows * 128 * math.prod(dims) - (4 * half + 3 * ff_half + 6 * D),), F32)
    pack = lambda i: jnp.concatenate(
        [v[j, i * n : (i + 1) * n] for v, m, n in ((g_qv, 2, half), (g_vec, 2, half), (g_wide, 3, ff_half)) for j in range(m)] + [shared, pad]
    )
    return jnp.stack([pack(0), pack(1)]).reshape((2,) + dims + (rows, 128))


def body(
    dims, tokens, grad_out, prefix, pre_gain, pre_bias, qkv_weight, qv_bias, sub_gain, sub_bias, out_weight, out_bias,
    ffn_gain, ffn_bias, up_weight, up_bias, inner_gain, inner_bias, down_weight, down_bias,
):
    half, ff_half = D // 2, up_bias.shape[0]
    qkv, n1t, wqkv, wo_far, vecs, wides = head_stage(
        tokens, pre_gain, pre_bias, qkv_weight.transpose(1, 0, 2), out_weight, sub_gain, sub_bias, up_bias, inner_gain, inner_bias,
        qv_bias, out_bias, ffn_gain, ffn_bias, down_bias,
    )
    attended, lse, wu_far, wd_far = attn_fwd(prefix, qkv, up_weight, down_weight)
    wo, wu, wd = (out_weight, wo_far), (up_weight, wu_far), (down_weight, wd_far)
    out, n2t, n3t, n4, gh, gm, gml, ga, svec, swide = middle_stage(tokens, attended, grad_out, vecs, wides, wo, wu, wd)
    g_down = tn(n4, grad_out).astype(BF16)
    if D // math.prod(dims) % 16 == 0:
        sums = tail_stage(
            dims, prefix, qkv, attended, ga, lse, n1t, wqkv, tokens, gm, pre_gain, svec, swide, gh, n2t, n3t, gml, g_down
        )
        input_grad, g_down, g_up, g_qkv, g_out, *vectors = unpack(*sums, ff_half)
        g_qv, g_sub_gain, g_sub_bias, g_up_bias, g_inner_gain, g_inner_bias = vectors[:6]
        g_pre_gain, g_pre_bias, g_out_bias, g_ffn_gain, g_ffn_bias, g_down_bias = vectors[6:]
        g_qkv = g_qkv.reshape(3, D, half)
    else:
        g_up, g_out = nn(n3t, gh).astype(BF16), nn(n2t, gml).astype(BF16)
        input_grad, g_pre, g_qkv, g_qv = back(prefix, tokens, pre_gain, wqkv, n1t.T, qkv, attended, lse, gm, ga)
        small = pack_small(dims, g_qv, jnp.sum(svec, 1), jnp.sum(swide, 1), g_pre)
        g_down, g_up, g_qkv, g_out, small = all_reduce(dims, (g_down, g_up, g_qkv, g_out), small)
        g_qkv = g_qkv.reshape(D, 3, half).transpose(1, 0, 2)
        g_qv = small[: 2 * half].reshape(2, half)
        g_sub_gain, g_sub_bias = [small[i * half : (i + 1) * half] for i in (2, 3)]
        g_up_bias, g_inner_gain, g_inner_bias = [small[4 * half + i * ff_half : 4 * half + (i + 1) * ff_half] for i in range(3)]
        base = 4 * half + 3 * ff_half
        g_pre_gain, g_pre_bias, g_out_bias, g_ffn_gain, g_ffn_bias, g_down_bias = [
            small[base + i * D : base + (i + 1) * D] for i in range(6)
        ]
    return (
        out, input_grad, g_pre_gain, g_pre_bias, g_qkv.transpose(1, 0, 2), g_qv, g_sub_gain, g_sub_bias, g_out, g_out_bias,
        g_ffn_gain, g_ffn_bias, g_up, g_up_bias, g_inner_gain, g_inner_bias, g_down, g_down_bias,
    )


def solution(mesh):
    rows = P(("dp", "tensor"), None)
    wide, tall, vec, whole = P(None, "tensor"), P("tensor", None), P("tensor"), P()
    cube = P(None, None, "tensor")
    return jax.shard_map(
        functools.partial(body, grid_of(mesh.shape["dp"])),
        mesh=mesh,
        in_specs=(
            rows, rows, P("dp"), whole, whole, cube, wide, vec, vec, tall, whole, whole, whole, wide, vec, vec, vec, tall, whole,
        ),
        out_specs=(
            rows, rows, whole, whole, cube, wide, vec, vec, tall, whole, whole, whole, wide, vec, vec, vec, tall, whole,
        ),
        check_vma=False,
    )
```

```python
import functools
import math

import jax
import jax.numpy as jnp
from jax import lax
from jax.sharding import PartitionSpec as P
from jax.experimental import pallas as pl
from jax.experimental.pallas import tpu as pltpu

D = 768
HEAD_DIM = 64
PREFIX_MAX = 512
EPS = 1e-05
F32 = jnp.float32
BF16 = jnp.bfloat16
QB = 512
VMEM = 67043328


def nn(a, b):
    return lax.dot_general(a, b, (((1,), (0,)), ((), ())), preferred_element_type=F32)


def nt(a, b):
    return lax.dot_general(a, b, (((1,), (1,)), ((), ())), preferred_element_type=F32)


def tn(a, b):
    return lax.dot_general(a, b, (((0,), (0,)), ((), ())), preferred_element_type=F32)


def halves(v):
    left = lax.broadcasted_iota(jnp.int32, v.shape, 1) < HEAD_DIM
    zero = jnp.zeros_like(v)
    return jnp.where(left, v, zero), jnp.where(left, zero, v)


def spans(start, length, block):
    last = min(length, max(start + block, PREFIX_MAX))
    out = []
    if start:
        out.append((0, start, False))
    out.append((start, last, True))
    return out


def masked(scores, key_start, query_start, prefix):
    key_pos = key_start + lax.broadcasted_iota(jnp.int32, scores.shape, 0)
    query_pos = query_start + lax.broadcasted_iota(jnp.int32, scores.shape, 1)
    seen = key_pos <= query_pos
    if key_start < PREFIX_MAX:
        seen = seen | (key_pos < prefix)
    return jnp.where(seen, scores, -1e30)


def head_block(i, c):
    each = D // 256
    return i // each * 3 * each + c * each + lax.rem(i, each)


def attn_fwd_kernel(prefix_ref, q_ref, k_ref, v_ref, wu_ref, wd_ref, o_ref, lse_ref, far_wu, far_wd, send_sem, recv_sem):
    pid = pl.program_id(0)
    other = (lax.axis_index("dp"), 1 - lax.axis_index("tensor"))

    def exchange(i, src, dst):
        return pltpu.make_async_remote_copy(
            src_ref=src, dst_ref=dst, send_sem=send_sem.at[i], recv_sem=recv_sem.at[i], device_id=other,
            device_id_type=pl.DeviceIdType.MESH,
        )

    @pl.when(pid == 0)
    def _():
        barrier = pltpu.get_barrier_semaphore()
        pl.semaphore_signal(barrier, inc=1, device_id=other, device_id_type=pl.DeviceIdType.MESH)
        pl.semaphore_wait(barrier, 1)
        exchange(0, wu_ref, far_wu).start()
        exchange(1, wd_ref, far_wd).start()

    length = q_ref.shape[0]
    prefix = prefix_ref[lax.axis_index("tensor")]
    keys = halves(k_ref[...])
    value_t = v_ref[...].T
    units = [(start, head) for start in range(0, length, QB) for head in range(2)]

    def score(start, head):
        query = q_ref[start : start + QB, :] * jnp.asarray(HEAD_DIM**-0.5, BF16)
        scores = []
        for first, last, mask in spans(start, length, QB):
            s = nt(keys[head][first:last], query)
            scores.append(masked(s, first, start, prefix) if mask else s)
        return scores

    parts = []
    ahead = score(*units[0])
    for unit, (start, head) in enumerate(units):
        scores = ahead
        if unit + 1 < len(units):
            ahead = score(*units[unit + 1])
        peak = functools.reduce(jnp.maximum, [jnp.max(s, axis=0, keepdims=True) for s in scores])
        total = jnp.zeros_like(peak)
        mixed = jnp.zeros((HEAD_DIM, QB), F32)
        rows = slice(head * HEAD_DIM, (head + 1) * HEAD_DIM)
        for s, (first, last, _) in zip(scores, spans(start, length, QB)):
            w = jnp.exp(s - peak)
            total = total + jnp.sum(w, axis=0, keepdims=True)
            mixed = mixed + nn(value_t[rows, first:last], w.astype(BF16))
        parts.append(mixed / total)
        lse_ref[0, head : head + 1, start : start + QB] = peak + jnp.log(total)
        if head == 1:
            o_ref[start : start + QB, :] = jnp.concatenate(parts, axis=0).T
            parts = []

    @pl.when(pid == pl.num_programs(0) - 1)
    def _():
        exchange(0, wu_ref, far_wu).wait()
        exchange(1, wd_ref, far_wd).wait()


def attn_fwd(prefix, qkv, wu, wd):
    length = qkv.shape[0]
    pairs = D // 128
    col = lambda c: pl.BlockSpec((length, 128), lambda i, c=c: (0, head_block(i, c)))
    hbm = pl.BlockSpec(memory_space=pl.ANY)
    return pl.pallas_call(
        attn_fwd_kernel,
        grid=(pairs,),
        in_specs=[pl.BlockSpec(memory_space=pltpu.SMEM), col(0), col(1), col(2), hbm, hbm],
        out_specs=[
            pl.BlockSpec((length, 128), lambda i: (0, i)),
            pl.BlockSpec((1, 8, length), lambda i: (i, 0, 0)),
            hbm,
            hbm,
        ],
        out_shape=[
            jax.ShapeDtypeStruct((length, D), F32),
            jax.ShapeDtypeStruct((pairs, 8, length), F32),
            jax.ShapeDtypeStruct(wu.shape, BF16),
            jax.ShapeDtypeStruct(wd.shape, BF16),
        ],
        scratch_shapes=[pltpu.SemaphoreType.DMA((2,))] * 2,
        compiler_params=pltpu.CompilerParams(collective_id=4, has_side_effects=True, vmem_limit_bytes=VMEM),
        name="attn_fwd",
    )(prefix, qkv, qkv, qkv, wu, wd)


def attn_bwd_kernel(prefix_ref, q_ref, k_ref, v_ref, o_ref, g_ref, lse_ref, dq_ref, dk_ref, dv_ref, bias_ref):
    length = q_ref.shape[0]
    prefix = prefix_ref[lax.axis_index("tensor")]
    scale = HEAD_DIM**-0.5
    keys = halves(k_ref[...])
    values = halves(v_ref[...])
    key_t = k_ref[...].T
    delta_t = (o_ref[...] * g_ref[...].astype(F32)).T
    dk = [jnp.zeros((b - a, 128), F32) for a, b in zip(range(0, length, QB), range(QB, length + 1, QB))]
    dv = list(dk)
    qsum = jnp.zeros((8, 128), F32)
    for start in range(0, length, QB):
        cols = slice(start, start + QB)
        query = q_ref[cols, :] * jnp.asarray(scale, BF16)
        query_half = halves(query)
        grad = g_ref[cols, :]
        grad_half = halves(grad)
        parts = []
        for head in range(2):
            rows = slice(head * HEAD_DIM, (head + 1) * HEAD_DIM)
            lse = lse_ref[0, head : head + 1, cols]
            delta = jnp.sum(delta_t[rows, cols], axis=0, keepdims=True)
            dq = jnp.zeros((HEAD_DIM, QB), F32)
            for first in range(0, length, QB):
                live = [s for s in spans(start, length, QB) if s[0] <= first < s[1]]
                if not live:
                    continue
                last = first + QB
                s = nt(keys[head][first:last], query)
                if live[0][2]:
                    s = masked(s, first, start, prefix)
                w = jnp.exp(s - lse)
                dp = nt(values[head][first:last], grad)
                ds = (w * (dp - delta)).astype(BF16)
                b = first // QB
                dv[b] = dv[b] + nn(w.astype(BF16), grad_half[head])
                dk[b] = dk[b] + nn(ds, query_half[head])
                dq = dq + nn(key_t[rows, first:last], ds)
            parts.append(dq)
        dq = jnp.concatenate(parts, axis=0).T * scale
        qsum = qsum + jnp.sum(dq.reshape(QB // 8, 8, 128), axis=0)
        dq_ref[cols, :] = dq.astype(BF16)
    vsum = jnp.zeros((8, 128), F32)
    for b in range(length // QB):
        cols = slice(b * QB, (b + 1) * QB)
        dk_ref[cols, :] = dk[b].astype(BF16)
        dv_ref[cols, :] = dv[b].astype(BF16)
        vsum = vsum + jnp.sum(dv[b].reshape(QB // 8, 8, 128), axis=0)
    bias_ref[0:1, :] = jnp.sum(qsum, axis=0, keepdims=True)
    bias_ref[1:2, :] = jnp.sum(vsum, axis=0, keepdims=True)


def attn_bwd(prefix, qkv, attended, grad_attended, lse):
    length = qkv.shape[0]
    pairs = D // 128
    col = lambda c: pl.BlockSpec((length, 128), lambda i, c=c: (0, head_block(i, c)))
    one = pl.BlockSpec((length, 128), lambda i: (0, i))
    return pl.pallas_call(
        attn_bwd_kernel,
        grid=(pairs,),
        in_specs=[
            pl.BlockSpec(memory_space=pltpu.SMEM), col(0), col(1), col(2), one, one,
            pl.BlockSpec((1, 8, length), lambda i: (i, 0, 0)),
        ],
        out_specs=[one, one, one, pl.BlockSpec((8, 128), lambda i: (0, i))],
        out_shape=[jax.ShapeDtypeStruct((length, D), BF16)] * 3 + [jax.ShapeDtypeStruct((8, D), F32)],
        name="attn_bwd",
    )(prefix, qkv, qkv, qkv, attended, grad_attended, lse)


def normed(v):
    centre = v - jnp.mean(v, axis=-1, keepdims=True)
    inv = lax.rsqrt(jnp.mean(centre * centre, axis=-1, keepdims=True) + EPS)
    return centre * inv, inv


def normed_back(e, xhat, inv):
    return inv * (e - jnp.mean(e, axis=-1, keepdims=True) - xhat * jnp.mean(e * xhat, axis=-1, keepdims=True))


def colsum(v):
    rows, cols = v.shape
    return jnp.sum(v.reshape(rows // 8, 8, cols), axis=0)


def mid_kernel(
    x_ref, att_ref, g_ref, vec_ref, wide_ref, near_wo, far_wo, near_wu, far_wu, near_wd, far_wd,
    out_ref, n2_ref, n3_ref, n4_ref, gh_ref, gm_ref, gml_ref, ga_ref, svec_ref, swide_ref,
    act_ref, slope_ref, wo_ref, wu_ref, wd_ref, sem,
):
    first = pl.program_id(0) == 0
    half, ff_half = near_wo.shape[0], near_wu.shape[1]
    moves = (
        (near_wo, wo_ref.at[:half]), (far_wo, wo_ref.at[half:]), (near_wu, wu_ref.at[:, :ff_half]), (far_wu, wu_ref.at[:, ff_half:]),
        (near_wd, wd_ref.at[:ff_half]), (far_wd, wd_ref.at[ff_half:]),
    )
    moves = [pltpu.make_async_copy(a, b, sem.at[i]) for i, (a, b) in enumerate(moves)]

    def arrive(some):
        @pl.when(first)
        def _():
            for copy in some:
                copy.wait()

    @pl.when(first)
    def _():
        for copy in moves:
            copy.start()
        svec_ref[...] = jnp.zeros_like(svec_ref)
        swide_ref[...] = jnp.zeros_like(swide_ref)

    arrive(moves)
    sub_gain, sub_bias, out_bias, ffn_gain, ffn_bias, down_bias = [vec_ref[i : i + 1, :] for i in range(6)]
    up_bias, inner_gain, inner_bias = [wide_ref[i : i + 1, :] for i in range(3)]
    xhat2, inv2 = normed(att_ref[...])
    n2 = (xhat2 * sub_gain + sub_bias).astype(BF16)
    n2_ref[...] = n2.T
    middle = x_ref[...].astype(F32) + nn(n2, wo_ref[...]) + out_bias
    xhat3, inv3 = normed(middle)
    n3 = (xhat3 * ffn_gain + ffn_bias).astype(BF16)
    n3_ref[...] = n3.T
    g = g_ref[...]
    hidden = nn(n3, wu_ref[...]) + up_bias
    e = nt(g, wd_ref[...])
    half = 0.5 + 0.5 * lax.erf(hidden * (2.0**-0.5))
    act_ref[...] = hidden * half
    slope_ref[...] = half + hidden * (jnp.exp(-0.5 * hidden * hidden) * 0.3989422804014327)
    xhat4, inv4 = normed(act_ref[...])
    n4 = (xhat4 * inner_gain + inner_bias).astype(BF16)
    n4_ref[...] = n4
    act_ref[...] = xhat4
    out_ref[...] = (middle + nn(n4, wd_ref[...]) + down_bias).astype(BF16)
    xhat4 = act_ref[...]
    swide_ref[1] += colsum(e * xhat4)
    swide_ref[2] += colsum(e)
    gh = normed_back(e * inner_gain, xhat4, inv4) * slope_ref[...]
    swide_ref[0] += colsum(gh)
    ghl = gh.astype(BF16)
    gh_ref[...] = ghl
    gf = g.astype(F32)
    e = nt(ghl, wu_ref[...])
    svec_ref[3] += colsum(e * xhat3)
    svec_ref[4] += colsum(e)
    gm = gf + normed_back(e * ffn_gain, xhat3, inv3)
    svec_ref[2] += colsum(gm)
    svec_ref[5] += colsum(gf)
    gm_ref[...] = gm
    gml = gm.astype(BF16)
    gml_ref[...] = gml
    e = nt(gml, wo_ref[...])
    svec_ref[0] += colsum(e * xhat2)
    svec_ref[1] += colsum(e)
    ga_ref[...] = normed_back(e * sub_gain, xhat2, inv2).astype(BF16)


def middle_stage(x, att, g, vecs, wides, wo, wu, wd, block=256):
    rows = x.shape[0]
    ff = 2 * wu[0].shape[1]
    row = lambda n: pl.BlockSpec((block, n), lambda i: (i, 0))
    turned = pl.BlockSpec((D, block), lambda i: (0, i))
    whole = lambda s: pl.BlockSpec(s, lambda i: (0,) * len(s), pipeline_mode=pl.Buffered(1))
    sds = jax.ShapeDtypeStruct
    return pl.pallas_call(
        mid_kernel,
        grid=(rows // block,),
        in_specs=[row(D), row(D), row(D), whole(vecs.shape), whole(wides.shape)] + [pl.BlockSpec(memory_space=pl.ANY)] * 6,
        out_specs=[row(D), turned, turned, row(ff), row(ff), row(D), row(D), row(D), whole((6, 8, D)), whole((3, 8, ff))],
        out_shape=[
            sds((rows, D), BF16), sds((D, rows), BF16), sds((D, rows), BF16), sds((rows, ff), BF16), sds((rows, ff), BF16),
            sds((rows, D), F32), sds((rows, D), BF16), sds((rows, D), BF16), sds((6, 8, D), F32), sds((3, 8, ff), F32),
        ],
        scratch_shapes=[pltpu.VMEM((block, ff), F32), pltpu.VMEM((block, ff), F32), pltpu.VMEM((D, D), BF16), pltpu.VMEM((D, ff), BF16), pltpu.VMEM((ff, D), BF16), pltpu.SemaphoreType.DMA((6,))],
        compiler_params=pltpu.CompilerParams(vmem_limit_bytes=VMEM),
        name="middle_stage",
    )(x, att, g, vecs, wides, *wo, *wu, *wd)


def back(prefix, tokens, pre_gain, wqkv, n1, qkv, attended, lse, gm, ga):
    xhat1, inv1 = normed(tokens.astype(F32))
    dq, dk, dv, dbias = attn_bwd(prefix, qkv, attended, ga, lse)
    h = D // 2
    gproj = jnp.concatenate([v[:, s] for s in (slice(0, h), slice(h, D)) for v in (dq, dk, dv)], axis=1)
    g_qkv = tn(n1, gproj).astype(BF16)
    e = nt(gproj, wqkv)
    g_pre = jnp.stack([jnp.sum(e * xhat1, axis=0), jnp.sum(e, axis=0)])
    input_grad = gm + normed_back(e * pre_gain, xhat1, inv1)
    return input_grad, g_pre, g_qkv, dbias


def grid_of(count):
    side = 1
    while 2 * side**3 < count:
        side += 1
    return (2 * side, side, side) if 2 * side**3 == count else (count, 1, 1)


class Piece:
    def __init__(self, dims, first, near, far, total, bufs, sems, place):
        self.dims, self.first, self.near, self.far, self.total = dims, first, near, far, total
        self.mine, self.pair, self.land, self.part, self.land2, self.part2, self.land3 = bufs
        self.sems, self.place = sems, place
        self.count = 0
        self.flight = []

    def send(self, src, dst, where):
        copy = pltpu.make_async_remote_copy(
            src_ref=src, dst_ref=dst, send_sem=self.sems.at[0, self.count], recv_sem=self.sems.at[1, self.count],
            device_id=where, device_id_type=pl.DeviceIdType.MESH,
        )
        self.count += 1
        copy.start()
        self.flight.append(copy)

    def settle(self):
        for copy in self.flight:
            copy.wait()
        self.flight = []

    def device(self, axis, shift):
        at = list(self.place[:3])
        at[axis] = lax.rem(at[axis] + shift, self.dims[axis])
        nz, ny, nx = self.dims
        return at[axis], ((at[0] * ny + at[1]) * nx + at[2], self.place[3])

    def steps(self):
        z, y, x = self.place[:3]
        nz, ny, nx = self.dims
        one, two = (2, 1) if self.first == "x" else (1, 2)
        pick1 = lambda ref, p: ref.at[:, :, p] if one == 2 else ref.at[:, p]
        own1, own2 = (x, y) if one == 2 else (y, x)

        def start():
            local = pltpu.make_async_copy(self.near, self.mine, self.sems.at[0, self.count])
            self.count += 1
            local.start()
            self.send(self.far, self.pair, (self.place[4], 1 - self.place[3]))
            self.flight.append(local)

        def pair_add():
            self.settle()
            def one_row(i, _):
                self.mine[i] = (self.mine[i].astype(F32) + self.pair[i].astype(F32)).astype(self.mine.dtype)
                return 0
            lax.fori_loop(0, nz, one_row, 0)
            for s in range(1, self.dims[one]):
                p, dev = self.device(one, s)
                self.send(pick1(self.mine, p), self.land.at[s - 1], dev)

        def add_one():
            self.settle()
            def one_row(i, _):
                v = (self.mine[i, :, x] if one == 2 else self.mine[i, y]).astype(F32)
                for s in range(1, self.dims[one]):
                    v = v + self.land[s - 1, i].astype(F32)
                self.part[i] = v.astype(self.part.dtype)
                return 0
            lax.fori_loop(0, nz, one_row, 0)
            for s in range(1, self.dims[two]):
                p, dev = self.device(two, s)
                self.send(self.part.at[:, p], self.land2.at[s - 1], dev)

        def add_two():
            self.settle()
            def one_row(i, _):
                v = self.part[i, own2].astype(F32)
                for s in range(1, self.dims[two]):
                    v = v + self.land2[s - 1, i].astype(F32)
                self.part2[i] = v.astype(self.part2.dtype)
                return 0
            lax.fori_loop(0, nz, one_row, 0)
            for s in range(1, nz):
                p, dev = self.device(0, s)
                self.send(self.part2.at[p], self.land3.at[s - 1], dev)

        def add_three():
            self.settle()
            v = self.part2[z].astype(F32)
            for s in range(1, nz):
                v = v + self.land3[s - 1].astype(F32)
            self.total[z, y, x] = v.astype(self.total.dtype)
            spread(0, self.total.at[z, y, x])

        def spread(axis, ref):
            for s in range(1, self.dims[axis]):
                self.send(ref, ref, self.device(axis, s)[1])

        def wide_two():
            self.settle()
            spread(two, self.total.at[:, y, x])

        def wide_one():
            self.settle()
            spread(one, self.total.at[:, :, x] if one == 2 else self.total.at[:, y])

        return [start, pair_add, add_one, add_two, add_three, wide_two, wide_one, self.settle]


def buffers(dims, rows, width, dtype, first):
    nz, ny, nx = dims
    na, nb = (nx, ny) if first == "x" else (ny, nx)
    tail = (rows, width)
    shapes = [
        (nz, ny, nx) + tail, (nz, ny, nx) + tail, (max(na - 1, 1), nz, nb) + tail, (nz, nb) + tail,
        (max(nb - 1, 1), nz) + tail, (nz,) + tail, (max(nz - 1, 1),) + tail,
    ]
    copies = 2 + 2 * (na + nb + nz - 3)
    return [pltpu.VMEM(s, dtype) for s in shapes] + [pltpu.SemaphoreType.DMA((2, copies))]


def reduce_kernel(dims, views, firsts, *refs):
    count = len(firsts)
    sources = refs[: len(views)]
    totals = refs[len(views) : len(views) + count]
    scratch = refs[len(views) + count :]
    index, side = lax.axis_index("dp"), lax.axis_index("tensor")
    nz, ny, nx = dims
    place = (index // (ny * nx), lax.rem(index // nx, ny), lax.rem(index, nx), side, index)
    barrier = pltpu.get_barrier_semaphore()
    peers = [(index, 1 - side)]
    probe = Piece(dims, "x", None, None, None, [None] * 7, None, place)
    for axis in range(3):
        for s in range(1, dims[axis]):
            peers.append(probe.device(axis, s)[1])
    for peer in peers:
        pl.semaphore_signal(barrier, inc=1, device_id=peer, device_id_type=pl.DeviceIdType.MESH)
    pl.semaphore_wait(barrier, len(peers))
    plans = []
    at = 0
    for source, view in zip(sources, views):
        for near, far in view(source):
            plans.append(Piece(dims, firsts[at], near, far, totals[at], scratch[8 * at : 8 * at + 7], scratch[8 * at + 7], place).steps())
            at += 1
    slots = len(plans[0]) + (count + 1) // 2 - 1
    for slot in range(slots):
        for i, plan in enumerate(plans):
            if 0 <= slot - i // 2 < len(plan):
                plan[slot - i // 2]()


def all_reduce(dims, grads, small):
    g_down, g_up, g_qkv, g_out = grads
    nz, ny, nx = dims
    parts = nz * ny * nx
    ff = g_down.shape[0] // 2
    half = ff // 2
    rows_d, rows_u, rows_o = half // parts, D // parts, D // 2 // parts
    cut = 640
    down = g_down.reshape(2, 2, nz, ny, nx, rows_d, D)
    up = g_up.reshape(nz, ny, nx, rows_u, 2 * ff)
    qkv = g_qkv.reshape(nz, ny, nx, rows_u, 3 * D)
    out = g_out.reshape(2, nz, ny, nx, rows_o, D)
    cols = lambda r, a, n: r.at[:, :, :, :, a : a + n]
    wide = 3 * D // 2
    views = [
        lambda r: [(r.at[0, 0], r.at[1, 0]), (r.at[0, 1], r.at[1, 1])],
        lambda r: [(cols(r, 0, half), cols(r, ff, half)), (cols(r, half, half), cols(r, ff + half, half))],
        lambda r: [(cols(r, 0, cut), cols(r, wide, cut)), (cols(r, cut, wide - cut), cols(r, wide + cut, wide - cut))],
        lambda r: [(r.at[0], r.at[1])],
        lambda r: [(r.at[0], r.at[1])],
    ]
    sizes = [(rows_d, D, BF16)] * 2 + [(rows_u, half, BF16)] * 2 + [(rows_u, cut, BF16), (rows_u, wide - cut, BF16), (rows_o, D, BF16)]
    sizes.append(small.shape[-2:] + (F32,))
    firsts = ["x", "y"] * 3 + ["y", "x"]
    scratch = []
    for (r, w, t), first in zip(sizes, firsts):
        scratch += buffers(dims, r, w, t, first)
    totals = pl.pallas_call(
        functools.partial(reduce_kernel, dims, views, firsts),
        in_specs=[pl.BlockSpec(memory_space=pl.ANY)] * 5,
        out_specs=[pl.BlockSpec(memory_space=pltpu.VMEM)] * len(sizes),
        out_shape=[jax.ShapeDtypeStruct((nz, ny, nx, r, w), t) for r, w, t in sizes],
        scratch_shapes=scratch,
        compiler_params=pltpu.CompilerParams(collective_id=0, has_side_effects=True, vmem_limit_bytes=60 * 2**20),
        name="all_reduce",
    )(down, up, qkv, out, small)
    flat = [t.reshape(-1, t.shape[-1]) for t in totals]
    return (
        jnp.concatenate(flat[:2], axis=0).astype(F32),
        jnp.concatenate(flat[2:4], axis=1).astype(F32),
        jnp.concatenate(flat[4:6], axis=1).astype(F32),
        flat[6].astype(F32),
        flat[7].reshape(-1),
    )


class Route:
    def __init__(self, dims, first, near, far, mine, pair, total, bufs, sems):
        self.dims, self.first, self.near, self.far = dims, first, near, far
        self.mine, self.pair, self.total = mine, pair, total
        self.land, self.land2, self.land3 = bufs
        self.sems = sems
        self.count = 0
        self.flight = []

    def launch(self, make):
        slot = self.count
        self.count += 1
        make(slot).start()
        self.flight.append(lambda: make(slot))

    def remote(self, src, dst, where):
        self.launch(
            lambda slot: pltpu.make_async_remote_copy(
                src_ref=src(), dst_ref=dst(), send_sem=self.sems.at[0, slot], recv_sem=self.sems.at[1, slot],
                device_id=where(), device_id_type=pl.DeviceIdType.MESH,
            )
        )

    def local(self, src, dst):
        self.launch(lambda slot: pltpu.make_async_copy(src(), dst(), self.sems.at[0, slot]))

    def settle(self):
        for make in self.flight:
            make().wait()
        self.flight = []

    def steps(self, place):
        z, y, x, side, index = place
        nz, ny, nx = self.dims
        plain = self.first == "x"
        one, two = (2, 1) if plain else (1, 2)
        own = (z, y, x)

        def peer(axis, shift):
            return lax.rem(own[axis] + shift, self.dims[axis])

        def device(axis, shift):
            at = list(own)
            at[axis] = peer(axis, shift)
            return ((at[0] * ny + at[1]) * nx + at[2], side)

        def row(ref, i):
            return ref[i, :, x] if plain else ref[i, y]

        def start():
            if self.near is not None:
                self.local(lambda: self.near(), lambda: self.mine())
            self.remote(lambda: self.far(), lambda: self.pair(), lambda: (index, 1 - side))

        def pair_add():
            self.settle()
            mine, pair = self.mine(), self.pair()

            def body(i, _):
                mine[i] = (mine[i].astype(F32) + pair[i].astype(F32)).astype(mine.dtype)
                return 0

            lax.fori_loop(0, nz, body, 0)
            for s in range(1, self.dims[one]):
                self.remote(
                    lambda s=s: self.mine().at[:, :, peer(one, s)] if plain else self.mine().at[:, peer(one, s)],
                    lambda s=s: self.land().at[s - 1],
                    lambda s=s: device(one, s),
                )

        def add_one():
            self.settle()
            mine, land = self.mine(), self.land()

            def body(i, _):
                v = row(mine, i).astype(F32)
                for s in range(1, self.dims[one]):
                    v = v + land[s - 1, i].astype(F32)
                if plain:
                    mine[i, :, x] = v.astype(mine.dtype)
                else:
                    mine[i, y] = v.astype(mine.dtype)
                return 0

            lax.fori_loop(0, nz, body, 0)
            for s in range(1, self.dims[two]):
                self.remote(
                    lambda s=s: self.mine().at[:, peer(two, s), x] if plain else self.mine().at[:, y, peer(two, s)],
                    lambda s=s: self.land2().at[s - 1],
                    lambda s=s: device(two, s),
                )

        def add_two():
            self.settle()
            mine, land = self.mine(), self.land2()

            def body(i, _):
                v = mine[i, y, x].astype(F32)
                for s in range(1, self.dims[two]):
                    v = v + land[s - 1, i].astype(F32)
                mine[i, y, x] = v.astype(mine.dtype)
                return 0

            lax.fori_loop(0, nz, body, 0)
            for s in range(1, nz):
                self.remote(
                    lambda s=s: self.mine().at[peer(0, s), y, x], lambda s=s: self.land3().at[s - 1], lambda s=s: device(0, s)
                )

        def spread(axis, view, source):
            for s in range(1, self.dims[axis]):
                self.remote(lambda: view(source()), lambda: view(self.total()), lambda s=s: device(axis, s))

        def add_three():
            self.settle()
            mine, land = self.mine(), self.land3()
            v = mine[z, y, x].astype(F32)
            for s in range(1, nz):
                v = v + land[s - 1].astype(F32)
            mine[z, y, x] = v.astype(mine.dtype)
            self.local(lambda: self.mine().at[z, y, x], lambda: self.total().at[z, y, x])
            spread(0, lambda t: t.at[z, y, x], self.mine)

        def wide_two():
            self.settle()
            spread(two, lambda t: t.at[:, y, x], self.total)

        def wide_one():
            self.settle()
            spread(one, lambda t: t.at[:, :, x] if plain else t.at[:, y], self.total)

        return [start, pair_add, add_one, add_two, add_three, wide_two, wide_one, self.settle]


def route_buffers(dims, rows, width, dtype, first):
    nz, ny, nx = dims
    na, nb = (nx, ny) if first == "x" else (ny, nx)
    tail = (rows, width)
    shapes = [(max(na - 1, 1), nz, nb) + tail, (max(nb - 1, 1), nz) + tail, (max(nz - 1, 1),) + tail]
    copies = 3 + 2 * (na + nb + nz - 3)
    return [pltpu.VMEM(s, dtype) for s in shapes] + [pltpu.SemaphoreType.DMA((2, copies))]


PAIRS = D // 128
BLOCK = 256


def greet(dims, place):
    z, y, x, side, index = place
    barrier = pltpu.get_barrier_semaphore()
    peers = [(index, 1 - side)]
    for axis in range(3):
        for s in range(1, dims[axis]):
            at = [z, y, x]
            at[axis] = lax.rem(at[axis] + s, dims[axis])
            peers.append(((at[0] * dims[1] + at[1]) * dims[2] + at[2], side))
    for peer in peers:
        pl.semaphore_signal(barrier, inc=1, device_id=peer, device_id_type=pl.DeviceIdType.MESH)
    pl.semaphore_wait(barrier, len(peers))


def place_of(dims):
    index, side = lax.axis_index("dp"), lax.axis_index("tensor")
    _, ny, nx = dims
    return (index // (ny * nx), lax.rem(index // nx, ny), lax.rem(index, nx), side, index)


def columns(ref, start, width):
    return ref.at[..., start : start + width]


STRIPS = 4
FIRST_PAIR = STRIPS + 1
QKV_STEP = FIRST_PAIR + PAIRS
ORDER = (
    (0, 3, 1, 2),
    (0, 3),
    (),
    (2,),
    (5, 0, 6, 7),
    (1, 3, 6, 4, 0, 2, 8),
    (9, 0, 1, 3, 5, 4, 9, 2),
    (0, 7, 3, 1, 5, 8, 2),
    (0, 4, 5),
    (2, 3, 1, 7, 6, 5),
    (1, 4, 3, 2),
    (5, 4, 1),
    (10, 4, 11, 9, 7, 6, 8, 10, 11, 13, 12, 8, 9, 12, 13, 7),
    (8, 10, 11, 6, 1, 4, 5, 9),
    (7, 8, 11, 10),
    (12, 6, 13),
    (
        11, 14, 8, 9, 10, 7, 14, 11, 12, 6, 13, 10, 0, 5, 12, 8, 14, 11, 2, 12, 13, 10, 7, 14, 6, 14, 13, 14, 9, 12, 14,
        13, 10, 9, 11, 4, 3, 12, 13, 14,
    ),
)


def tail_kernel(dims, table, late, schedule, count, *refs):
    (
        prefix_ref, q_ref, k_ref, v_ref, o_ref, g_ref, lse_ref, n1t_ref, w_ref, x_ref, gm_ref, gain_ref, svec_ref, swide_ref,
        gh_ref, n2t_ref, n3t_ref, gml_ref, down_ref, ig_ref, odown_ref, oup_ref, oqkv_ref, oout_ref, osmall_ref,
        gproj, gqkv, gup, gout, bias, sums, small, mdown, pdown, pup, pout, pqkv, psmall,
    ) = refs[:38]
    scratch = refs[38:]
    pid = pl.program_id(0)
    _, ny, nx = dims
    place = place_of(dims)

    @pl.when(pid == 0)
    def _():
        greet(dims, place)
        sums[...] = jnp.zeros_like(sums)

    homes = {
        "up": (gup, pup, oup_ref),
        "qkv": (gqkv, pqkv, oqkv_ref),
        "out": (gout, pout, oout_ref),
        "small": (small, psmall, osmall_ref),
    }
    plans = []
    for n, (name, lead, start, width, first) in enumerate(table):
        bufs = scratch[4 * n : 4 * n + 4]
        cut = lambda r, at=start, width=width: columns(r, at, width)
        if name == "down":
            views = [down_ref.at[0, lead], down_ref.at[1, lead], mdown.at[lead], pdown.at[lead], odown_ref.at[lead]]
            views = [lambda v=v, cut=cut: cut(v) for v in views]
        else:
            src, pair, total = homes[name]
            near = lambda s=src, cut=cut: cut(s)
            far = lambda s=src, at=start + lead, width=width: columns(s, at, width)
            if name in ("out", "small"):
                near, far = [lambda s=src, i=i, cut=cut: cut(s.at[i]) for i in (0, 1)]
            done = lambda t=total, cut=cut: cut(t)
            if name == "qkv":
                third = D // 2
                done = lambda t=total, at=start, width=width: columns(t.at[at // third], at % third, width)
            views = [None, far, near, lambda p=pair, cut=cut: cut(p), done]
        plans.append(Route(dims, first, *views, [(lambda b=b: b) for b in bufs[:3]], bufs[3]).steps(place))

    def advance(step):
        for n, k in schedule.get(step, ()):
            plans[n][k]()

    for step in range(count):
        if schedule.get(step):
            pl.when(pid == step)(functools.partial(advance, step))

    @pl.when(pid < STRIPS)
    def _():
        width = gh_ref.shape[1]
        at = pl.ds(pl.multiple_of(pid * width, width), width)
        gup[:, :, :, :, at] = nn(n3t_ref[...], gh_ref[...]).astype(BF16).reshape(gup.shape[:4] + (width,))

    @pl.when(pid == STRIPS)
    def _():
        gout[...] = nn(n2t_ref[...], gml_ref[...]).reshape(gout.shape).astype(BF16)

    @pl.when((pid >= FIRST_PAIR) & (pid < QKV_STEP))
    def _():
        i = pid - FIRST_PAIR
        column = lambda c: gproj.at[:, pl.ds(pl.multiple_of(head_block(i, c) * 128, 128), 128)]
        attn_bwd_kernel(
            prefix_ref, q_ref, k_ref, v_ref, o_ref, g_ref, lse_ref, column(0), column(1), column(2),
            bias.at[:, pl.ds(pl.multiple_of(i * 128, 128), 128)],
        )

    @pl.when(pid == QKV_STEP)
    def _():
        def body(c, _):
            at = pl.ds(pl.multiple_of(c * D, 128), D)
            part = nn(n1t_ref[...], gproj[:, at]).astype(BF16)
            gqkv[:, :, :, :, at] = part.reshape(gqkv.shape[:4] + (D,))
            return 0

        lax.fori_loop(0, 3, body, 0)

    @pl.when(pid > QKV_STEP)
    def _():
        rows = pl.ds(pl.multiple_of((pid - QKV_STEP - 1) * BLOCK, BLOCK), BLOCK)
        e = nt(gproj[rows, :], w_ref[...])
        xhat, inv = normed(x_ref[...].astype(F32))
        sums[0] += colsum(e * xhat)
        sums[1] += colsum(e)
        ig_ref[...] = gm_ref[...] + normed_back(e * gain_ref[...].reshape(1, D), xhat, inv)

    @pl.when(pid == count - 1)
    def _():
        small[...] = jnp.zeros_like(small)
        split = [bias[i : i + 1, :] for i in range(2)]
        split += [jnp.sum(svec_ref[i], axis=0, keepdims=True) for i in range(2)]
        split += [jnp.sum(swide_ref[i], axis=0, keepdims=True) for i in range(3)]
        shared = [jnp.sum(sums[i], axis=0, keepdims=True) for i in range(2)]
        shared += [jnp.sum(svec_ref[i], axis=0, keepdims=True) for i in range(2, 6)]
        for s in range(2):
            at = 0
            for v in [v[:, s * (v.shape[1] // 2) : (s + 1) * (v.shape[1] // 2)] for v in split] + shared:
                for c in range(v.shape[1] // 128):
                    p = at // 8
                    small[s, p // (ny * nx), p // nx % ny, p % nx, at % 8 : at % 8 + 1, :] = v[:, c * 128 : (c + 1) * 128]
                    at += 1
        for n, k in late:
            plans[n][k]()


def tail_stage(dims, prefix, qkv, attended, ga, lse, n1t, wqkv, tokens, gm, pre_gain, svec, swide, gh, n2t, n3t, gml, g_down):
    nz, ny, nx = dims
    parts = nz * ny * nx
    length = qkv.shape[0]
    ff = gh.shape[1] // 2
    half, third = ff // 2, D // 2
    rows = D // parts
    wide = 3 * D // 2
    small_rows = 8
    down = g_down.reshape(2, 2, nz, ny, nx, rows, D)
    table = []
    for a in (0, D // 2):
        table += [("down", 0, a, D // 2, "x"), ("down", 1, a, D // 2, "y")]
    for a in (0, half // 2):
        table += [("up", ff, a, half // 2, "x"), ("up", ff, half + a, half // 2, "y")]
    table += [("out", 0, 0, third, "x"), ("out", 0, third, third, "y")]
    table += [("qkv", wide, 0, third, "x"), ("qkv", wide, 2 * third, third, "y")]
    table += [("qkv", wide, third, 256, "x"), ("qkv", wide, third + 256, 128, "y")]
    table += [("small", 0, 0, 128, "x")]
    count = QKV_STEP + 1 + length // BLOCK
    phase = [0] * len(table)
    steps = []
    for pieces in ORDER:
        steps.append([])
        for n in pieces:
            steps[-1].append((n, phase[n]))
            phase[n] += 1
    schedule, late = dict(enumerate(steps[:count])), steps[count]
    sds = jax.ShapeDtypeStruct
    box = (nz, ny, nx)
    shapes = {
        "down": (2, *box, rows, D), "up": (*box, rows, ff), "qkv": (*box, rows, wide), "out": (*box, rows // 2, D),
        "small": (*box, small_rows, 128),
    }
    kinds = {n: F32 if n == "small" else BF16 for n in shapes}
    landed = dict(shapes, qkv=(3, *box, rows, third))
    scratch = [
        pltpu.VMEM((length, 3 * D), BF16), pltpu.VMEM((*box, rows, 3 * D), BF16), pltpu.VMEM((*box, rows, 2 * ff), BF16),
        pltpu.VMEM((2, *box, rows // 2, D), BF16), pltpu.VMEM((8, D), F32), pltpu.VMEM((2, 8, D), F32),
        pltpu.VMEM((2, *box, small_rows, 128), F32), pltpu.VMEM(shapes["down"], BF16),
    ]
    scratch += [pltpu.VMEM(shapes[n], kinds[n]) for n in ("down", "up", "out", "qkv", "small")]
    heights = {"down": rows, "up": rows, "qkv": rows, "out": rows // 2, "small": small_rows}
    for name, _, _, width, first in table:
        scratch += route_buffers(dims, heights[name], width, kinds[name], first)
    pair_at = lambda i: jnp.clip(i - FIRST_PAIR, 0, PAIRS - 1)
    block_at = lambda i: jnp.maximum(i - QKV_STEP - 1, 0)
    col = lambda c: pl.BlockSpec((length, 128), lambda i, c=c: (0, head_block(pair_at(i), c)))
    one = pl.BlockSpec((length, 128), lambda i: (0, pair_at(i)))
    block = pl.BlockSpec((BLOCK, D), lambda i: (block_at(i), 0))
    strip = pl.BlockSpec((length, 2 * ff // STRIPS), lambda i: (0, jnp.minimum(i, STRIPS - 1)))
    whole = lambda v: pl.BlockSpec(v.shape, lambda i, n=v.ndim: (0,) * n, pipeline_mode=pl.Buffered(1))
    hbm = pl.BlockSpec(memory_space=pl.ANY)
    return pl.pallas_call(
        functools.partial(tail_kernel, dims, table, late, schedule, count),
        grid=(count,),
        in_specs=[
            pl.BlockSpec(memory_space=pltpu.SMEM), col(0), col(1), col(2), one, one,
            pl.BlockSpec((1, 8, length), lambda i: (pair_at(i), 0, 0)), whole(n1t), whole(wqkv), block, block, whole(pre_gain),
            whole(svec), whole(swide), strip, whole(n2t), whole(n3t), whole(gml), hbm,
        ],
        out_specs=[block] + [hbm] * 5,
        out_shape=[sds((length, D), F32)] + [sds(landed[n], kinds[n]) for n in ("down", "up", "qkv", "out", "small")],
        scratch_shapes=scratch,
        compiler_params=pltpu.CompilerParams(collective_id=1, has_side_effects=True, vmem_limit_bytes=VMEM),
        name="tail_stage",
    )(
        prefix, qkv, qkv, qkv, attended, ga, lse, n1t, wqkv, tokens, gm, pre_gain, svec, swide, gh, n2t, n3t, gml, down,
    )


def unpack_kernel(ig_ref, down_ref, up_ref, qkv_ref, out_ref, small_ref, oig, odown, oup, oqkv, oout, *vectors):
    oig[...] = ig_ref[...]
    odown[...] = down_ref[...].astype(F32)
    oup[...] = up_ref[...].astype(F32)
    oqkv[...] = qkv_ref[...].astype(F32)
    oout[...] = out_ref[...].astype(F32).reshape(oout.shape)

    @pl.when(pl.program_id(0) == 0)
    def _():
        at = 0
        for ref in vectors:
            for row in range(ref.shape[0] if ref.ndim == 2 else 1):
                for c in range(ref.shape[-1] // 128):
                    lanes = pl.ds(c * 128, 128)
                    if ref.ndim == 2:
                        ref[row, lanes] = small_ref[at, :]
                    else:
                        ref[lanes] = small_ref[at, :]
                    at += 1


def unpack(input_grad, down, up, qkv, out, small, ff):
    steps = 8
    half = D // 2
    down, up, qkv = down.reshape(ff, D), up.reshape(D, ff), qkv.reshape(3 * D, half)
    out = out.reshape((-1,) + out.shape[-2:])
    small = small.reshape(-1, 128)
    block = lambda v: pl.BlockSpec((v.shape[0] // steps,) + v.shape[1:], lambda i, n=v.ndim: (i,) + (0,) * (n - 1))
    whole = lambda s: pl.BlockSpec(s, lambda i: (0,) * len(s), pipeline_mode=pl.Buffered(1))
    sds = lambda s: jax.ShapeDtypeStruct(s, F32)
    vectors = [(2, half), (half,), (half,), (ff,), (ff,), (ff,)] + [(D,)] * 6
    shapes = [input_grad.shape, (ff, D), (D, ff), (3 * D, half), (half, D)]
    return pl.pallas_call(
        unpack_kernel,
        grid=(steps,),
        in_specs=[block(v) for v in (input_grad, down, up, qkv, out)] + [whole(small.shape)],
        out_specs=[block(sds(s)) for s in shapes] + [whole(s) for s in vectors],
        out_shape=[sds(s) for s in shapes + vectors],
        compiler_params=pltpu.CompilerParams(vmem_limit_bytes=VMEM),
        name="unpack",
    )(input_grad, down, up, qkv, out, small)


def head_kernel(
    x_ref, gain_ref, bias_ref, w_ref, wo_ref, sub_gain, sub_bias, up_bias, inner_gain, inner_bias, qv_ref,
    out_bias, ffn_gain, ffn_bias, down_bias,
    qkv_ref, n1t_ref, wall_ref, far_wo, vec_ref, wide_ref,
    near_sem, send_sem, recv_sem, norm_ref, far_sg, far_sb, far_ub, far_ig, far_ib, far_qv,
):
    index, side = lax.axis_index("dp"), lax.axis_index("tensor")
    other = (index, 1 - side)
    mesh_id = pl.DeviceIdType.MESH
    barrier = pltpu.get_barrier_semaphore()
    pl.semaphore_signal(barrier, inc=1, device_id=other, device_id_type=mesh_id)
    half = D // 2
    wide = 3 * half
    here = [pltpu.make_async_copy(w_ref.at[c], wall_ref.at[:, c * half : (c + 1) * half], near_sem.at[c]) for c in range(3)]
    for copy in here:
        copy.start()
    pl.semaphore_wait(barrier, 1)
    away = [(w_ref.at[c], wall_ref.at[:, wide + c * half : wide + (c + 1) * half]) for c in range(3)]
    away += [(qv_ref, far_qv), (sub_gain, far_sg), (sub_bias, far_sb)]
    away += [(up_bias, far_ub), (inner_gain, far_ig), (inner_bias, far_ib), (wo_ref, far_wo)]
    away = [
        pltpu.make_async_remote_copy(
            src_ref=a, dst_ref=b, send_sem=send_sem.at[i], recv_sem=recv_sem.at[i], device_id=other, device_id_type=mesh_id
        )
        for i, (a, b) in enumerate(away)
    ]
    for copy in away:
        copy.start()
    length = x_ref.shape[0]
    block = 256
    line = lambda ref: ref[...].reshape(1, -1)
    gain, bias = line(gain_ref), line(bias_ref)

    def norm(i, _):
        rows = pl.ds(pl.multiple_of(i * block, block), block)
        xhat, _ = normed(x_ref[rows, :].astype(F32))
        n1 = (xhat * gain + bias).astype(BF16)
        norm_ref[rows, :] = n1
        n1t_ref[:, rows] = n1.T
        return 0

    lax.fori_loop(0, length // block, norm, 0)

    def product(first, biases):
        weight = wall_ref[:, first : first + wide]
        bias = jnp.concatenate([biases[0:1, :], jnp.zeros((1, half), F32), biases[1:2, :]], axis=1)

        def rows(i, _):
            at = pl.ds(pl.multiple_of(i * block, block), block)
            qkv_ref[at, first : first + wide] = (nn(norm_ref[at, :], weight) + bias).astype(BF16)
            return 0

        lax.fori_loop(0, length // block, rows, 0)

    for copy in here:
        copy.wait()
    product(0, qv_ref[...])
    for copy in away:
        copy.wait()
    product(wide, far_qv[...])
    both = lambda near, far: jnp.concatenate([line(near), line(far)], axis=1)
    vec_ref[0:1, :] = both(sub_gain, far_sg)
    vec_ref[1:2, :] = both(sub_bias, far_sb)
    for i, v in enumerate((out_bias, ffn_gain, ffn_bias, down_bias)):
        vec_ref[i + 2 : i + 3, :] = line(v)
    for i, (near, far) in enumerate(((up_bias, far_ub), (inner_gain, far_ig), (inner_bias, far_ib))):
        wide_ref[i : i + 1, :] = both(near, far)


def head_stage(tokens, pre_gain, pre_bias, w3, wo, sub_gain, sub_bias, up_bias, inner_gain, inner_bias, qv_bias, *rest):
    length = tokens.shape[0]
    ff_half = up_bias.shape[0]
    half = D // 2
    sds = jax.ShapeDtypeStruct
    vmem, hbm = pl.BlockSpec(memory_space=pltpu.VMEM), pl.BlockSpec(memory_space=pl.ANY)
    return pl.pallas_call(
        head_kernel,
        in_specs=[vmem] * 3 + [hbm] * 2 + [vmem] * 10,
        out_specs=[vmem] * 3 + [hbm] + [vmem] * 2,
        out_shape=[
            sds((length, 3 * D), BF16), sds((D, length), BF16), sds((D, 3 * D), BF16), sds(wo.shape, BF16),
            sds((6, D), F32), sds((3, 2 * ff_half), F32),
        ],
        scratch_shapes=[
            pltpu.SemaphoreType.DMA((3,)), pltpu.SemaphoreType.DMA((10,)), pltpu.SemaphoreType.DMA((10,)),
            pltpu.VMEM((length, D), BF16), *[pltpu.VMEM((half,), F32)] * 2,
            *[pltpu.VMEM((ff_half,), F32)] * 3, pltpu.VMEM((2, half), F32),
        ],
        compiler_params=pltpu.CompilerParams(collective_id=2, has_side_effects=True, vmem_limit_bytes=VMEM),
        name="head_stage",
    )(tokens, pre_gain, pre_bias, w3, wo, sub_gain, sub_bias, up_bias, inner_gain, inner_bias, qv_bias, *rest)


def pack_small(dims, g_qv, g_vec, g_wide, g_pre):
    half, ff_half = D // 2, g_wide.shape[1] // 2
    shared = jnp.concatenate([g_pre.reshape(-1), g_vec[2:].reshape(-1)])
    rows = -(-(4 * half + 3 * ff_half + 6 * D) // (128 * 8 * math.prod(dims))) * 8
    pad = jnp.zeros((rows * 128 * math.prod(dims) - (4 * half + 3 * ff_half + 6 * D),), F32)
    pack = lambda i: jnp.concatenate(
        [v[j, i * n : (i + 1) * n] for v, m, n in ((g_qv, 2, half), (g_vec, 2, half), (g_wide, 3, ff_half)) for j in range(m)] + [shared, pad]
    )
    return jnp.stack([pack(0), pack(1)]).reshape((2,) + dims + (rows, 128))


def body(
    dims, tokens, grad_out, prefix, pre_gain, pre_bias, qkv_weight, qv_bias, sub_gain, sub_bias, out_weight, out_bias,
    ffn_gain, ffn_bias, up_weight, up_bias, inner_gain, inner_bias, down_weight, down_bias,
):
    half, ff_half = D // 2, up_bias.shape[0]
    qkv, n1t, wqkv, wo_far, vecs, wides = head_stage(
        tokens, pre_gain, pre_bias, qkv_weight.transpose(1, 0, 2), out_weight, sub_gain, sub_bias, up_bias, inner_gain, inner_bias,
        qv_bias, out_bias, ffn_gain, ffn_bias, down_bias,
    )
    attended, lse, wu_far, wd_far = attn_fwd(prefix, qkv, up_weight, down_weight)
    wo, wu, wd = (out_weight, wo_far), (up_weight, wu_far), (down_weight, wd_far)
    out, n2t, n3t, n4, gh, gm, gml, ga, svec, swide = middle_stage(tokens, attended, grad_out, vecs, wides, wo, wu, wd)
    g_down = tn(n4, grad_out).astype(BF16)
    if D // math.prod(dims) % 16 == 0:
        sums = tail_stage(
            dims, prefix, qkv, attended, ga, lse, n1t, wqkv, tokens, gm, pre_gain, svec, swide, gh, n2t, n3t, gml, g_down
        )
        input_grad, g_down, g_up, g_qkv, g_out, *vectors = unpack(*sums, ff_half)
        g_qv, g_sub_gain, g_sub_bias, g_up_bias, g_inner_gain, g_inner_bias = vectors[:6]
        g_pre_gain, g_pre_bias, g_out_bias, g_ffn_gain, g_ffn_bias, g_down_bias = vectors[6:]
        g_qkv = g_qkv.reshape(3, D, half)
    else:
        g_up, g_out = nn(n3t, gh).astype(BF16), nn(n2t, gml).astype(BF16)
        input_grad, g_pre, g_qkv, g_qv = back(prefix, tokens, pre_gain, wqkv, n1t.T, qkv, attended, lse, gm, ga)
        small = pack_small(dims, g_qv, jnp.sum(svec, 1), jnp.sum(swide, 1), g_pre)
        g_down, g_up, g_qkv, g_out, small = all_reduce(dims, (g_down, g_up, g_qkv, g_out), small)
        g_qkv = g_qkv.reshape(D, 3, half).transpose(1, 0, 2)
        g_qv = small[: 2 * half].reshape(2, half)
        g_sub_gain, g_sub_bias = [small[i * half : (i + 1) * half] for i in (2, 3)]
        g_up_bias, g_inner_gain, g_inner_bias = [small[4 * half + i * ff_half : 4 * half + (i + 1) * ff_half] for i in range(3)]
        base = 4 * half + 3 * ff_half
        g_pre_gain, g_pre_bias, g_out_bias, g_ffn_gain, g_ffn_bias, g_down_bias = [
            small[base + i * D : base + (i + 1) * D] for i in range(6)
        ]
    return (
        out, input_grad, g_pre_gain, g_pre_bias, g_qkv.transpose(1, 0, 2), g_qv, g_sub_gain, g_sub_bias, g_out, g_out_bias,
        g_ffn_gain, g_ffn_bias, g_up, g_up_bias, g_inner_gain, g_inner_bias, g_down, g_down_bias,
    )


def solution(mesh):
    rows = P(("dp", "tensor"), None)
    wide, tall, vec, whole = P(None, "tensor"), P("tensor", None), P("tensor"), P()
    cube = P(None, None, "tensor")
    return jax.shard_map(
        functools.partial(body, grid_of(mesh.shape["dp"])),
        mesh=mesh,
        in_specs=(
            rows, rows, P("dp"), whole, whole, cube, wide, vec, vec, tall, whole, whole, whole, wide, vec, vec, vec, tall, whole,
        ),
        out_specs=(
            rows, rows, whole, whole, cube, wide, vec, vec, tall, whole, whole, whole, wide, vec, vec, vec, tall, whole,
        ),
        check_vma=False,
    )
```
